32 devices in a mesh: fsdp: 4 (over y, x), ctx: 4 (over z), tp: 2 (over core).
Axes of the slice: x: 2, y: 2, z: 4, core: 2. Of those that a mesh axis runs over, the one named last changes fastest.
Arguments:
- inputs: bfloat16 [3, 1024, 4, 1024], P(None, 'ctx', 'fsdp'), may hold values from -8 to 8
- block_order: int32 [3, 4, 4], P(None, 'fsdp'), may hold values from 0 to 3, each once within a row
- first_gain: bfloat16 [1024], replicated, may hold values from 0.5 to 1.5
- first_shift: bfloat16 [1024], replicated, may hold values from -1.25 to 1.25
- second_gain: bfloat16 [1024], replicated, may hold values from 0.5 to 1.5
- second_shift: bfloat16 [1024], replicated, may hold values from -1.25 to 1.25
- qkv_weight: bfloat16 [3, 1024, 1024], P(None, ('fsdp', 'ctx'), 'tp'), may hold values from -0.1875 to 0.1875
- qkv_bias: bfloat16 [3, 1024], P(None, 'tp'), may hold values from -1.25 to 1.25
- out_weight: bfloat16 [1024, 1024], P('tp', ('fsdp', 'ctx')), may hold values from -5 to 5
- out_bias: bfloat16 [1024], replicated, may hold values from -1.25 to 1.25
- up_weight: bfloat16 [1024, 4096], P(('fsdp', 'ctx'), 'tp'), may hold values from -0.1875 to 0.1875
- up_bias: bfloat16 [4096], P('tp'), may hold values from -1.25 to 1.25
- down_weight: bfloat16 [4096, 1024], P('tp', ('fsdp', 'ctx')), may hold values from -0.09375 to 0.09375
- down_bias: bfloat16 [1024], replicated, may hold values from -1.25 to 1.25
- out_grad: bfloat16 [3, 1024, 4, 1024], P(None, 'ctx', 'fsdp'), may hold values from -8 to 8
Outputs:
- outputs: bfloat16 [3, 1024, 4, 1024], P(None, 'ctx', 'fsdp')
- input_grad: bfloat16 [3, 1024, 4, 1024], P(None, 'ctx', 'fsdp')
- first_gain_grad: float32 [1024], replicated
- first_shift_grad: float32 [1024], replicated
- second_gain_grad: float32 [1024], replicated
- second_shift_grad: float32 [1024], replicated
- qkv_weight_grad: float32 [3, 1024, 1024], P(None, ('fsdp', 'ctx'), 'tp')
- qkv_bias_grad: float32 [3, 1024], P(None, 'tp')
- out_weight_grad: float32 [1024, 1024], P('tp', ('fsdp', 'ctx'))
- out_bias_grad: float32 [1024], replicated
- up_weight_grad: float32 [1024, 4096], P(('fsdp', 'ctx'), 'tp')
- up_bias_grad: float32 [4096], P('tp')
- down_weight_grad: float32 [4096, 1024], P('tp', ('fsdp', 'ctx'))
- down_bias_grad: float32 [1024], replicated
The draws below stay inside these ranges and needn't reach their ends.
Inputs may be any that keep to these rules, and one draw needn't show every extreme that they name: block_order[m, s, c] is the position block of the tokens at rows c * 256 to (c + 1) * 256 - 1 of sequence s of micro-batch m; each row names every block once.
All inputs are finite; a program needn't handle non-finite values.
Results may differ from the reference program's by a relative error of at most 0.014.
Values may be sent and summed in bfloat16 or wider, within the bound.
No kernel may reach another device: no remote copies, remote signals or barrier semaphores. Data moves between devices by JAX's collectives and lax.ppermute only.
A program may use at most 192 MiB of HBM per device.

```python
import math
import jax
import jax.numpy as jnp
from jax import lax

D = 1024
H = 16
HD = 64
ROT = 16
FF = 4096
BLK = 256
MICRO = 3
LEN = 1024
SEQS = 4
N_CTX = 4


def strengthened(array, own_key, source, target, parts, factor):
    def block_of(position):
        return (jnp.arange(array.shape[position]) // (array.shape[position] // parts)).reshape((-1,) + (1,) * (array.ndim - 1 - position))

    near = jax.random.permutation(own_key, parts)[block_of(target)]
    far = (block_of(target) + parts // 2) % parts
    return jnp.where((block_of(source) == near) | (block_of(source) == far), factor * array, array)


def shard_levels(key, extent, shards, low, top_value):
    def one(dim, blocks):
        steps = jax.random.uniform(jax.random.fold_in(jax.random.fold_in(key, 6), dim), (blocks,), jnp.float32, low / len(shards), top_value / len(shards))
        return jnp.repeat(jnp.exp(steps), extent[dim] // blocks).reshape((-1,) + (1,) * (len(extent) - dim - 1))

    level = one(*shards[0])
    for cut in shards[1:]:
        level = level * one(*cut)
    return level


def scatter_about(own_key, dims, scale, reach, split=(), held_as=jnp.bfloat16):
    entries = jax.random.normal(own_key, dims, jnp.float32) * scale
    if len(split) > 0:
        entries = shard_levels(own_key, dims, split, -0.22, 0.18) * entries
    return jnp.clip(entries, min=-reach, max=reach).astype(held_as)


def heavy_noise(own_key, extent, scale, bound, pieces, heavy, held_as=jnp.bfloat16):
    drawn = scale * jax.random.normal(own_key, extent, jnp.float32)
    if pieces:
        drawn = drawn * shard_levels(own_key, extent, pieces, -0.22, 0.18)
    return jnp.clip(strengthened(drawn, jax.random.fold_in(own_key, 3), *heavy), -bound, bound).astype(held_as)


def setup_inputs(seed: int = 0) -> dict:
    seeds = jax.random.split(jax.random.key(seed), 16)
    return {
        "inputs": heavy_noise(seeds[0], (MICRO, LEN, SEQS, D), 1.0, 8.0, ((1, 4), (2, 4)), (1, 3, 4, 2.0)),
        "block_order": jax.vmap(lambda own: jax.random.permutation(own, N_CTX))(jax.random.split(seeds[1], MICRO * SEQS)).reshape((MICRO, SEQS, N_CTX)).astype(jnp.int32),
        "first_gain": jnp.clip(1.0 + 0.1 * jax.random.normal(seeds[2], (D,), jnp.float32), 0.5, 1.5).astype(jnp.bfloat16),
        "first_shift": scatter_about(seeds[3], (D,), 0.2, 1.25),
        "second_gain": jnp.clip(1.0 + 0.1 * jax.random.normal(seeds[4], (D,), jnp.float32), 0.5, 1.5).astype(jnp.bfloat16),
        "second_shift": scatter_about(seeds[5], (D,), 0.2, 1.25),
        "qkv_weight": scatter_about(seeds[6], (3, D, D), D ** -0.5, 0.1875, ((1, 16), (2, 2))),
        "qkv_bias": scatter_about(seeds[7], (3, D), 0.2, 1.25, ((1, 2),)),
        "out_weight": scatter_about(seeds[8], (D, D), ((BLK * (N_CTX + 1) // 2) ** 0.5 * D ** -0.5), 5.0, ((0, 2), (1, 16))),
        "out_bias": scatter_about(seeds[9], (D,), 0.2, 1.25),
        "up_weight": scatter_about(seeds[10], (D, FF), D ** -0.5, 0.1875, ((0, 16), (1, 2))),
        "up_bias": scatter_about(seeds[11], (FF,), 0.2, 1.25, ((0, 2),)),
        "down_weight": scatter_about(seeds[12], (FF, D), FF ** -0.5, 0.09375, ((0, 2), (1, 16))),
        "down_bias": scatter_about(seeds[13], (D,), 0.2, 1.25),
        "out_grad": heavy_noise(seeds[14], (MICRO, LEN, SEQS, D), 1.0, 8.0, ((1, 4), (2, 4)), (1, 3, 4, 2.0)),
    }


highest = lax.Precision.HIGHEST

@jax.custom_vjp
def low(v):
    return lax.optimization_barrier(v.astype(jnp.bfloat16)).astype(jnp.float32)

@jax.custom_vjp
def low_back(v):
    return v

def low_keep(v):
    return (low(v), None)

def low_pass(kept, grad):
    return (grad,)

def back_keep(v):
    return (v, None)

def back_low(kept, grad):
    return (low(grad),)
low.defvjp(low_keep, low_pass)
low_back.defvjp(back_keep, back_low)

def norm_rows(values, scales, biases):
    centre = lax.optimization_barrier(jnp.mean(values, axis=-1, keepdims=True))
    offset = values - centre
    spread = lax.optimization_barrier(jnp.mean(offset * offset, axis=-1, keepdims=True))
    return offset * lax.rsqrt(spread + 1e-05) * scales + biases

def rotate(values, places, rotary):
    halves = rotary // 2
    frequency = jnp.exp(jnp.arange(halves, dtype=jnp.float32) * (-2.0 * math.log(10000.0) / rotary))
    angles = places[..., None] * frequency
    cosine_table = jnp.cos(angles)[..., None, :]
    sine_table = jnp.sin(angles)[..., None, :]
    leading = values[..., :halves]
    trailing = values[..., halves:rotary]
    return jnp.concatenate([leading * cosine_table - trailing * sine_table, trailing * cosine_table + leading * sine_table, values[..., rotary:]], axis=-1)

def sequence_out(inputs_seq, params, blocks):
    first_gain, first_shift, second_gain, second_shift, qkv_weight, qkv_bias, out_weight, out_bias, up_weight, up_bias, down_weight, down_bias = params
    normed_one = low(norm_rows(inputs_seq, first_gain, first_shift))
    normed_two = low(norm_rows(inputs_seq, second_gain, second_shift))
    projected = low_back(jnp.einsum('td,jde->jte', normed_one, qkv_weight, precision=highest) + qkv_bias[:, None, :])
    places = (blocks * BLK + jnp.arange(LEN, dtype=jnp.int32) % BLK).astype(jnp.float32)
    head_views = projected.reshape(3, LEN, H, HD)
    queries = low(rotate(head_views[0], places, ROT))
    key_heads = low(rotate(head_views[1], places, ROT))
    value_heads = low(head_views[2])
    block_span = math.gcd(LEN, 512)
    block_count = LEN // block_span

    def attend(query_pair):
        query_block, block_ids = query_pair
        scores = low_back(jnp.einsum('qhe,khe->hqk', query_block, key_heads, precision=highest) * HD ** (-0.5))
        allowed = blocks[None, :] <= block_ids[:, None]
        scores = jnp.where(allowed[None], scores, -1e+30)
        probability = low(jax.nn.softmax(scores, axis=-1))
        return jnp.einsum('hqk,khe->qhe', probability, value_heads, precision=highest)
    attended = lax.map(jax.checkpoint(attend), (queries.reshape(block_count, block_span, H, HD), blocks.reshape(block_count, block_span)))
    attended = low(low_back(attended.reshape(LEN, D)))
    up_pre = low_back(jnp.dot(normed_two, up_weight, precision=highest) + up_bias)
    hidden = low(jax.nn.gelu(up_pre, approximate=False))
    return inputs_seq + jnp.dot(attended, out_weight, precision=highest) + jnp.dot(hidden, down_weight, precision=highest) + out_bias + down_bias

def reference(inputs, block_order, first_gain, first_shift, second_gain, second_shift, qkv_weight, qkv_bias, out_weight, out_bias, up_weight, up_bias, down_weight, down_bias, out_grad):
    sequences = MICRO * SEQS
    series = jnp.transpose(inputs.astype(jnp.float32), (0, 2, 1, 3)).reshape(sequences, LEN, D)
    cotangent = jnp.transpose(out_grad.astype(jnp.float32), (0, 2, 1, 3)).reshape(sequences, LEN, D)
    orders = block_order.reshape(sequences, N_CTX).astype(jnp.int32)
    params = tuple((weight_arg.astype(jnp.float32) for weight_arg in (first_gain, first_shift, second_gain, second_shift, qkv_weight, qkv_bias, out_weight, out_bias, up_weight, up_bias, down_weight, down_bias)))
    zeros_init = tuple((jnp.zeros_like(weight_arg) for weight_arg in params))

    def per_sequence(running, sequence_item):
        inputs_seq, grad_seq, order_row = sequence_item
        blocks = jnp.repeat(order_row, BLK, total_repeat_length=LEN).astype(jnp.int32)
        result, pullback = jax.vjp(lambda values, weights: sequence_out(values, weights, blocks), inputs_seq, params)
        input_part, weight_parts = pullback(grad_seq)
        running = jax.tree.map(jnp.add, running, weight_parts)
        return (running, (result.astype(jnp.bfloat16), input_part.astype(jnp.bfloat16)))
    totals, (results, input_parts) = lax.scan(per_sequence, zeros_init, (series, cotangent, orders))
    outputs = jnp.transpose(results.reshape(MICRO, SEQS, LEN, D), (0, 2, 1, 3))
    input_grad = jnp.transpose(input_parts.reshape(MICRO, SEQS, LEN, D), (0, 2, 1, 3))
    return (outputs, input_grad, totals[0], totals[1], totals[2], totals[3], totals[4], totals[5], totals[6], totals[7], totals[8], totals[9], totals[10], totals[11])
```

```python
import math

import jax
import jax.numpy as jnp
from jax import lax
from jax.experimental import pallas as pl
from jax.experimental.pallas import tpu as pltpu
from jax.sharding import PartitionSpec as P

HD = 64
ROT = 16
LANES = 128
F32 = jnp.float32
BF16 = jnp.bfloat16
VMEM_BYTES = 56 * 1024 * 1024


def rotate_ring(value, axis, step):
    size = lax.axis_size(axis)
    return lax.ppermute(value, axis, [(i, (i + step) % size) for i in range(size)])


def swap_bit(value, axis, bit):
    size = lax.axis_size(axis)
    return lax.ppermute(value, axis, [(i, i ^ bit) for i in range(size)])


def place(buffer, value, starts):
    return lax.dynamic_update_slice(buffer, value, starts)


def gather_rows(shard, bit_orders):
    rows, width = shard.shape
    fsdp, ctx = lax.axis_size("fsdp"), lax.axis_size("ctx")
    f, z = lax.axis_index("fsdp"), lax.axis_index("ctx")
    column = jnp.zeros((ctx * rows, width), shard.dtype)
    column = place(column, shard, (z * rows, 0))
    for step in range(1, ctx):
        got = rotate_ring(shard, "ctx", step)
        column = place(column, got, (((z - step) % ctx) * rows, 0))
    part = width // len(bit_orders)
    whole = jnp.zeros((fsdp * ctx * rows, width), shard.dtype)
    for index, bits in enumerate(bit_orders):
        pieces = {0: column[:, index * part : (index + 1) * part]}
        for bit in bits:
            for offset in list(pieces):
                pieces[offset | bit] = swap_bit(pieces[offset], "fsdp", bit)
        for offset, piece in pieces.items():
            whole = place(whole, piece, ((f ^ offset) * (ctx * rows), index * part))
    return whole


def scatter_rows(partial, bits):
    fsdp, ctx = lax.axis_size("fsdp"), lax.axis_size("ctx")
    f, z = lax.axis_index("fsdp"), lax.axis_index("ctx")
    rows, width = partial.shape[0] // (fsdp * ctx), partial.shape[1]
    block = ctx * rows
    sums = {
        offset: lax.dynamic_slice(partial, ((f ^ offset) * block, 0), (block, width))
        for offset in range(fsdp)
    }
    for bit in reversed(bits):
        for offset in [key for key in sums if key & bit]:
            got = swap_bit(sums.pop(offset).astype(BF16), "fsdp", bit)
            sums[offset ^ bit] = sums[offset ^ bit] + got.astype(F32)
    mine = sums[0]
    total = lax.dynamic_slice(mine, (z * rows, 0), (rows, width))
    for step in range(1, ctx):
        piece = lax.dynamic_slice(mine, (((z + step) % ctx) * rows, 0), (rows, width))
        total = total + rotate_ring(piece.astype(BF16), "ctx", step).astype(F32)
    return total


def sum_small(value):
    for axis in ("fsdp", "ctx"):
        bit = 1
        while bit < lax.axis_size(axis):
            value = value + swap_bit(value, axis, bit)
            bit *= 2
    return value


def other_core(value):
    return lax.ppermute(value, "tp", [(0, 1), (1, 0)])


def turn(values, cosine, sine):
    lane = lax.broadcasted_iota(jnp.int32, values.shape, 1) % HD
    ahead = pltpu.roll(values, LANES - ROT // 2, 1)
    behind = pltpu.roll(values, ROT // 2, 1)
    return values * cosine + jnp.where(lane < ROT // 2, -ahead, behind) * sine


def project_kernel(order_ref, normed_ref, grad_ref, weight_ref, bias_ref, table_ref, out_ref):
    width = 3 * LANES
    weight = weight_ref[...]
    pre = jnp.dot(normed_ref[...], weight[:, :width], preferred_element_type=F32) + bias_ref[0]
    cosine, sine = table_ref[0], table_ref[1]
    out_ref[0, 0, :, :LANES] = turn(pre[:, :LANES], cosine, sine).astype(BF16)
    out_ref[0, 0, :, LANES : 2 * LANES] = turn(pre[:, LANES : 2 * LANES], cosine, sine).astype(BF16)
    out_ref[0, 0, :, 2 * LANES : width] = pre[:, 2 * LANES :].astype(BF16)
    back = jnp.dot(grad_ref[...], weight[:, width:], preferred_element_type=F32)
    out_ref[0, 0, :, width:] = back.astype(BF16)


def project(own_order, normed, grad_rows, weight, bias, table, block_rows):
    tokens, width = normed.shape
    micro = tokens // block_rows
    groups = weight.shape[1] // (4 * LANES)
    return pl.pallas_call(
        project_kernel,
        out_shape=jax.ShapeDtypeStruct((groups, micro, block_rows, 4 * LANES), BF16),
        grid_spec=pltpu.PrefetchScalarGridSpec(
            num_scalar_prefetch=1,
            grid=(groups, micro),
            in_specs=[
                pl.BlockSpec((block_rows, width), lambda g, m, order: (m, 0)),
                pl.BlockSpec((block_rows, width), lambda g, m, order: (m, 0)),
                pl.BlockSpec((width, 4 * LANES), lambda g, m, order: (0, g)),
                pl.BlockSpec((1, 1, 3 * LANES), lambda g, m, order: (g, 0, 0)),
                pl.BlockSpec((2, block_rows, LANES), lambda g, m, order: (0, order[m], 0)),
            ],
            out_specs=pl.BlockSpec(
                (1, 1, block_rows, 4 * LANES), lambda g, m, order: (g, m, 0, 0)
            ),
        ),
        compiler_params=pltpu.CompilerParams(vmem_limit_bytes=VMEM_BYTES),
        cost_estimate=pl.CostEstimate(
            flops=2 * tokens * width * weight.shape[1],
            bytes_accessed=2 * (weight.size + groups * tokens * 4 * LANES + 2 * normed.size),
            transcendentals=0,
        ),
    )(own_order, normed, grad_rows, weight, bias, table)


def attend_kernel(blocks, block_rows, scale, rank_ref, table_ref, *refs):
    chunk_refs, out_refs = refs[:blocks], refs[blocks : 2 * blocks]
    q_s, k_s, v_s, d_s, kt_s, vt_s, ot_s, qt_s, dk_s, dv_s = refs[2 * blocks :]
    for index in range(blocks):
        rows = pl.ds(pl.multiple_of(rank_ref[index] * block_rows, block_rows), block_rows)
        q_s[rows, :] = chunk_refs[index][:, :LANES]
        k_s[rows, :] = chunk_refs[index][:, LANES : 2 * LANES]
        v_s[rows, :] = chunk_refs[index][:, 2 * LANES : 3 * LANES]
        d_s[rows, :] = chunk_refs[index][:, 3 * LANES :]
    kt_s[...] = k_s[...].T
    vt_s[...] = v_s[...].T
    dk_s[...] = jnp.zeros_like(dk_s)
    dv_s[...] = jnp.zeros_like(dv_s)
    lane = lax.broadcasted_iota(jnp.int32, (block_rows, LANES), 1)
    matmul = lambda a, b: jnp.dot(a, b, preferred_element_type=F32)
    outer = lambda a, b: lax.dot_general(a, b, (((1,), (1,)), ((), ())), preferred_element_type=F32)
    for rank in range(blocks):
        rows = slice(rank * block_rows, (rank + 1) * block_rows)
        keys = slice(0, (rank + 1) * block_rows)
        for head in range(LANES // HD):
            inside = (lane // HD) == head
            heads = slice(head * HD, (head + 1) * HD)
            q_h = jnp.where(inside, q_s[rows, :], 0).astype(BF16)
            d_h = jnp.where(inside, d_s[rows, :], 0).astype(BF16)
            scores = outer(k_s[keys, :], q_h) * scale
            weights = jnp.exp(scores - jnp.max(scores, axis=0, keepdims=True))
            weights = weights * (1.0 / jnp.sum(weights, axis=0, keepdims=True))
            low = weights.astype(BF16)
            ot_s[heads, rows] = matmul(vt_s[heads, keys], low)
            dv_s[keys, :] += matmul(low, d_h)
            slope = outer(v_s[keys, :], d_h)
            delta = jnp.sum(weights * slope, axis=0, keepdims=True)
            slope = (weights * (slope - delta)).astype(BF16)
            qt_s[heads, rows] = matmul(kt_s[heads, keys], slope)
            dk_s[keys, :] += matmul(slope, q_h)
    for index in range(blocks):
        rows = pl.ds(pl.multiple_of(rank_ref[index] * block_rows, block_rows), block_rows)
        cosine, sine = table_ref[0, rows, :], -table_ref[1, rows, :]
        out_refs[index][:, :LANES] = ot_s[:, rows].T.astype(BF16)
        out_refs[index][:, LANES : 2 * LANES] = turn(qt_s[:, rows].T * scale, cosine, sine).astype(BF16)
        out_refs[index][:, 2 * LANES : 3 * LANES] = turn(dk_s[rows, :] * scale, cosine, sine).astype(BF16)
        out_refs[index][:, 3 * LANES :] = dv_s[rows, :].astype(BF16)


def attend(ranks, table, chunks):
    blocks, block_rows = len(chunks), chunks[0].shape[0]
    length = blocks * block_rows
    spec = pl.BlockSpec(memory_space=pltpu.VMEM)
    pairs = blocks * (blocks + 1) // 2 * block_rows * block_rows
    return pl.pallas_call(
        lambda *refs: attend_kernel(blocks, block_rows, HD ** (-0.5), *refs),
        out_shape=[jax.ShapeDtypeStruct(chunk.shape, BF16) for chunk in chunks],
        in_specs=[pl.BlockSpec(memory_space=pltpu.SMEM), spec] + [spec] * blocks,
        out_specs=[spec] * blocks,
        scratch_shapes=[pltpu.VMEM((length, LANES), BF16)] * 4
        + [pltpu.VMEM((LANES, length), BF16)] * 2
        + [pltpu.VMEM((LANES, length), F32)] * 2
        + [pltpu.VMEM((length, LANES), F32)] * 2,
        compiler_params=pltpu.CompilerParams(vmem_limit_bytes=VMEM_BYTES),
        cost_estimate=pl.CostEstimate(
            flops=pairs * 2 * 2 * LANES * 7,
            bytes_accessed=length * 4 * LANES * 4,
            transcendentals=pairs * 2,
        ),
    )(ranks, table, *chunks)


def exchange_attention(packed, order, table):
    groups, micro, block_rows, width = packed.shape
    z = lax.axis_index("ctx")
    results = []
    for m in range(micro):
        chunks = []
        for step in range(groups):
            chunk = lax.dynamic_slice(packed, ((z + step) % groups, m, 0, 0), (1, 1, block_rows, width))
            chunk = chunk.reshape(block_rows, width)
            chunks.append(chunk if step == 0 else rotate_ring(chunk, "ctx", step))
        ranks = jnp.stack([order[m, (z - step) % groups] for step in range(groups)])
        outs = attend(ranks, table, chunks)
        back = jnp.zeros((groups, block_rows, width), BF16)
        for step in range(groups):
            got = outs[step] if step == 0 else rotate_ring(outs[step], "ctx", groups - step)
            back = place(back, got[None], ((z + step) % groups, 0, 0))
        results.append(back)
    return results


def gathered_attention(packed, order, table):
    groups, micro, block_rows, width = packed.shape
    ctx, z = lax.axis_size("ctx"), lax.axis_index("ctx")
    heads = groups * LANES // HD
    scale = HD ** (-0.5)

    def split(array):
        lead = array.shape[:-2]
        array = array.reshape(*lead, block_rows, LANES // HD, HD)
        array = jnp.moveaxis(array, 0, -3)
        return array.reshape(*array.shape[:-3], heads, HD)

    results = []
    for m in range(micro):
        own = order[m, z]
        parts = packed[:, m].reshape(groups, block_rows, 4, LANES)
        queries, keys, values, douts = (split(parts[:, :, i]) for i in range(4))
        all_keys = lax.all_gather(keys, "ctx", axis=0)
        all_values = lax.all_gather(values, "ctx", axis=0)
        allowed = order[m] <= own

        def peak_step(state, item):
            key, value, ok = item
            peak, total, sums = state
            scores = jnp.einsum("bhe,rhe->hbr", queries, key, preferred_element_type=F32) * scale
            scores = jnp.where(ok, scores, -1e30)
            new = jnp.maximum(peak, jnp.max(scores, axis=-1))
            weights = jnp.where(ok, jnp.exp(scores - new[..., None]), 0.0)
            keep = jnp.exp(peak - new)
            part = jnp.einsum("hbr,rhe->hbe", weights.astype(BF16), value, preferred_element_type=F32)
            return (new, total * keep + jnp.sum(weights, axis=-1), sums * keep[..., None] + part), None

        start = (
            jnp.full((heads, block_rows), -1e30, F32),
            jnp.zeros((heads, block_rows), F32),
            jnp.zeros((heads, block_rows, HD), F32),
        )
        (peak, total, sums), _ = lax.scan(peak_step, start, (all_keys, all_values, allowed))
        attended = jnp.transpose(sums / total[..., None], (1, 0, 2))
        level = peak + jnp.log(total)
        delta = jnp.transpose(jnp.sum(douts.astype(F32) * attended, axis=-1))

        def back_step(query_sum, item):
            key, value, ok = item
            scores = jnp.einsum("bhe,rhe->hbr", queries, key, preferred_element_type=F32) * scale
            weights = jnp.where(ok, jnp.exp(scores - level[..., None]), 0.0)
            value_grad = jnp.einsum("hbr,bhe->rhe", weights.astype(BF16), douts, preferred_element_type=F32)
            slope = jnp.einsum("bhe,rhe->hbr", douts, value, preferred_element_type=F32)
            slope = (weights * (slope - delta[..., None])).astype(BF16)
            query_part = jnp.einsum("hbr,rhe->bhe", slope, key, preferred_element_type=F32) * scale
            key_grad = jnp.einsum("hbr,bhe->rhe", slope, queries, preferred_element_type=F32) * scale
            return query_sum + query_part, (key_grad.astype(BF16), value_grad.astype(BF16))

        query_grad, (key_grads, value_grads) = lax.scan(
            back_step, jnp.zeros(queries.shape, F32), (all_keys, all_values, allowed)
        )
        key_grad = lax.psum_scatter(key_grads, "ctx", scatter_dimension=0).astype(F32)
        value_grad = lax.psum_scatter(value_grads, "ctx", scatter_dimension=0)
        rows = lax.dynamic_slice(table, (0, own * block_rows, 0), (2, block_rows, LANES))

        def join(array):
            array = array.reshape(block_rows, groups, LANES)
            return jnp.transpose(array, (1, 0, 2))

        def unturn(array):
            half = ROT // 2
            cosine, sine = rows[0, :, :half][:, None], rows[1, :, :half][:, None]
            first, second = array[..., :half], array[..., half:ROT]
            return jnp.concatenate(
                [first * cosine + second * sine, second * cosine - first * sine, array[..., ROT:]], axis=-1
            )

        results.append(
            jnp.concatenate(
                [
                    join(attended.astype(BF16)),
                    join(unturn(query_grad).astype(BF16)),
                    join(unturn(key_grad).astype(BF16)),
                    join(value_grad.astype(BF16)),
                ],
                axis=-1,
            )
        )
    return results


def across(lhs, rhs):
    return lax.dot_general(lhs, rhs, (((0,), (0,)), ((), ())), preferred_element_type=F32)


def against(lhs, rhs):
    return lax.dot_general(lhs, rhs, (((1,), (1,)), ((), ())), preferred_element_type=F32)


def local(
    inputs,
    block_order,
    first_gain,
    first_shift,
    second_gain,
    second_shift,
    qkv_weight,
    qkv_bias,
    out_weight,
    out_bias,
    up_weight,
    up_bias,
    down_weight,
    down_bias,
    out_grad,
):
    micro, block_rows, seqs, width = inputs.shape
    fsdp, ctx = lax.axis_size("fsdp"), lax.axis_size("ctx")
    z = lax.axis_index("ctx")
    rows = up_weight.shape[0]
    head_width, hidden_width = qkv_weight.shape[2], up_weight.shape[1]
    groups = head_width // LANES
    tokens = micro * block_rows
    order = block_order[:, 0]

    bits = [1 << i for i in range(fsdp.bit_length() - 1)]
    bit_orders = (bits, bits[::-1])

    attention_shard = jnp.concatenate([qkv_weight, jnp.transpose(out_weight)[None]], axis=0)
    attention_shard = jnp.transpose(attention_shard.reshape(4, rows, groups, LANES), (1, 2, 0, 3))
    attention_weight = gather_rows(attention_shard.reshape(rows, 4 * head_width), bit_orders)
    up_full = gather_rows(up_weight, bit_orders)
    down_full = gather_rows(jnp.transpose(down_weight), bit_orders)

    halves = ROT // 2
    frequency = jnp.exp(jnp.arange(halves, dtype=F32) * (-2.0 * math.log(10000.0) / ROT))
    angles = jnp.arange(ctx * block_rows, dtype=F32)[:, None] * frequency
    rest = ((0, 0), (0, HD - ROT))
    cosine = jnp.pad(jnp.tile(jnp.cos(angles), (1, 2)), rest, constant_values=1.0)
    sine = jnp.pad(jnp.tile(jnp.sin(angles), (1, 2)), rest)
    table = jnp.tile(jnp.stack([cosine, sine]), (1, 1, LANES // HD))

    values = inputs.reshape(tokens, width).astype(F32)
    grad_rows = out_grad.reshape(tokens, width)
    gains = [item.astype(F32) for item in (first_gain, first_shift, second_gain, second_shift)]
    centre = jnp.mean(values, axis=-1, keepdims=True)
    offset = values - centre
    spread = lax.rsqrt(jnp.mean(offset * offset, axis=-1, keepdims=True) + 1e-05)
    normal = offset * spread
    normed_one = (normal * gains[0] + gains[1]).astype(BF16)
    normed_two = (normal * gains[2] + gains[3]).astype(BF16)

    own_order = lax.dynamic_slice(order, (0, z), (micro, 1))[:, 0]
    bias = jnp.transpose(qkv_bias.astype(F32).reshape(3, groups, LANES), (1, 0, 2))
    packed = project(
        own_order, normed_one, grad_rows, attention_weight, bias.reshape(groups, 1, 3 * LANES), table, block_rows
    )
    attention = exchange_attention if groups == ctx else gathered_attention
    returned = jnp.stack(attention(packed, order, table), axis=1)

    up_pre = jnp.dot(normed_two, up_full, preferred_element_type=F32) + up_bias.astype(F32)
    hidden, pull = jax.vjp(lambda item: jax.nn.gelu(item, approximate=False), up_pre)
    hidden = hidden.astype(BF16)
    hidden_grad = jnp.dot(grad_rows, down_full, preferred_element_type=F32)
    up_grad = pull(hidden_grad)[0].astype(BF16)

    part = hidden_width // 2
    down_sums = jnp.concatenate(
        [
            scatter_rows(across(grad_rows, hidden[:, i * part : (i + 1) * part]), bit_orders[i])
            for i in range(2)
        ],
        axis=1,
    )
    up_sums = jnp.concatenate(
        [
            scatter_rows(across(normed_two, up_grad[:, i * part : (i + 1) * part]), bit_orders[i])
            for i in range(2)
        ],
        axis=1,
    )
    branch = against(hidden, down_full)
    normed_grad_two = against(up_grad, up_full)

    returned = returned.reshape(groups, tokens, 4 * LANES)
    flat = jnp.transpose(returned, (1, 0, 2))
    attended = flat[:, :, :LANES].reshape(tokens, head_width)
    pre_grad = flat[:, :, LANES:].reshape(tokens, 3 * head_width)
    weight_groups = attention_weight.reshape(width, groups, 4 * LANES)
    out_full = weight_groups[:, :, 3 * LANES :].reshape(width, head_width)
    qkv_full = weight_groups[:, :, : 3 * LANES].reshape(width, 3 * head_width)
    branch = branch + against(attended, out_full)
    normed_grad_one = against(pre_grad, qkv_full)

    qkv_part = across(normed_one, pre_grad).reshape(width, groups, 3 * LANES)
    out_part = across(grad_rows, attended).reshape(width, groups, LANES)
    attention_part = jnp.concatenate([qkv_part, out_part], axis=2).reshape(width, 4 * head_width)
    part = 2 * head_width
    attention_sums = jnp.concatenate(
        [scatter_rows(attention_part[:, i * part : (i + 1) * part], bit_orders[i]) for i in range(2)], axis=1
    )
    attention_sums = attention_sums.reshape(rows, groups, 4, LANES)
    qkv_sums = jnp.transpose(attention_sums[:, :, :3], (2, 0, 1, 3)).reshape(3, rows, head_width)
    out_sums = jnp.transpose(attention_sums[:, :, 3].reshape(rows, head_width))

    end_shift = out_bias.astype(F32) + down_bias.astype(F32)
    branch_low = branch.astype(BF16)
    branch_total = branch_low.astype(F32) + other_core(branch_low).astype(F32)
    outputs = (values + branch_total + end_shift).astype(BF16)

    slope = (normed_grad_one * gains[0] + normed_grad_two * gains[2]).astype(BF16)
    slope = slope.astype(F32) + other_core(slope).astype(F32)
    slope_mean = jnp.mean(slope, axis=-1, keepdims=True)
    slope_dot = jnp.mean(slope * normal, axis=-1, keepdims=True)
    input_grad = grad_rows.astype(F32) + spread * (slope - slope_mean - normal * slope_dot)

    norm_sums = jnp.stack(
        [
            jnp.sum(normed_grad_one * normal, axis=0),
            jnp.sum(normed_grad_one, axis=0),
            jnp.sum(normed_grad_two * normal, axis=0),
            jnp.sum(normed_grad_two, axis=0),
        ]
    )
    norm_sums = norm_sums + other_core(norm_sums)
    pre_sums = jnp.sum(pre_grad.astype(F32), axis=0).reshape(groups, 3, LANES)
    pre_sums = jnp.transpose(pre_sums, (1, 0, 2)).reshape(-1)
    small = jnp.concatenate(
        [
            norm_sums.reshape(-1),
            jnp.sum(grad_rows.astype(F32), axis=0),
            pre_sums,
            jnp.sum(up_grad.astype(F32), axis=0),
        ]
    )
    small = sum_small(small.reshape(-1, LANES)).reshape(-1)
    edges = [0]
    for extent in (width, width, width, width, width, 3 * head_width, hidden_width):
        edges.append(edges[-1] + extent)
    small = [small[a:b] for a, b in zip(edges[:-1], edges[1:])]
    return (
        outputs.reshape(inputs.shape),
        input_grad.astype(BF16).reshape(inputs.shape),
        small[0],
        small[1],
        small[2],
        small[3],
        qkv_sums,
        small[5].reshape(3, head_width),
        out_sums,
        small[4],
        up_sums,
        small[6],
        jnp.transpose(down_sums),
        small[4],
    )


def solution(mesh):
    placed = (
        P(None, "ctx", "fsdp", None),
        P(None, "fsdp", None),
        P(),
        P(),
        P(),
        P(),
        P(None, ("fsdp", "ctx"), "tp"),
        P(None, "tp"),
        P("tp", ("fsdp", "ctx")),
        P(),
        P(("fsdp", "ctx"), "tp"),
        P("tp"),
        P("tp", ("fsdp", "ctx")),
        P(),
        P(None, "ctx", "fsdp", None),
    )
    return jax.shard_map(
        local,
        mesh=mesh,
        in_specs=placed,
        out_specs=(
            P(None, "ctx", "fsdp", None),
            P(None, "ctx", "fsdp", None),
            P(),
            P(),
            P(),
            P(),
            P(None, ("fsdp", "ctx"), "tp"),
            P(None, "tp"),
            P("tp", ("fsdp", "ctx")),
            P(),
            P(("fsdp", "ctx"), "tp"),
            P("tp"),
            P("tp", ("fsdp", "ctx")),
            P(),
        ),
        check_vma=False,
    )
```

```python
import math

import jax
import jax.numpy as jnp
from jax import lax
from jax.experimental import pallas as pl
from jax.experimental.pallas import tpu as pltpu
from jax.sharding import PartitionSpec as P

HD = 64
ROT = 16
LANES = 128
F32 = jnp.float32
BF16 = jnp.bfloat16
VMEM_BYTES = 56 * 1024 * 1024
EPSILON = 1e-05


def swap(value, axis, bit):
    size = lax.axis_size(axis)
    return lax.ppermute(value, axis, [(i, i ^ bit) for i in range(size)])


def sequence_of(bits):
    offsets = [0]
    for bit in bits:
        offsets += [offset | bit for offset in offsets]
    return offsets


def gather_column(shard):
    return jnp.concatenate([shard] + [swap(shard, "ctx", j) for j in range(1, lax.axis_size("ctx"))], axis=0)


def gather_pieces(column, bits):
    pieces = {0: column}
    for bit in bits:
        for offset in list(pieces):
            pieces[offset | bit] = swap(pieces[offset], "fsdp", bit)
    return [pieces[offset] for offset in range(len(pieces))]


def scatter_pieces(keep, send, bits):
    for bit in reversed(bits):
        got = swap(send, "fsdp", bit).astype(F32)
        half = keep.shape[0] // 2
        if half:
            send = (keep[half:] + got[half:]).astype(BF16)
            keep = keep[:half] + got[:half]
        else:
            keep = keep + got
    return keep[0]


def scatter_column(parts):
    ctx = lax.axis_size("ctx")
    rows = parts[0].shape[0] // ctx
    cut = lambda j: jnp.concatenate([part[j * rows : (j + 1) * rows] for part in parts], axis=1)
    total = cut(0)
    for j in range(1, ctx):
        total = total + swap(cut(j).astype(BF16), "ctx", j).astype(F32)
    return total


def sum_small(value):
    for axis in ("fsdp", "ctx"):
        bit = 1
        while bit < lax.axis_size(axis):
            value = value + swap(value, axis, bit)
            bit *= 2
    return value


def unpermute(vectors, rows):
    width = vectors.shape[-1]
    index = lax.axis_index("fsdp") * lax.axis_size("ctx") + lax.axis_index("ctx")
    blocks = vectors.reshape(-1, width // rows, rows)
    bit = 1
    while bit < width // rows:
        paired = blocks.reshape(blocks.shape[0], -1, 2, bit, rows)
        blocks = jnp.where((index & bit) != 0, paired[:, :, ::-1], paired).reshape(blocks.shape)
        bit *= 2
    return blocks.reshape(vectors.shape)


def params(**more):
    return pltpu.CompilerParams(vmem_limit_bytes=VMEM_BYTES, **more)


def matmul(lhs, rhs):
    return jnp.dot(lhs, rhs, preferred_element_type=F32)


def against(lhs, rhs):
    return lax.dot_general(lhs, rhs, (((1,), (1,)), ((), ())), preferred_element_type=F32)


def exchanged(load, width, index, rows):
    shift = index * rows
    high, low = shift // LANES, lax.rem(shift, LANES)
    blocks = []
    for block in range(width // LANES):
        start = pl.multiple_of((block ^ high) * LANES, LANES)
        value = load(pl.ds(start, LANES)).astype(F32)
        step = rows
        while step < LANES:
            lane = lax.broadcasted_iota(jnp.int32, value.shape, 1)
            turned = jnp.where((lane & step) != 0, pltpu.roll(value, step, 1), pltpu.roll(value, LANES - step, 1))
            value = jnp.where((low & step) != 0, turned, value)
            step *= 2
        blocks.append(value)
    return jnp.concatenate(blocks, axis=1)


def normal_of(values):
    centre = jnp.mean(values, axis=-1, keepdims=True)
    offset = values - centre
    spread = lax.rsqrt(jnp.mean(offset * offset, axis=-1, keepdims=True) + EPSILON)
    return offset * spread, spread


def prepare_kernel(rows, index_ref, x_ref, g_ref, gains_ref, x_out, g_out, one_out, two_out, one_t, two_t, g_t, sum_out):
    width = x_ref.shape[1]
    index = index_ref[0]
    values = exchanged(lambda lanes: x_ref[:, lanes], width, index, rows)
    grads = exchanged(lambda lanes: g_ref[:, lanes], width, index, rows)
    gains = exchanged(lambda lanes: gains_ref[:, lanes], width, index, rows)
    normal, _ = normal_of(values)
    one = normal * gains[0:1] + gains[1:2]
    two = normal * gains[2:3] + gains[3:4]
    x_out[...] = values.astype(BF16)
    g_out[...] = grads.astype(BF16)
    one_out[...] = one.astype(BF16)
    two_out[...] = two.astype(BF16)
    one_t[...] = one.T.astype(BF16)
    two_t[...] = two.T.astype(BF16)
    g_t[...] = grads.T.astype(BF16)

    @pl.when(pl.program_id(0) == 0)
    def _():
        sum_out[...] = jnp.zeros_like(sum_out)

    sum_out[...] += jnp.sum(g_ref[...].astype(F32), axis=0, keepdims=True)


def prepare(index, x, g, gains, rows, block_rows):
    tokens, width = x.shape
    row_spec = pl.BlockSpec((block_rows, width), lambda m, *_: (m, 0))
    column_spec = pl.BlockSpec((width, block_rows), lambda m, *_: (0, m))
    plain = jax.ShapeDtypeStruct((tokens, width), BF16)
    turned = jax.ShapeDtypeStruct((width, tokens), BF16)
    return pl.pallas_call(
        lambda *refs: prepare_kernel(rows, *refs),
        out_shape=[plain] * 4 + [turned] * 3 + [jax.ShapeDtypeStruct((1, width), F32)],
        grid_spec=pltpu.PrefetchScalarGridSpec(
            num_scalar_prefetch=1,
            grid=(tokens // block_rows,),
            in_specs=[row_spec, row_spec, pl.BlockSpec(gains.shape, lambda m, *_: (0, 0))],
            out_specs=[row_spec] * 4 + [column_spec] * 3 + [pl.BlockSpec((1, width), lambda m, *_: (0, 0))],
        ),
        compiler_params=params(),
        cost_estimate=pl.CostEstimate(flops=tokens * width * 30, bytes_accessed=tokens * width * 18, transcendentals=0),
        name="prepare",
    )(index, x, g, gains)


def turn(values, cosine, sine):
    lane = lax.broadcasted_iota(jnp.int32, values.shape, 1) % HD
    ahead = pltpu.roll(values, LANES - ROT // 2, 1)
    behind = pltpu.roll(values, ROT // 2, 1)
    return values * cosine + jnp.where(lane < ROT // 2, ahead, behind) * sine


def project_kernel(fsdp, groups, parts, block_rows, place_ref, order_ref, one_ref, g_ref, table_ref, bias_ref, *refs):
    qk_refs, vo_refs, out_refs = refs[:fsdp], refs[fsdp : 2 * fsdp], refs[2 * fsdp :]
    tokens, width = one_ref.shape
    span = width // fsdp
    slot = pl.program_id(0)
    qk, value, back = bias_ref[0, :, : 2 * LANES], bias_ref[0, :, 2 * LANES :], None
    for offset in range(fsdp):
        lanes = slice(offset * span, (offset + 1) * span)
        qk = qk + matmul(one_ref[:, lanes], qk_refs[offset][...])
        value = value + matmul(one_ref[:, lanes], vo_refs[offset][:, :LANES])
        part = matmul(g_ref[:, lanes], vo_refs[offset][:, LANES:])
        back = part if back is None else back + part
    pieces = []
    for m in range(tokens // block_rows):
        rows = slice(m * block_rows, (m + 1) * block_rows)
        places = pl.ds(pl.multiple_of(order_ref[m] * block_rows, block_rows), block_rows)
        cosine, sine = table_ref[0, places, :], table_ref[1, places, :]
        pieces.append(
            jnp.concatenate(
                [turn(qk[rows, :LANES], cosine, sine), turn(qk[rows, LANES:], cosine, sine), value[rows], back[rows]],
                axis=1,
            ).astype(BF16)
        )
    for index in range(groups):

        @pl.when(slot == index)
        def _():
            start = 0
            for number, count in enumerate(parts):
                for m in range(count):
                    out_refs[index * len(parts) + number][m] = pieces[start + m]
                start += count


def project(place, own_order, one, g, table, bias, qk_pieces, vo_pieces, parts, block_rows):
    tokens, width = one.shape
    fsdp = len(qk_pieces)
    groups = bias.shape[0]
    span = width // fsdp
    whole = pl.BlockSpec(one.shape, lambda s, place, order: (0, 0))
    piece = pl.BlockSpec((span, 2 * LANES), lambda s, place, order: (0, place[0] ^ s))
    shapes = [jax.ShapeDtypeStruct((count, block_rows, 4 * LANES), BF16) for count in parts] * groups
    return pl.pallas_call(
        lambda *refs: project_kernel(fsdp, groups, parts, block_rows, *refs),
        out_shape=shapes,
        grid_spec=pltpu.PrefetchScalarGridSpec(
            num_scalar_prefetch=2,
            grid=(groups,),
            in_specs=[
                whole,
                whole,
                pl.BlockSpec(table.shape, lambda s, place, order: (0, 0, 0)),
                pl.BlockSpec((1, 1, 3 * LANES), lambda s, place, order: (place[0] ^ s, 0, 0)),
            ]
            + [piece] * (2 * fsdp),
            out_specs=[pl.BlockSpec(item.shape, lambda s, place, order: (0, 0, 0)) for item in shapes],
        ),
        compiler_params=params(),
        cost_estimate=pl.CostEstimate(
            flops=2 * tokens * width * groups * 4 * LANES,
            bytes_accessed=2 * (width * groups * 4 * LANES + tokens * groups * 4 * LANES + 2 * tokens * width),
            transcendentals=0,
        ),
        name="project",
    )(place, own_order, one, g, table, bias, *qk_pieces, *vo_pieces)


def attend_kernel(blocks, block_rows, scale, rank_ref, table_ref, *refs):
    chunk_refs, out_refs = refs[:blocks], refs[blocks : 2 * blocks]
    q_s, k_s, v_s, d_s, kt_s, vt_s, ot_s, qt_s, dk_s, dv_s = refs[2 * blocks :]
    item = pl.program_id(0)

    def rows_of(index):
        return pl.ds(pl.multiple_of(rank_ref[item * blocks + index] * block_rows, block_rows), block_rows)

    for index in range(blocks):
        rows = rows_of(index)
        q_s[rows, :] = chunk_refs[index][0, :, :LANES]
        k_s[rows, :] = chunk_refs[index][0, :, LANES : 2 * LANES]
        v_s[rows, :] = chunk_refs[index][0, :, 2 * LANES : 3 * LANES]
        d_s[rows, :] = chunk_refs[index][0, :, 3 * LANES :]
    kt_s[...] = k_s[...].T
    vt_s[...] = v_s[...].T
    lane = lax.broadcasted_iota(jnp.int32, (block_rows, LANES), 1)
    for rank in reversed(range(blocks)):
        rows = slice(rank * block_rows, (rank + 1) * block_rows)
        keys = slice(0, (rank + 1) * block_rows)
        dk, dv = None, None
        for head in range(LANES // HD):
            inside = (lane // HD) == head
            heads = slice(head * HD, (head + 1) * HD)
            q_h = jnp.where(inside, q_s[rows, :], 0).astype(BF16)
            d_h = jnp.where(inside, d_s[rows, :], 0).astype(BF16)
            scores = against(k_s[keys, :], q_h) * scale
            weights = jnp.exp(scores - jnp.max(scores, axis=0, keepdims=True))
            weights = weights * (1.0 / jnp.sum(weights, axis=0, keepdims=True))
            low = weights.astype(BF16)
            ot_s[heads, rows] = matmul(vt_s[heads, keys], low)
            dv_part = matmul(low, d_h)
            slope = against(v_s[keys, :], d_h)
            delta = jnp.sum(weights * slope, axis=0, keepdims=True)
            slope = (weights * (slope - delta)).astype(BF16)
            qt_s[heads, rows] = matmul(kt_s[heads, keys], slope)
            dk_part = matmul(slope, q_h)
            dk, dv = (dk_part, dv_part) if dk is None else (dk + dk_part, dv + dv_part)
        if rank == blocks - 1:
            dk_s[...], dv_s[...] = dk, dv
        else:
            dk_s[keys, :] += dk
            dv_s[keys, :] += dv
    for index in range(blocks):
        rows = rows_of(index)
        cosine, sine = table_ref[0, rows, :], -table_ref[1, rows, :]
        out_refs[index][0, :, :LANES] = turn(qt_s[:, rows].T * scale, cosine, sine).astype(BF16)
        out_refs[index][0, :, LANES : 2 * LANES] = turn(dk_s[rows, :] * scale, cosine, sine).astype(BF16)
        out_refs[index][0, :, 2 * LANES : 3 * LANES] = dv_s[rows, :].astype(BF16)
        out_refs[index][0, :, 3 * LANES :] = ot_s[:, rows].T.astype(BF16)


def attend(ranks, table, chunks):
    blocks = len(chunks)
    count, block_rows, _ = chunks[0].shape
    length = blocks * block_rows
    spec = pl.BlockSpec((1, block_rows, 4 * LANES), lambda m, *_: (m, 0, 0))
    pairs = count * blocks * (blocks + 1) // 2 * block_rows * block_rows
    return pl.pallas_call(
        lambda *refs: attend_kernel(blocks, block_rows, HD ** (-0.5), *refs),
        out_shape=[jax.ShapeDtypeStruct(chunk.shape, BF16) for chunk in chunks],
        grid_spec=pltpu.PrefetchScalarGridSpec(
            num_scalar_prefetch=1,
            grid=(count,),
            in_specs=[pl.BlockSpec(table.shape, lambda m, *_: (0, 0, 0))] + [spec] * blocks,
            out_specs=[spec] * blocks,
            scratch_shapes=[pltpu.VMEM((length, LANES), BF16)] * 4
            + [pltpu.VMEM((LANES, length), BF16)] * 2
            + [pltpu.VMEM((LANES, length), F32)] * 2
            + [pltpu.VMEM((length, LANES), F32)] * 2,
        ),
        compiler_params=params(),
        cost_estimate=pl.CostEstimate(
            flops=pairs * 2 * 2 * LANES * 7 * 2,
            bytes_accessed=count * length * 4 * LANES * 4,
            transcendentals=pairs * 2,
        ),
        name="attend",
    )(ranks, table, *chunks)


def forward_kernel(fsdp, up_sequence, down_sequence, two_ref, g_ref, two_t, g_t, bias_ref, *refs):
    up_refs, down_refs = refs[:fsdp], refs[fsdp : 2 * fsdp]
    branch_ref, slope_ref, up_keep, up_send, down_keep, down_send, sum_ref = refs[2 * fsdp :]
    tokens, width = two_ref.shape
    span = width // fsdp
    lanes = [slice(offset * span, (offset + 1) * span) for offset in range(fsdp)]

    @pl.when(pl.program_id(0) == 0)
    def _():
        branch_ref[...] = jnp.zeros_like(branch_ref)
        slope_ref[...] = jnp.zeros_like(slope_ref)

    pre, back = bias_ref[...], None
    for offset in range(fsdp):
        pre = pre + matmul(two_ref[:, lanes[offset]], up_refs[offset][...])
        part = matmul(g_ref[:, lanes[offset]], down_refs[offset][...])
        back = part if back is None else back + part
    gate = 0.5 * (1.0 + lax.erf(pre * math.sqrt(0.5)))
    bell = jnp.exp(-0.5 * pre * pre) * (1.0 / math.sqrt(2.0 * math.pi))
    hidden = (pre * gate).astype(BF16)
    pre_grad = (back * (gate + pre * bell)).astype(BF16)
    sum_ref[...] = jnp.sum(pre_grad.astype(F32), axis=0, keepdims=True)
    for offset in range(fsdp):
        branch_ref[:, lanes[offset]] += against(hidden, down_refs[offset][...])
        slope_ref[:, lanes[offset]] += against(pre_grad, up_refs[offset][...])
    half = fsdp // 2
    for number in range(fsdp):
        up_part = matmul(two_t[lanes[up_sequence[number]], :], pre_grad)
        down_part = matmul(g_t[lanes[down_sequence[number]], :], hidden)
        if number < half:
            up_keep[number], down_keep[number] = up_part, down_part
        else:
            up_send[number - half], down_send[number - half] = up_part.astype(BF16), down_part.astype(BF16)


def feed_forward(two, g, two_t, g_t, bias, up_pieces, down_pieces, up_sequence, down_sequence):
    tokens, width = two.shape
    fsdp = len(up_pieces)
    span, hidden = up_pieces[0].shape
    tile = 256
    half = fsdp // 2
    whole = pl.BlockSpec((tokens, width), lambda n: (0, 0))
    whole_t = pl.BlockSpec((width, tokens), lambda n: (0, 0))
    piece = pl.BlockSpec((span, tile), lambda n: (0, n))
    stack = pl.BlockSpec((half, span, tile), lambda n: (0, 0, n))
    line = pl.BlockSpec((1, tile), lambda n: (0, n))
    keep = jax.ShapeDtypeStruct((half, span, hidden), F32)
    send = jax.ShapeDtypeStruct((half, span, hidden), BF16)
    return pl.pallas_call(
        lambda *refs: forward_kernel(fsdp, up_sequence, down_sequence, *refs),
        out_shape=[jax.ShapeDtypeStruct((tokens, width), F32)] * 2
        + [keep, send, keep, send, jax.ShapeDtypeStruct((1, hidden), F32)],
        grid=(hidden // tile,),
        in_specs=[whole, whole, whole_t, whole_t, line] + [piece] * (2 * fsdp),
        out_specs=[whole, whole, stack, stack, stack, stack, line],
        compiler_params=params(),
        cost_estimate=pl.CostEstimate(
            flops=2 * tokens * width * hidden * 6,
            bytes_accessed=4 * width * hidden + 12 * width * hidden + 16 * tokens * width,
            transcendentals=2 * tokens * hidden,
        ),
        name="feed_forward",
    )(two, g, two_t, g_t, bias, *up_pieces, *down_pieces)


def finish_kernel(fsdp, groups, parts, qk_sequence, vo_sequence, place_ref, x_ref, one_t, g_t, gains_ref, branch_ref, slope_ref, *refs):
    count = groups * len(parts)
    back_refs, qk_refs, vo_refs = refs[:count], refs[count : count + fsdp], refs[count + fsdp : count + 2 * fsdp]
    both_ref, qk_keep, qk_send, vo_keep, vo_send, norm_ref, bias_ref, stack_s, one_s, out_s = refs[count + 2 * fsdp :]
    tokens, width = x_ref.shape
    block_rows = back_refs[0].shape[1]
    span = width // fsdp
    half = fsdp // 2
    lanes = [slice(offset * span, (offset + 1) * span) for offset in range(fsdp)]
    for slot in range(groups):
        start = 0
        for number, extent in enumerate(parts):
            for m in range(extent):
                rows = slice((start + m) * block_rows, (start + m + 1) * block_rows)
                stack_s[slot, rows, :] = back_refs[slot * len(parts) + number][m]
            start += extent
    one_s[...] = jnp.zeros_like(one_s)
    out_s[...] = branch_ref[...]

    def slot_step(slot, carry):
        group = place_ref[0] ^ slot
        columns = pl.ds(pl.multiple_of(group * 2 * LANES, 2 * LANES), 2 * LANES)
        first = pl.ds(pl.multiple_of(group * 2 * LANES, LANES), LANES)
        second = pl.ds(pl.multiple_of(group * 2 * LANES + LANES, LANES), LANES)
        dqk = stack_s[slot, :, : 2 * LANES]
        dv = stack_s[slot, :, 2 * LANES : 3 * LANES]
        out = stack_s[slot, :, 3 * LANES :]
        for offset in range(fsdp):
            one_s[:, lanes[offset]] += against(dqk, qk_refs[offset][:, columns]) + against(dv, vo_refs[offset][:, first])
            out_s[:, lanes[offset]] += against(out, vo_refs[offset][:, second])
        for number in range(fsdp):
            qk_part = matmul(one_t[lanes[qk_sequence[number]], :], dqk)
            dv_part = matmul(one_t[lanes[vo_sequence[number]], :], dv)
            out_part = matmul(g_t[lanes[vo_sequence[number]], :], out)
            if number < half:
                qk_keep[number, :, columns] = qk_part
                vo_keep[number, :, first] = dv_part
                vo_keep[number, :, second] = out_part
            else:
                qk_send[number - half, :, columns] = qk_part.astype(BF16)
                vo_send[number - half, :, first] = dv_part.astype(BF16)
                vo_send[number - half, :, second] = out_part.astype(BF16)
        bias_ref[pl.ds(group, 1), :] = jnp.sum(stack_s[slot, :, : 3 * LANES].astype(F32), axis=0, keepdims=True)
        return carry

    lax.fori_loop(0, groups, slot_step, 0)
    normal, _ = normal_of(x_ref[...].astype(F32))
    one, two = one_s[...], slope_ref[...]
    norm_ref[0:1, :] = jnp.sum(one * normal, axis=0, keepdims=True)
    norm_ref[1:2, :] = jnp.sum(one, axis=0, keepdims=True)
    norm_ref[2:3, :] = jnp.sum(two * normal, axis=0, keepdims=True)
    norm_ref[3:4, :] = jnp.sum(two, axis=0, keepdims=True)
    both_ref[0] = out_s[...].astype(BF16)
    both_ref[1] = (one * gains_ref[0:1, :] + two * gains_ref[2:3, :]).astype(BF16)


def finish(place, x, one_t, g_t, gains, branch, slope, returned, qk_pieces, vo_pieces, qk_sequence, vo_sequence, parts):
    tokens, width = x.shape
    fsdp = len(qk_pieces)
    groups = len(returned) // len(parts)
    span, columns = qk_pieces[0].shape
    half = fsdp // 2
    spec = pl.BlockSpec(memory_space=pltpu.VMEM)
    keep = jax.ShapeDtypeStruct((half, span, columns), F32)
    send = jax.ShapeDtypeStruct((half, span, columns), BF16)
    arrays = [x, one_t, g_t, gains, branch, slope, *returned, *qk_pieces, *vo_pieces]
    return pl.pallas_call(
        lambda *refs: finish_kernel(fsdp, groups, parts, qk_sequence, vo_sequence, *refs),
        out_shape=[
            jax.ShapeDtypeStruct((2, tokens, width), BF16),
            keep,
            send,
            keep,
            send,
            jax.ShapeDtypeStruct((4, width), F32),
            jax.ShapeDtypeStruct((groups, 3 * LANES), F32),
        ],
        in_specs=[pl.BlockSpec(memory_space=pltpu.SMEM)] + [spec] * len(arrays),
        out_specs=[spec] * 7,
        scratch_shapes=[
            pltpu.VMEM((groups, tokens, 4 * LANES), BF16),
            pltpu.VMEM((tokens, width), F32),
            pltpu.VMEM((tokens, width), F32),
        ],
        compiler_params=params(),
        cost_estimate=pl.CostEstimate(
            flops=2 * tokens * width * groups * 4 * LANES * 2,
            bytes_accessed=20 * tokens * width + 8 * width * columns * 2,
            transcendentals=0,
        ),
        name="finish",
    )(place, *arrays)


def close_kernel(rows, index_ref, x_ref, g_ref, own_ref, other_ref, shift_ref, out_ref, grad_ref, out_s, grad_s):
    width = x_ref.shape[1]
    values = x_ref[...].astype(F32)
    normal, spread = normal_of(values)
    out_s[...] = values + (own_ref[0].astype(F32) + other_ref[0].astype(F32))
    slope = own_ref[1].astype(F32) + other_ref[1].astype(F32)
    slope_mean = jnp.mean(slope, axis=-1, keepdims=True)
    slope_dot = jnp.mean(slope * normal, axis=-1, keepdims=True)
    grad_s[...] = g_ref[...].astype(F32) + spread * (slope - slope_mean - normal * slope_dot)
    out_ref[...] = (exchanged(lambda lanes: out_s[:, lanes], width, index_ref[0], rows) + shift_ref[...]).astype(BF16)
    grad_ref[...] = exchanged(lambda lanes: grad_s[:, lanes], width, index_ref[0], rows).astype(BF16)


def close(index, x, g, own, other, shift, rows, block_rows):
    tokens, width = x.shape
    row_spec = pl.BlockSpec((block_rows, width), lambda m, *_: (m, 0))
    both_spec = pl.BlockSpec((2, block_rows, width), lambda m, *_: (0, m, 0))
    return pl.pallas_call(
        lambda *refs: close_kernel(rows, *refs),
        out_shape=[jax.ShapeDtypeStruct((tokens, width), BF16)] * 2,
        grid_spec=pltpu.PrefetchScalarGridSpec(
            num_scalar_prefetch=1,
            grid=(tokens // block_rows,),
            in_specs=[row_spec, row_spec, both_spec, both_spec, pl.BlockSpec((1, width), lambda m, *_: (0, 0))],
            out_specs=[row_spec] * 2,
            scratch_shapes=[pltpu.VMEM((block_rows, width), F32)] * 2,
        ),
        compiler_params=params(),
        cost_estimate=pl.CostEstimate(flops=tokens * width * 30, bytes_accessed=tokens * width * 16, transcendentals=0),
        name="close",
    )(index, x, g, own, other, shift)


def exchange_attention(packed, order, table, parts):
    groups = len(packed) // len(parts)
    z = lax.axis_index("ctx")
    sources = z ^ jnp.arange(groups, dtype=jnp.int32)
    ranks = jnp.sum(jnp.where(sources[:, None] == jnp.arange(groups)[None, :], order[:, None, :], 0), axis=-1)
    returned = [None] * len(packed)
    start = 0
    for number, count in enumerate(parts):
        chunks = [packed[slot * len(parts) + number] for slot in range(groups)]
        chunks = [chunk if slot == 0 else swap(chunk, "ctx", slot) for slot, chunk in enumerate(chunks)]
        outs = attend(ranks[start : start + count].reshape(-1), table, chunks)
        for slot in range(groups):
            returned[slot * len(parts) + number] = outs[slot] if slot == 0 else swap(outs[slot], "ctx", slot)
        start += count
    return returned


def gathered_attention(packed, order, table, parts):
    groups = len(packed) // len(parts)
    micro, block_rows = order.shape[0], packed[0].shape[1]
    z = lax.axis_index("ctx")
    heads = groups * LANES // HD
    scale = HD ** (-0.5)
    slots = [
        jnp.concatenate([packed[slot * len(parts) + number] for number in range(len(parts))], axis=0)
        for slot in range(groups)
    ]
    packed = jnp.stack(slots)

    def split(array):
        array = array.reshape(groups, block_rows, LANES // HD, HD)
        return jnp.transpose(array, (1, 0, 2, 3)).reshape(block_rows, heads, HD)

    def join(array):
        return jnp.transpose(array.reshape(block_rows, groups, LANES), (1, 0, 2))

    results = []
    for m in range(micro):
        own = jnp.sum(jnp.where(jnp.arange(order.shape[1]) == z, order[m], 0))
        parted = packed[:, m].reshape(groups, block_rows, 4, LANES)
        queries, keys, values, douts = (split(parted[:, :, i]) for i in range(4))
        all_keys = lax.all_gather(keys, "ctx", axis=0)
        all_values = lax.all_gather(values, "ctx", axis=0)
        allowed = order[m] <= own

        def peak_step(state, item):
            key, value, ok = item
            peak, total, sums = state
            scores = jnp.einsum("bhe,rhe->hbr", queries, key, preferred_element_type=F32) * scale
            scores = jnp.where(ok, scores, -1e30)
            new = jnp.maximum(peak, jnp.max(scores, axis=-1))
            weights = jnp.where(ok, jnp.exp(scores - new[..., None]), 0.0)
            fade = jnp.exp(peak - new)
            part = jnp.einsum("hbr,rhe->hbe", weights.astype(BF16), value, preferred_element_type=F32)
            return (new, total * fade + jnp.sum(weights, axis=-1), sums * fade[..., None] + part), None

        start = (
            jnp.full((heads, block_rows), -1e30, F32),
            jnp.zeros((heads, block_rows), F32),
            jnp.zeros((heads, block_rows, HD), F32),
        )
        (peak, total, sums), _ = lax.scan(peak_step, start, (all_keys, all_values, allowed))
        attended = jnp.transpose(sums / total[..., None], (1, 0, 2))
        level = peak + jnp.log(total)
        delta = jnp.transpose(jnp.sum(douts.astype(F32) * attended, axis=-1))

        def back_step(query_sum, item):
            key, value, ok = item
            scores = jnp.einsum("bhe,rhe->hbr", queries, key, preferred_element_type=F32) * scale
            weights = jnp.where(ok, jnp.exp(scores - level[..., None]), 0.0)
            value_grad = jnp.einsum("hbr,bhe->rhe", weights.astype(BF16), douts, preferred_element_type=F32)
            slope = jnp.einsum("bhe,rhe->hbr", douts, value, preferred_element_type=F32)
            slope = (weights * (slope - delta[..., None])).astype(BF16)
            query_part = jnp.einsum("hbr,rhe->bhe", slope, key, preferred_element_type=F32) * scale
            key_grad = jnp.einsum("hbr,bhe->rhe", slope, queries, preferred_element_type=F32) * scale
            return query_sum + query_part, (key_grad.astype(BF16), value_grad.astype(BF16))

        query_grad, (key_grads, value_grads) = lax.scan(
            back_step, jnp.zeros(queries.shape, F32), (all_keys, all_values, allowed)
        )
        key_grad = lax.psum_scatter(key_grads, "ctx", scatter_dimension=0).astype(F32)
        value_grad = lax.psum_scatter(value_grads, "ctx", scatter_dimension=0)
        rows = lax.dynamic_slice(table, (0, own * block_rows, 0), (2, block_rows, LANES))

        def unturn(array):
            half = ROT // 2
            cosine, sine = rows[0, :, :half][:, None], rows[1, :, half:ROT][:, None]
            first, second = array[..., :half], array[..., half:ROT]
            return jnp.concatenate(
                [first * cosine + second * sine, second * cosine - first * sine, array[..., ROT:]], axis=-1
            )

        fields = (unturn(query_grad), unturn(key_grad), value_grad, attended)
        results.append(jnp.concatenate([join(field.astype(BF16)) for field in fields], axis=-1))
    results = jnp.stack(results, axis=1)
    edges = [sum(parts[:number]) for number in range(len(parts) + 1)]
    return [results[slot, a:b] for slot in range(groups) for a, b in zip(edges[:-1], edges[1:])]


def rotation_table(length):
    lane = jnp.arange(LANES, dtype=jnp.int32) % HD
    halves = ROT // 2
    frequency = jnp.exp((lane % halves).astype(F32) * (-2.0 * math.log(10000.0) / ROT))
    frequency = jnp.where(lane < ROT, frequency, 0.0)
    angles = jnp.arange(length, dtype=F32)[:, None] * frequency
    return jnp.stack([jnp.cos(angles), jnp.where(lane < halves, -1.0, 1.0) * jnp.sin(angles)])


def local(
    inputs,
    block_order,
    first_gain,
    first_shift,
    second_gain,
    second_shift,
    qkv_weight,
    qkv_bias,
    out_weight,
    out_bias,
    up_weight,
    up_bias,
    down_weight,
    down_bias,
    out_grad,
):
    micro, block_rows, _, width = inputs.shape
    fsdp, ctx = lax.axis_size("fsdp"), lax.axis_size("ctx")
    f, z = lax.axis_index("fsdp"), lax.axis_index("ctx")
    rows = up_weight.shape[0]
    head_width, hidden_width = qkv_weight.shape[2], up_weight.shape[1]
    groups = head_width // LANES
    tokens = micro * block_rows
    order = block_order[:, 0]
    parts = (1, micro - 1)
    exchanging = groups == ctx

    bits = [1 << i for i in range(fsdp.bit_length() - 1)]
    back_bits = bits[::-1]
    forth, back = sequence_of(bits), sequence_of(back_bits)

    shard = jnp.concatenate([qkv_weight, jnp.transpose(out_weight)[None]], axis=0)
    shard = jnp.transpose(shard.reshape(2, 2, rows, groups, LANES), (2, 0, 3, 1, 4)).reshape(rows, 4 * head_width)
    column = gather_column(shard)
    forward_shard = jnp.concatenate([up_weight, jnp.transpose(down_weight)], axis=1)
    forward_shard, column = lax.optimization_barrier((forward_shard, column))
    qk_pieces = gather_pieces(column[:, : 2 * head_width], bits)
    vo_pieces = gather_pieces(column[:, 2 * head_width :], back_bits)
    forward_column = gather_column(forward_shard)
    up_pieces = gather_pieces(forward_column[:, :hidden_width], bits)
    down_pieces = gather_pieces(forward_column[:, hidden_width:], back_bits)

    index = (f * ctx + z).astype(jnp.int32).reshape(1)
    gains = jnp.stack([first_gain, first_shift, second_gain, second_shift]).astype(F32)
    x, g, one, two, one_t, two_t, g_t, grad_sum = prepare(
        index, inputs.reshape(tokens, width), out_grad.reshape(tokens, width), gains, rows, block_rows
    )

    table = rotation_table(ctx * block_rows)
    place = (z if exchanging else jnp.zeros_like(z)).astype(jnp.int32).reshape(1)
    own_order = jnp.sum(jnp.where(jnp.arange(ctx)[None, :] == z, order, 0), axis=1)
    bias = jnp.transpose(qkv_bias.astype(F32).reshape(3, groups, LANES), (1, 0, 2)).reshape(groups, 1, 3 * LANES)
    packed = project(place, own_order, one, g, table, bias, qk_pieces, vo_pieces, parts, block_rows)
    attention = exchange_attention if exchanging else gathered_attention
    returned = attention(packed, order, table, parts)

    branch, slope, up_keep, up_send, down_keep, down_send, up_sum = feed_forward(
        two, g, two_t, g_t, up_bias.astype(F32).reshape(1, -1), up_pieces, down_pieces, forth, back
    )
    forward_sums = scatter_column(
        [scatter_pieces(up_keep, up_send, bits), scatter_pieces(down_keep, down_send, back_bits)]
    )

    gains_here = unpermute(gains, rows)
    both, qk_keep, qk_send, vo_keep, vo_send, norm_sums, pre_sums = finish(
        place, x, one_t, g_t, gains_here, branch, slope, returned, qk_pieces, vo_pieces, forth, back, parts
    )
    attention_sums = scatter_column(
        [scatter_pieces(qk_keep, qk_send, bits), scatter_pieces(vo_keep, vo_send, back_bits)]
    )
    attention_sums = attention_sums.reshape(rows, 2, groups, 2, LANES)
    attention_sums = jnp.transpose(attention_sums, (1, 3, 0, 2, 4)).reshape(4, rows, head_width)

    end_shift = (out_bias.astype(F32) + down_bias.astype(F32)).reshape(1, width)
    outputs, input_grad = close(index, x, g, both, swap(both, "tp", 1), end_shift, rows, block_rows)

    norm_sums = unpermute(norm_sums + swap(norm_sums, "tp", 1), rows)
    pre_sums = jnp.transpose(pre_sums.reshape(groups, 3, LANES), (1, 0, 2))
    small = [norm_sums.reshape(-1), grad_sum.reshape(-1), pre_sums.reshape(-1), up_sum.reshape(-1)]
    small = sum_small(jnp.concatenate(small).reshape(-1, LANES)).reshape(-1)
    edges = [0]
    for extent in (width, width, width, width, width, 3 * head_width, hidden_width):
        edges.append(edges[-1] + extent)
    small = [small[a:b] for a, b in zip(edges[:-1], edges[1:])]
    return (
        outputs.reshape(inputs.shape),
        input_grad.reshape(inputs.shape),
        small[0],
        small[1],
        small[2],
        small[3],
        attention_sums[:3],
        small[5].reshape(3, head_width),
        jnp.transpose(attention_sums[3]),
        small[4],
        forward_sums[:, :hidden_width],
        small[6],
        jnp.transpose(forward_sums[:, hidden_width:]),
        small[4],
    )


def solution(mesh):
    placed = (
        P(None, "ctx", "fsdp", None),
        P(None, "fsdp", None),
        P(),
        P(),
        P(),
        P(),
        P(None, ("fsdp", "ctx"), "tp"),
        P(None, "tp"),
        P("tp", ("fsdp", "ctx")),
        P(),
        P(("fsdp", "ctx"), "tp"),
        P("tp"),
        P("tp", ("fsdp", "ctx")),
        P(),
        P(None, "ctx", "fsdp", None),
    )
    return jax.shard_map(
        local,
        mesh=mesh,
        in_specs=placed,
        out_specs=(
            P(None, "ctx", "fsdp", None),
            P(None, "ctx", "fsdp", None),
            P(),
            P(),
            P(),
            P(),
            P(None, ("fsdp", "ctx"), "tp"),
            P(None, "tp"),
            P("tp", ("fsdp", "ctx")),
            P(),
            P(("fsdp", "ctx"), "tp"),
            P("tp"),
            P("tp", ("fsdp", "ctx")),
            P(),
        ),
        check_vma=False,
    )
```

```python
import math

import jax
import jax.numpy as jnp
from jax import lax
from jax.experimental import pallas as pl
from jax.experimental.pallas import tpu as pltpu
from jax.sharding import PartitionSpec as P

HD = 64
ROT = 16
LANES = 128
F32 = jnp.float32
BF16 = jnp.bfloat16
VMEM_BYTES = 60 * 1024 * 1024
EPSILON = 1e-05
TASKS = (
    "finish_a",
    "weights_a",
    "forward_first",
    "finish_b",
    "weights_b",
    "forward_second",
    "sums_a",
    "attention_first",
    "sums_b",
    "close_a",
    "close_b",
)
SMALL_ROWS = 16
SHARE = 1 / 0.6


def swap(value, axis, bit):
    size = lax.axis_size(axis)
    return lax.ppermute(value, axis, [(i, i ^ bit) for i in range(size)])


def choose(bit, first, second):
    return jnp.where(bit == 0, first, second), jnp.where(bit == 0, second, first)


def gather_column(own, other):
    return [own] + [swap(other if j & 1 else own, "ctx", j) for j in range(1, lax.axis_size("ctx"))]


def gather_pieces(column):
    return [column] + [swap(column, "fsdp", j) for j in range(1, lax.axis_size("fsdp"))]


def params(**more):
    return pltpu.CompilerParams(vmem_limit_bytes=VMEM_BYTES, **more)


def launch(kernel, scalars, operands, waits, us, *, grid, in_specs, out_specs, out_shape, scratch_shapes=(), **more):
    count = (scalars is not None) + len(operands)

    def body(*refs):
        kernel(*refs[:count], *refs[count + len(waits) :])

    return pl.pallas_call(
        body,
        out_shape=out_shape,
        grid_spec=pltpu.PrefetchScalarGridSpec(
            num_scalar_prefetch=0 if scalars is None else 1,
            grid=grid,
            in_specs=[*in_specs] + [pl.BlockSpec(memory_space=pl.ANY)] * len(waits),
            out_specs=out_specs,
            scratch_shapes=scratch_shapes,
        ),
        compiler_params=params(),
        cost_estimate=pl.CostEstimate(flops=int(us * SHARE * 1.1e9), bytes_accessed=1024, transcendentals=0),
        **more,
    )(*([] if scalars is None else [scalars]), *operands, *waits)


def matmul(lhs, rhs):
    return jnp.dot(lhs, rhs, preferred_element_type=F32)


def against(lhs, rhs):
    return lax.dot_general(lhs, rhs, (((1,), (1,)), ((), ())), preferred_element_type=F32)


def exchanged(load, width, index, rows):
    shift = index * rows
    high, low = shift // LANES, lax.rem(shift, LANES)
    blocks = []
    for block in range(width // LANES):
        start = pl.multiple_of((block ^ high) * LANES, LANES)
        value = load(pl.ds(start, LANES)).astype(F32)
        step = rows
        while step < LANES:
            lane = lax.broadcasted_iota(jnp.int32, value.shape, 1)
            turned = pltpu.roll(value, step, 1)
            if 2 * step != LANES:
                turned = jnp.where((lane & step) != 0, turned, pltpu.roll(value, LANES - step, 1))
            value = jnp.where((low & step) != 0, turned, value)
            step *= 2
        blocks.append(value)
    return jnp.concatenate(blocks, axis=1)


def normal_of(values):
    centre = jnp.mean(values, axis=-1, keepdims=True)
    offset = values - centre
    spread = lax.rsqrt(jnp.mean(offset * offset, axis=-1, keepdims=True) + EPSILON)
    return offset * spread, spread


def prepare_block(rows, index, load_x, load_g, gains_ref, outs):
    x_out, g_out, one_out = outs
    width = x_out.shape[1]
    values = exchanged(load_x, width, index, rows)
    gains = exchanged(lambda lanes: gains_ref[:, lanes], width, index, rows)
    normal, _ = normal_of(values)
    x_out[...] = values.astype(BF16)
    g_out[...] = exchanged(load_g, width, index, rows).astype(BF16)
    one_out[...] = (normal * gains[0:1] + gains[1:2]).astype(BF16)


def prepare_own_kernel(rows, index_ref, x_ref, g_ref, gains_ref, *refs):
    outs, sum_out = refs[:3], refs[3]
    prepare_block(rows, index_ref[0], lambda lanes: x_ref[:, lanes], lambda lanes: g_ref[:, lanes], gains_ref, outs)

    @pl.when(pl.program_id(0) == 0)
    def _():
        sum_out[...] = jnp.zeros_like(sum_out)

    sum_out[...] += jnp.sum(g_ref[...].astype(F32), axis=0, keepdims=True)


def prepare_pair_kernel(rows, index_ref, mine_ref, other_ref, gains_ref, *refs):
    half = mine_ref.shape[2]

    def loader(field):
        def load(lanes):
            inside = pl.ds(pl.multiple_of(lax.rem(lanes.start, half), LANES), lanes.size)
            mine, other = mine_ref[field, :, inside].astype(F32), other_ref[field, :, inside].astype(F32)
            return jnp.where(lanes.start // half == index_ref[1], mine, other)

        return load

    prepare_block(rows, index_ref[0], loader(0), loader(1), gains_ref, refs[3:])


def prepare_late_kernel(rows, index_ref, x_ref, g_ref, one_ref, gains_ref, two_out, one_t, two_t, g_t):
    normal, _ = normal_of(x_ref[...].astype(F32))
    gains = exchanged(lambda lanes: gains_ref[:, lanes], x_ref.shape[1], index_ref[0], rows)
    two = (normal * gains[2:3] + gains[3:4]).astype(BF16)
    two_out[...] = two
    one_t[...] = one_ref[...].T
    two_t[...] = two.T
    g_t[...] = g_ref[...].T


def prepare_shapes(tokens, width, block_rows, first_part):
    count = tokens // block_rows

    def spec(side):
        def place(m):
            return m + jnp.where(m < first_part, side * first_part, first_part + side * (count - first_part))

        return pl.BlockSpec((block_rows, width), lambda m, *_: (place(m), 0))

    return count, [jax.ShapeDtypeStruct((2 * tokens, width), BF16)] * 3, spec


def prepare_own(index, x, g, gains, rows, block_rows, first_part, waits=()):
    tokens, width = x.shape
    count, shapes, spec = prepare_shapes(tokens, width, block_rows, first_part)
    row_spec = pl.BlockSpec((block_rows, width), lambda m, *_: (m, 0))
    *outs, grad_sum = launch(
        lambda *refs: prepare_own_kernel(rows, *refs),
        index,
        [x, g, gains],
        waits,
        2.100,
        out_shape=shapes + [jax.ShapeDtypeStruct((1, width), F32)],
        grid=(count,),
        in_specs=[row_spec, row_spec, pl.BlockSpec(gains.shape, lambda m, *_: (0, 0))],
        out_specs=[spec(0)] * 3 + [pl.BlockSpec((1, width), lambda m, *_: (0, 0))],
        name="prepare_own",
    )
    return outs, grad_sum


def prepare_pair(index, arrived, gains, outs, rows, block_rows, first_part, waits=()):
    _, tokens, half = arrived[0].shape
    count, shapes, spec = prepare_shapes(tokens, 2 * half, block_rows, first_part)
    half_spec = pl.BlockSpec((2, block_rows, half), lambda m, *_: (0, m, 0))
    return launch(
        lambda *refs: prepare_pair_kernel(rows, *refs),
        index,
        [*arrived, gains, *outs],
        waits,
        2.100,
        out_shape=shapes,
        grid=(count,),
        in_specs=[half_spec, half_spec, pl.BlockSpec(gains.shape, lambda m, *_: (0, 0))]
        + [pl.BlockSpec(memory_space=pl.ANY)] * 3,
        out_specs=[spec(1)] * 3,
        input_output_aliases={4 + i: i for i in range(3)},
        name="prepare_pair",
    )


def prepare_late(index, x, g, one, gains, rows, block_rows, waits=()):
    tokens, width = x.shape
    row_spec = pl.BlockSpec((block_rows, width), lambda m, *_: (m, 0))
    column_spec = pl.BlockSpec((width, block_rows), lambda m, *_: (0, m))
    plain, turned = jax.ShapeDtypeStruct((tokens, width), BF16), jax.ShapeDtypeStruct((width, tokens), BF16)
    return launch(
        lambda *refs: prepare_late_kernel(rows, *refs),
        index,
        [x, g, one, gains],
        waits,
        3.600,
        out_shape=[plain, turned, turned, turned],
        grid=(tokens // block_rows,),
        in_specs=[row_spec, row_spec, row_spec, pl.BlockSpec(gains.shape, lambda m, *_: (0, 0))],
        out_specs=[row_spec, column_spec, column_spec, column_spec],
        name="prepare_late",
    )


def turn(values, cosine, sine):
    lane = lax.broadcasted_iota(jnp.int32, values.shape, 1) % HD
    ahead = pltpu.roll(values, LANES - ROT // 2, 1)
    behind = pltpu.roll(values, ROT // 2, 1)
    return values * cosine + jnp.where(lane < ROT // 2, ahead, behind) * sine


def gather_weight(piece_refs, weight_s):
    @pl.when(pl.program_id(0) == 0)
    def _():
        start = 0
        for ref in piece_refs:
            weight_s[start : start + ref.shape[0], :] = ref[...]
            start += ref.shape[0]


def pick(place, first, second):
    return jnp.where(place == 0, first, second), jnp.where(place == 0, second, first)


def project_kernel(fsdp, block_rows, scalar_ref, one_ref, g_ref, table_ref, bias_ref, *refs):
    piece_refs, (local_ref, remote_ref, weight_s) = refs[:fsdp], refs[fsdp:]
    tokens, width = one_ref.shape
    gather_weight(piece_refs, weight_s)
    pre = matmul(one_ref[...], weight_s[:, : 6 * LANES]) + bias_ref[...]
    back = matmul(g_ref[...], weight_s[:, 6 * LANES :])
    for block in range(tokens // block_rows):
        rows = slice(block * block_rows, (block + 1) * block_rows)
        rank = scalar_ref[1 + pl.program_id(0) * (tokens // block_rows) + block]
        places = pl.ds(pl.multiple_of(rank * block_rows, block_rows), block_rows)
        cosine, sine = table_ref[0, places, :], table_ref[1, places, :]
        for field in range(4):
            source = pre[rows] if field < 3 else back[rows]
            start = 2 * field * LANES if field < 3 else 0
            both = [source[:, start + group * LANES : start + (group + 1) * LANES] for group in range(2)]
            if field < 2:
                both = [turn(item, cosine, sine) for item in both]
            here = slice(field * LANES, (field + 1) * LANES)
            mine, other = pick(scalar_ref[0], *both)
            local_ref[rows, here] = mine.astype(BF16)
            remote_ref[rows, here] = other.astype(BF16)


def project(place, ranks, one, g, first, count, table, bias, pieces, block_rows, waits=()):
    width = one.shape[1]
    fsdp = len(pieces)
    tokens = count * block_rows
    tile = 2 * block_rows
    base = first // 2
    side = pl.BlockSpec((tile, width), lambda t, *_: (base + t, 0))
    once = pl.Buffered(1)
    out = pl.BlockSpec((tile, 4 * LANES), lambda t, *_: (t, 0))
    return launch(
        lambda *refs: project_kernel(fsdp, block_rows, *refs),
        jnp.concatenate([place, ranks]),
        [one, g, table, bias, *pieces],
        waits,
        tokens / 500.000,
        out_shape=[jax.ShapeDtypeStruct((tokens, 4 * LANES), BF16)] * 2,
        grid=(tokens // tile,),
        in_specs=[
            side,
            side,
            pl.BlockSpec(table.shape, lambda t, *_: (0, 0, 0), pipeline_mode=once),
            pl.BlockSpec(bias.shape, lambda t, *_: (0, 0)),
        ]
        + [pl.BlockSpec(piece.shape, lambda t, *_: (0, 0), pipeline_mode=once) for piece in pieces],
        out_specs=[out, out],
        scratch_shapes=[pltpu.VMEM((width, 8 * LANES), BF16)],
        name="project",
    )


def attend_kernel(blocks, block_rows, scale, rank_ref, table_ref, *refs):
    count = blocks // 2
    chunk_refs, out_refs = refs[:count], refs[count : 2 * count]
    q_s, k_s, v_s, d_s, kt_s, vt_s, ot_s, qt_s, dk_s, dv_s = refs[2 * count :]
    item = pl.program_id(0)

    def rows_of(index):
        return pl.ds(pl.multiple_of(rank_ref[item * blocks + index] * block_rows, block_rows), block_rows)

    for index in range(blocks):
        rows, chunk, side = rows_of(index), chunk_refs[index // 2], index % 2
        q_s[rows, :] = chunk[side, 0, :, :LANES]
        k_s[rows, :] = chunk[side, 0, :, LANES : 2 * LANES]
        v_s[rows, :] = chunk[side, 0, :, 2 * LANES : 3 * LANES]
        d_s[rows, :] = chunk[side, 0, :, 3 * LANES :]
    kt_s[...] = k_s[...].T
    vt_s[...] = v_s[...].T
    lane = lax.broadcasted_iota(jnp.int32, (block_rows, LANES), 1)
    for rank in reversed(range(blocks)):
        rows = slice(rank * block_rows, (rank + 1) * block_rows)
        keys = slice(0, (rank + 1) * block_rows)
        dk, dv = None, None
        for head in range(LANES // HD):
            inside = (lane // HD) == head
            heads = slice(head * HD, (head + 1) * HD)
            q_h = jnp.where(inside, q_s[rows, :], 0).astype(BF16)
            d_h = jnp.where(inside, d_s[rows, :], 0).astype(BF16)
            scores = against(k_s[keys, :], q_h) * scale
            weights = jnp.exp(scores - jnp.max(scores, axis=0, keepdims=True))
            weights = weights * (1.0 / jnp.sum(weights, axis=0, keepdims=True))
            low = weights.astype(BF16)
            ot_s[heads, rows] = matmul(vt_s[heads, keys], low)
            dv_part = matmul(low, d_h)
            slope = against(v_s[keys, :], d_h)
            delta = jnp.sum(weights * slope, axis=0, keepdims=True)
            slope = (weights * (slope - delta)).astype(BF16)
            qt_s[heads, rows] = matmul(kt_s[heads, keys], slope)
            dk_part = matmul(slope, q_h)
            dk, dv = (dk_part, dv_part) if dk is None else (dk + dk_part, dv + dv_part)
        if rank == blocks - 1:
            dk_s[...], dv_s[...] = dk, dv
        else:
            dk_s[keys, :] += dk
            dv_s[keys, :] += dv
    for index in range(blocks):
        rows, out, side = rows_of(index), out_refs[index // 2], index % 2
        cosine, sine = table_ref[0, rows, :], -table_ref[1, rows, :]
        out[side, 0, :, :LANES] = turn(qt_s[:, rows].T * scale, cosine, sine).astype(BF16)
        out[side, 0, :, LANES : 2 * LANES] = turn(dk_s[rows, :] * scale, cosine, sine).astype(BF16)
        out[side, 0, :, 2 * LANES : 3 * LANES] = dv_s[rows, :].astype(BF16)
        out[side, 0, :, 3 * LANES :] = ot_s[:, rows].T.astype(BF16)


def attend(ranks, table, chunks, waits=()):
    sides, count, block_rows, _ = chunks[0].shape
    blocks = sides * len(chunks)
    length = blocks * block_rows
    spec = pl.BlockSpec((sides, 1, block_rows, 4 * LANES), lambda m, *_: (0, m, 0, 0))
    pairs = count * blocks * (blocks + 1) // 2 * block_rows * block_rows
    return launch(
        lambda *refs: attend_kernel(blocks, block_rows, HD ** (-0.5), *refs),
        ranks,
        [table, *chunks],
        waits,
        11 * count,
        out_shape=[jax.ShapeDtypeStruct(chunk.shape, BF16) for chunk in chunks],
        grid=(count,),
        in_specs=[pl.BlockSpec(table.shape, lambda m, *_: (0, 0, 0))] + [spec] * len(chunks),
        out_specs=[spec] * len(chunks),
        scratch_shapes=[pltpu.VMEM((length, LANES), BF16)] * 4
        + [pltpu.VMEM((LANES, length), BF16)] * 2
        + [pltpu.VMEM((LANES, length), F32)] * 2
        + [pltpu.VMEM((length, LANES), F32)] * 2,
        name="attend",
    )


def forward_kernel(fsdp, two_ref, g_ref, two_t, g_t, bias_ref, *refs):
    up_refs, down_refs = refs[:fsdp], refs[fsdp : 2 * fsdp]
    branch_ref, slope_ref, sum_ref = refs[2 * fsdp : 2 * fsdp + 3]
    out_refs, (up_s, down_s) = refs[2 * fsdp + 3 : -2], refs[-2:]
    width = two_ref.shape[1]
    span = width // fsdp
    lanes = [slice(offset * span, (offset + 1) * span) for offset in range(fsdp)]
    for offset in range(fsdp):
        up_s[lanes[offset], :] = up_refs[offset][...]
        down_s[lanes[offset], :] = down_refs[offset][...]
    pre = matmul(two_ref[...], up_s[...]) + bias_ref[...]
    back = matmul(g_ref[...], down_s[...])
    gate = 0.5 * (1.0 + lax.erf(pre * math.sqrt(0.5)))
    bell = jnp.exp(-0.5 * pre * pre) * (1.0 / math.sqrt(2.0 * math.pi))
    hidden = (pre * gate).astype(BF16)
    pre_grad = (back * (gate + pre * bell)).astype(BF16)
    sum_ref[...] = jnp.sum(pre_grad.astype(F32), axis=0, keepdims=True)

    @pl.when(pl.program_id(0) == 0)
    def _():
        branch_ref[...] = against(hidden, down_s[...])
        slope_ref[...] = against(pre_grad, up_s[...])

    @pl.when(pl.program_id(0) != 0)
    def _():
        branch_ref[...] += against(hidden, down_s[...])
        slope_ref[...] += against(pre_grad, up_s[...])

    for offset in range(fsdp):
        out = out_refs[offset]
        out[0] = matmul(two_t[lanes[offset], :], pre_grad).astype(out.dtype)
        out[1] = matmul(g_t[lanes[offset], :], hidden).astype(out.dtype)


def feed_forward(two, g, two_t, g_t, bias, pieces, waits=()):
    tokens, width = two.shape
    fsdp = len(pieces)
    span, hidden = pieces[0].shape[0], pieces[0].shape[1] // 2
    tile = 256
    tiles = hidden // tile
    once = pl.Buffered(1)
    whole = pl.BlockSpec((tokens, width), lambda n: (0, 0), pipeline_mode=once)
    whole_t = pl.BlockSpec((width, tokens), lambda n: (0, 0), pipeline_mode=once)
    piece = pl.BlockSpec((span, tile), lambda n: (0, n))
    later = pl.BlockSpec((span, tile), lambda n: (0, n + tiles))
    line = pl.BlockSpec((1, tile), lambda n: (0, n))
    grads = [jax.ShapeDtypeStruct((2, span, hidden), BF16 if offset else F32) for offset in range(fsdp)]
    grad = pl.BlockSpec((2, span, tile), lambda n: (0, 0, n))
    branch, slope, sums, *grads = launch(
        lambda *refs: forward_kernel(fsdp, *refs),
        None,
        [two, g, two_t, g_t, bias, *pieces, *pieces],
        waits,
        34,
        out_shape=[jax.ShapeDtypeStruct((tokens, width), F32)] * 2
        + [jax.ShapeDtypeStruct((1, hidden), F32)]
        + grads,
        grid=(tiles,),
        in_specs=[whole, whole, whole_t, whole_t, line] + [piece] * fsdp + [later] * fsdp,
        out_specs=[whole, whole, line] + [grad] * fsdp,
        scratch_shapes=[pltpu.VMEM((width, tile), BF16)] * 2,
        name="feed_forward",
    )
    return branch, slope, sums, grads


def collect(place, local_ref, remote_ref, stack_s):
    for ref, group in ((local_ref, place), (remote_ref, 1 - place)):
        for field in range(4):
            here = pl.ds(pl.multiple_of((2 * field + group) * LANES, LANES), LANES)
            stack_s[:, here] = ref[:, field * LANES : (field + 1) * LANES]


def weights_kernel(fsdp, last, place_ref, one_t, g_t, local_ref, remote_ref, *refs):
    before_ref, small_ref = refs[:2] if last else (None, None)
    out_refs, stack_s = refs[2 if last else 0 : -1], refs[-1]
    step = pl.program_id(0)
    span = one_t.shape[0]

    @pl.when(step == 0)
    def _():
        collect(place_ref[0], local_ref, remote_ref, stack_s)

    pre_part = matmul(one_t[...], stack_s[:, : 6 * LANES])
    out_part = matmul(g_t[...], stack_s[:, 6 * LANES :])
    if not last:
        out_refs[0][0, :, : 6 * LANES] = pre_part
        out_refs[0][0, :, 6 * LANES :] = out_part
    else:
        pre_part = pre_part + before_ref[0, :, : 6 * LANES]
        out_part = out_part + before_ref[0, :, 6 * LANES :]
        small = small_ref[...].astype(BF16)
        for offset in range(fsdp):

            @pl.when(step == offset)
            def _():
                out = out_refs[offset]
                out[0, :span, : 6 * LANES] = pre_part.astype(out.dtype)
                out[0, :span, 6 * LANES :] = out_part.astype(out.dtype)
                out[0, span:, :] = small.astype(out.dtype)


def attention_weights(place, one_t, g_t, first, local, remote, before, fsdp, waits=()):
    width = one_t.shape[0]
    tokens = local.shape[0]
    span = width // fsdp
    columns = 8 * LANES
    last = before is not None
    stack = jax.ShapeDtypeStruct((fsdp, span, columns), F32)
    grads = [
        jax.ShapeDtypeStruct((1, span + SMALL_ROWS, columns), BF16 if offset else F32) for offset in range(fsdp)
    ]
    piece = pl.BlockSpec((span, tokens), lambda o, *_: (o, first // tokens))
    slab = pl.BlockSpec((1, span, columns), lambda o, *_: (o, 0, 0))
    whole = lambda item: pl.BlockSpec(item.shape, lambda o, *_: (0,) * len(item.shape))
    grads = launch(
        lambda *refs: weights_kernel(fsdp, last, *refs),
        place,
        [one_t, g_t, local, remote, *(before if last else [])],
        waits,
        7 if last else 0.5,
        out_shape=grads if last else [stack],
        grid=(fsdp,),
        in_specs=[piece, piece, whole(local), whole(remote)] + ([slab, whole(before[1])] if last else []),
        out_specs=[whole(item) for item in grads] if last else [slab],
        scratch_shapes=[pltpu.VMEM((tokens, columns), BF16)],
        name="attention_weights",
    )
    return list(grads) if last else grads[0]


def finish_kernel(fsdp, rows, scalar_ref, x_ref, gains_ref, branch_ref, slope_ref, local_ref, remote_ref, before_ref, *refs):
    piece_refs, (own_ref, pair_ref, small_ref, stack_s, one_s, branch_s, out_s, norm_s) = refs[:fsdp], refs[fsdp:]
    half, width = x_ref.shape
    span = width // fsdp
    step = pl.program_id(0)
    index = scalar_ref[0]
    gains = exchanged(lambda item: gains_ref[:, item], width, index, rows)

    @pl.when(step == 0)
    def _():
        norm_s[...] = jnp.zeros_like(norm_s)
        collect(scalar_ref[1], local_ref, remote_ref, stack_s)
        for offset in range(fsdp):
            lanes = slice(offset * span, (offset + 1) * span)
            one_s[:, lanes] = against(stack_s[:, : 6 * LANES], piece_refs[offset][:, : 6 * LANES])
            branch_s[:, lanes] = against(stack_s[:, 6 * LANES :], piece_refs[offset][:, 6 * LANES :])

    here = pl.ds(pl.multiple_of(step * half, half), half)
    one, two = one_s[here, :], slope_ref[...]
    normal, _ = normal_of(x_ref[...].astype(F32))
    norm_s[0:1, :] += jnp.sum(one * normal, axis=0, keepdims=True)
    norm_s[1:2, :] += jnp.sum(one, axis=0, keepdims=True)
    norm_s[2:3, :] += jnp.sum(two * normal, axis=0, keepdims=True)
    norm_s[3:4, :] += jnp.sum(two, axis=0, keepdims=True)
    plain = []
    for value in (branch_ref[...] + branch_s[here, :], one * gains[0:1] + two * gains[2:3]):
        out_s[...] = value
        plain.append(exchanged(lambda item: out_s[:, item], width, index, rows).astype(BF16))

    for side, ref in enumerate((own_ref, pair_ref)):

        @pl.when(step // 2 == side)
        def _():
            ref[0], ref[1] = plain

    @pl.when(step == 3)
    def _():
        small_ref[...] = before_ref[...]
        small_ref[0:4, :] += exchanged(lambda item: norm_s[0:4, item], width, index, rows)
        small_ref[pl.ds(5 + scalar_ref[2], 1), : 6 * LANES] += jnp.sum(
            stack_s[:, : 6 * LANES].astype(F32), axis=0, keepdims=True
        )


def finish(scalars, x, gains, branch, slope, first, local, remote, small, pieces, rows, waits=()):
    width = x.shape[1]
    fsdp = len(pieces)
    half = local.shape[0] // 4
    base = first // half
    once = pl.Buffered(1)
    fixed = lambda item: pl.BlockSpec(item.shape, lambda t, *_: (0, 0))
    row_spec = pl.BlockSpec((half, width), lambda t, *_: (base + t, 0))
    back_spec = pl.BlockSpec(local.shape, lambda t, *_: (0, 0), pipeline_mode=once)
    own_spec = pl.BlockSpec((2, half, width), lambda t, *_: (0, jnp.minimum(t, 1), 0))
    pair_spec = pl.BlockSpec((2, half, width), lambda t, *_: (0, jnp.maximum(t - 2, 0), 0))
    sums = jax.ShapeDtypeStruct((2, 2 * half, width), BF16)
    return launch(
        lambda *refs: finish_kernel(fsdp, rows, *refs),
        scalars,
        [x, gains, branch, slope, local, remote, small, *pieces],
        waits,
        half / 20 if first else 0.5,
        out_shape=[sums, sums, jax.ShapeDtypeStruct(small.shape, F32)],
        grid=(4,),
        in_specs=[row_spec, fixed(gains), row_spec, row_spec, back_spec, back_spec, fixed(small)]
        + [pl.BlockSpec(piece.shape, lambda t, *_: (0, 0), pipeline_mode=once) for piece in pieces],
        out_specs=[own_spec, pair_spec, fixed(small)],
        scratch_shapes=[
            pltpu.VMEM((4 * half, 8 * LANES), BF16),
            pltpu.VMEM((4 * half, width), F32),
            pltpu.VMEM((4 * half, width), F32),
            pltpu.VMEM((half, width), F32),
            pltpu.VMEM((8, width), F32),
        ],
        name="finish",
    )


def pair_kernel(own_ref, got_ref, out_ref):
    out_ref[...] = (own_ref[...].astype(F32) + got_ref[...].astype(F32)).astype(BF16)


def pair_sums(own, got, waits=(), us=2):
    fields, tokens, width = own.shape
    field = pl.BlockSpec((1, tokens, width), lambda n: (n, 0, 0))
    return launch(
        pair_kernel,
        None,
        [own, got],
        waits,
        us,
        out_shape=jax.ShapeDtypeStruct(own.shape, BF16),
        grid=(fields,),
        in_specs=[field, field],
        out_specs=field,
        name="pair_sums",
    )


def tree_sum(terms):
    while len(terms) > 1:
        terms = [first + second for first, second in zip(terms[::2], terms[1::2])]
    return terms[0]


def reduce_kernel(body, cuts, *refs):
    in_refs, out_refs = refs[: -len(cuts)], refs[-len(cuts) :]
    extra = in_refs[0].shape[1] - body
    for (start, count, _), out in zip(cuts, out_refs):
        rows = slice(start, start + count)
        out[0, :count, :] = tree_sum([ref[0, rows, :].astype(F32) for ref in in_refs]).astype(out.dtype)
    if extra:
        small = tree_sum([ref[0, body:, :].astype(F32) for ref in in_refs]).astype(BF16)
        for (_, count, _), out in zip(cuts, out_refs):
            out[0, count:, :] = small.astype(out.dtype)


def reduce_and_cut(terms, cuts, waits=(), extra=0, us=3):
    stacks, rows, columns = terms[0].shape
    tile = min(columns, 512)
    spec = lambda count: pl.BlockSpec((1, count, tile), lambda a, b: (a, 0, b))
    return launch(
        lambda *refs: reduce_kernel(rows - extra, cuts, *refs),
        None,
        terms,
        waits,
        us,
        out_shape=[jax.ShapeDtypeStruct((stacks, count + extra, columns), dtype) for _, count, dtype in cuts],
        grid=(stacks, columns // tile),
        in_specs=[spec(rows)] * len(terms),
        out_specs=[spec(count + extra) for _, count, _ in cuts],
        name="reduce_and_cut",
    )


def scatter(stack):
    return [stack[0]] + [swap(piece, "fsdp", j) for j, piece in enumerate(stack) if j > 0]


def close_kernel(x_ref, g_ref, own_ref, other_ref, shift_ref, *refs):
    out_ref, grad_ref = refs[-2:]
    values = x_ref[...].astype(F32)
    normal, spread = normal_of(values)
    total, slope = (own_ref[field].astype(F32) + other_ref[field].astype(F32) for field in range(2))
    out_ref[...] = (values + total + shift_ref[...]).astype(BF16)
    slope_mean = jnp.mean(slope, axis=-1, keepdims=True)
    slope_dot = jnp.mean(slope * normal, axis=-1, keepdims=True)
    grad_ref[...] = (g_ref[...].astype(F32) + spread * (slope - slope_mean - normal * slope_dot)).astype(BF16)


def close(x, g, own, other, shift, first, results, waits=()):
    tokens, width = x.shape
    count = own.shape[1]
    block = math.gcd(count, 128)
    base = first // block
    row_spec = pl.BlockSpec((block, width), lambda m: (base + m, 0))
    three_spec = pl.BlockSpec((2, block, width), lambda m: (0, m, 0))
    return launch(
        close_kernel,
        None,
        [x, g, own, other, shift, *results],
        waits,
        3,
        out_shape=[jax.ShapeDtypeStruct((tokens, width), BF16)] * 2,
        grid=(count // block,),
        in_specs=[row_spec, row_spec, three_spec, three_spec, pl.BlockSpec((1, width), lambda m: (0, 0))]
        + [pl.BlockSpec(memory_space=pl.ANY)] * len(results),
        out_specs=[row_spec] * 2,
        input_output_aliases={5 + i: i for i in range(len(results))},
        name="close",
    )


def ranks_of(order, offsets):
    sources = lax.axis_index("ctx") ^ jnp.array(offsets, dtype=jnp.int32)
    match = sources[:, None] == jnp.arange(order.shape[1], dtype=jnp.int32)[None, :]
    return jnp.sum(jnp.where(match, order[:, None, :], 0), axis=-1)


def exchange_attention(local, remote, order, table, block_rows, waits):
    shape = (2, order.shape[0], block_rows, 4 * LANES)
    ranks = ranks_of(order, range(4)).reshape(-1)
    outs = attend(ranks, table, [local.reshape(shape), remote.reshape(shape)], waits)
    mine, theirs = (out.reshape(local.shape) for out in outs)
    return mine, swap(theirs, "ctx", 2)


def gathered_attention(local, remote, order, table, block_rows, waits):
    groups, micro = 2, order.shape[0]
    ctx = lax.axis_size("ctx")
    heads = groups * LANES // HD
    scale = HD ** (-0.5)
    packed = jnp.stack([local, remote]).reshape(groups, 2, micro, block_rows, 4 * LANES)
    packed = jnp.transpose(packed, (0, 2, 1, 3, 4))
    ranks = ranks_of(order, range(ctx))

    def split(array):
        array = array.reshape(groups, 2 * block_rows, LANES // HD, HD)
        return jnp.transpose(array, (1, 0, 2, 3)).reshape(2 * block_rows, heads, HD)

    def join(array):
        return jnp.transpose(array.reshape(2, block_rows, groups, LANES), (2, 0, 1, 3))

    def everywhere(array):
        return jnp.stack([array] + [swap(array, "ctx", j) for j in range(2, ctx, 2)])

    def home(array):
        total = array[0].astype(F32)
        for j in range(2, ctx, 2):
            total = total + swap(array[j // 2], "ctx", j).astype(F32)
        return total

    results = []
    for m in range(micro):
        parted = packed[:, m].reshape(groups, 2 * block_rows, 4, LANES)
        queries, keys, values, douts = (split(parted[:, :, i]) for i in range(4))
        all_keys, all_values = everywhere(keys), everywhere(values)
        key_ranks = jnp.repeat(ranks[m].reshape(-1, 2), block_rows, axis=1)
        query_ranks = key_ranks[0]
        allowed = (key_ranks[:, None, :] <= query_ranks[None, :, None])[:, None]

        def peak_step(state, item):
            key, value, ok = item
            peak, total, sums = state
            scores = jnp.einsum("bhe,rhe->hbr", queries, key, preferred_element_type=F32) * scale
            scores = jnp.where(ok, scores, -1e30)
            new = jnp.maximum(peak, jnp.max(scores, axis=-1))
            weights = jnp.where(ok, jnp.exp(scores - new[..., None]), 0.0)
            fade = jnp.exp(peak - new)
            part = jnp.einsum("hbr,rhe->hbe", weights.astype(BF16), value, preferred_element_type=F32)
            return (new, total * fade + jnp.sum(weights, axis=-1), sums * fade[..., None] + part), None

        start = (
            jnp.full((heads, 2 * block_rows), -1e30, F32),
            jnp.zeros((heads, 2 * block_rows), F32),
            jnp.zeros((heads, 2 * block_rows, HD), F32),
        )
        (peak, total, sums), _ = lax.scan(peak_step, start, (all_keys, all_values, allowed))
        attended = jnp.transpose(sums / total[..., None], (1, 0, 2))
        level = peak + jnp.log(total)
        delta = jnp.transpose(jnp.sum(douts.astype(F32) * attended, axis=-1))

        def back_step(query_sum, item):
            key, value, ok = item
            scores = jnp.einsum("bhe,rhe->hbr", queries, key, preferred_element_type=F32) * scale
            weights = jnp.where(ok, jnp.exp(scores - level[..., None]), 0.0)
            value_grad = jnp.einsum("hbr,bhe->rhe", weights.astype(BF16), douts, preferred_element_type=F32)
            slope = jnp.einsum("bhe,rhe->hbr", douts, value, preferred_element_type=F32)
            slope = (weights * (slope - delta[..., None])).astype(BF16)
            query_part = jnp.einsum("hbr,rhe->bhe", slope, key, preferred_element_type=F32) * scale
            key_grad = jnp.einsum("hbr,bhe->rhe", slope, queries, preferred_element_type=F32) * scale
            return query_sum + query_part, (key_grad.astype(BF16), value_grad.astype(BF16))

        query_grad, (key_grads, value_grads) = lax.scan(
            back_step, jnp.zeros(queries.shape, F32), (all_keys, all_values, allowed)
        )
        rows = [
            lax.dynamic_slice(table, (0, ranks[m, side] * block_rows, 0), (2, block_rows, LANES)) for side in range(2)
        ]
        rows = jnp.concatenate(rows, axis=1)

        def unturn(array):
            half = ROT // 2
            cosine, sine = rows[0, :, :half][:, None], rows[1, :, half:ROT][:, None]
            first, second = array[..., :half], array[..., half:ROT]
            return jnp.concatenate(
                [first * cosine + second * sine, second * cosine - first * sine, array[..., ROT:]], axis=-1
            )

        fields = (unturn(query_grad), unturn(home(key_grads)), home(value_grads), attended)
        results.append(jnp.concatenate([join(field.astype(BF16)) for field in fields], axis=-1))
    results = jnp.transpose(jnp.stack(results, axis=1), (0, 2, 1, 3, 4))
    mine, theirs = results.reshape(groups, *local.shape)
    return mine, theirs


def rotation_table(length):
    lane = jnp.arange(LANES, dtype=jnp.int32) % HD
    halves = ROT // 2
    frequency = jnp.exp((lane % halves).astype(F32) * (-2.0 * math.log(10000.0) / ROT))
    frequency = jnp.where(lane < ROT, frequency, 0.0)
    angles = jnp.arange(length, dtype=F32)[:, None] * frequency
    return jnp.stack([jnp.cos(angles), jnp.where(lane < halves, -1.0, 1.0) * jnp.sin(angles)])


def local(
    inputs,
    block_order,
    first_gain,
    first_shift,
    second_gain,
    second_shift,
    qkv_weight,
    qkv_bias,
    out_weight,
    out_bias,
    up_weight,
    up_bias,
    down_weight,
    down_bias,
    out_grad,
):
    micro, block_rows, _, width = inputs.shape
    ctx = lax.axis_size("ctx")
    f, z, core = lax.axis_index("fsdp"), lax.axis_index("ctx"), lax.axis_index("tp")
    low = z & 1
    rows = up_weight.shape[0]
    groups, hidden = 2, up_weight.shape[1] // 2
    tokens = micro * block_rows
    order = block_order[:, 0]
    first_part = micro - 1
    parts = ((0, first_part), (first_part, micro))
    exchanging = ctx == 2 * groups

    fields = [qkv_weight[0], qkv_weight[1], qkv_weight[2], jnp.transpose(out_weight)]
    extent = groups * LANES
    halves = [jnp.concatenate([field[:, i * extent : (i + 1) * extent] for field in fields], axis=1) for i in range(2)]
    shard = jnp.stack(halves)

    x, g = inputs.reshape(tokens, width), out_grad.reshape(tokens, width)
    both, shard = lax.optimization_barrier((jnp.stack([x, g]), shard))
    column = jnp.concatenate(gather_column(*choose(low, shard[0], shard[1])), axis=0)
    lanes, _ = choose(core, both[:, :, : width // 2], both[:, :, width // 2 :])
    lanes, column = lax.optimization_barrier((lanes, column))
    lanes = swap(lanes, "ctx", 1)
    fields = [up_weight, jnp.transpose(down_weight)]
    halves = [jnp.concatenate([field[:, i * hidden : (i + 1) * hidden] for field in fields], axis=1) for i in range(2)]
    forward_shard, column = lax.optimization_barrier((jnp.stack(halves), column))
    pieces = gather_pieces(column)

    index = jnp.stack([f * ctx + z, core]).astype(jnp.int32)
    gains = jnp.stack([first_gain, first_shift, second_gain, second_shift]).astype(F32)
    prepared, grad_sum = prepare_own(index, x, g, gains, rows, block_rows, first_part, (column,))
    own, other = choose(low, forward_shard[0], forward_shard[1])
    forward_pair = jnp.concatenate([own, swap(other, "ctx", 1)], axis=0)
    lanes, grad_sum, *pieces = lax.optimization_barrier((lanes, grad_sum, *pieces))
    arrived = (lanes, swap(lanes, "tp", 1))
    x_both, g_both, one = prepare_pair(
        index, arrived, gains, prepared, rows, block_rows, first_part, (forward_pair,)
    )
    forward_column = [forward_pair] + [swap(forward_pair, "ctx", j) for j in range(2, ctx, 2)]

    table = rotation_table(ctx * block_rows)
    place = ((z >> 1) if exchanging else jnp.zeros_like(z)).astype(jnp.int32).reshape(1)
    bias = qkv_bias.astype(F32)
    bias = choose(low, bias[:, :extent], bias[:, extent:])[0].reshape(1, -1)
    attention = exchange_attention if exchanging else gathered_attention
    send = (lambda item: swap(item, "ctx", 2)) if exchanging else (lambda item: item)
    packed, first_block = [], 0
    for begin, end in parts:
        ranks = jnp.transpose(ranks_of(order[begin:end], (0, 1))).reshape(-1)
        count = 2 * (end - begin)
        waits = [forward_column] if packed else []
        mine, other = project(
            place, ranks, one, g_both, first_block, count, table, bias, pieces, block_rows, waits
        )
        if not packed:
            forward_column[0], mine = lax.optimization_barrier((forward_column[0], mine))
            forward_column = jnp.concatenate(forward_column, axis=0)
            forward_pieces = gather_pieces(forward_column)
        packed.append((first_block * block_rows, mine, other))
        first_block += count

    two, one_t, two_t, g_t = prepare_late(index, x_both, g_both, one, gains, rows, block_rows, (packed[1][1],))
    up_shift = up_bias.astype(F32).reshape(2, 1, hidden)
    up_shift = choose(low, up_shift[0], up_shift[1])[0]
    arrivals = [send(theirs) for _, _, theirs in packed]
    returned = [attention(packed[0][1], arrivals[0], order[: parts[0][1]], table, block_rows, (g_t,))]
    branch, slope, up_sum, forward_grads = feed_forward(
        two, g_both, two_t, g_t, up_shift, forward_pieces, (returned[0][0],)
    )
    returned.append(attention(packed[1][1], arrivals[1], order[parts[1][0] :], table, block_rows, (up_sum,)))
    wait = returned[1][0]

    scalars = jnp.stack([f * ctx + z, place[0], low]).astype(jnp.int32)
    end_shift = (out_bias.astype(F32) + down_bias.astype(F32)).reshape(1, width)
    forward_terms = scatter(forward_grads)
    pairs = range(2, ctx, 2)

    def finish_part(number, small, waits):
        first, (local, remote) = packed[number][0], returned[number]
        own, pair, small = finish(
            scalars, x_both, gains, branch, slope, first, local, remote, small, pieces, rows, waits
        )
        return own, swap(pair, "ctx", 1), small

    def weights_part(number, before, waits):
        first, (local, remote) = packed[number][0], returned[number]
        return attention_weights(place, one_t, g_t, first, local, remote, before, len(pieces), waits)

    zero = jnp.zeros((1, width), F32)
    small = jnp.concatenate([zero] * 4 + [grad_sum, zero, zero, *choose(low, up_sum, zero)] + [zero] * (SMALL_ROWS - 9))
    made = {}

    def run(task, wait):
        if task == "finish_a":
            made["own_a"], made["got_a"], made["small"] = finish_part(0, small, (wait,))
            return made["small"]
        if task == "weights_a":
            made["grads_a"] = weights_part(0, None, (wait,))
            return made["grads_a"]
        if task == "forward_first":
            keep, *send = reduce_and_cut(
                forward_terms, [(0, 2 * rows, F32)] + [(j * rows, 2 * rows, BF16) for j in pairs], (wait,)
            )
            made["forward"] = [keep] + [swap(item, "ctx", j) for j, item in zip(pairs, send)]
            return keep
        if task == "finish_b":
            made["own_b"], made["got_b"], made["small"] = finish_part(1, made["small"], (wait,))
            return made["small"]
        if task == "weights_b":
            grads = weights_part(1, (made["grads_a"], made["small"]), (wait,))
            made["attention"] = scatter(grads)
            return grads[0]
        if task == "forward_second":
            made["mine"], made["send"] = reduce_and_cut(
                made["forward"], [(0, rows, F32), (rows, rows, BF16)], (wait,)
            )
            return made["mine"]
        if task == "attention_first":
            made["keep"], *send = reduce_and_cut(
                made["attention"],
                [(0, rows, F32)] + [(j * rows, rows, BF16) for j in range(1, ctx)],
                (wait,),
                SMALL_ROWS,
            )
            made["sent"] = [swap(item, "ctx", j) for j, item in enumerate(send, 1)]
            return made["keep"]
        if task in ("sums_a", "sums_b"):
            sums = pair_sums(made["own" + task[4:]], made["got" + task[4:]], (wait,))
            made[task] = (sums, swap(sums, "tp", 1))
            return sums
        number = 0 if task == "close_a" else 1
        made["results"] = close(
            x, g, *made["sums" + task[5:]], end_shift, packed[number][0] // 2, made.get("results", ()), (wait,)
        )
        return made["results"][0]

    wait = returned[1][0]
    for task in TASKS:
        if task == "sums_b":
            wait, made["got"] = lax.optimization_barrier((wait, swap(made["send"], "ctx", 1)))
        wait = run(task, wait)
    forward_mine, forward_send, attention_keep, results = (made[key] for key in ("mine", "send", "keep", "results"))
    *attention_got, done = lax.optimization_barrier((*made["sent"], results[0]))
    results = [done, results[1]]
    outputs, input_grad = (item.reshape(inputs.shape) for item in results)
    forward_sums = choose(low, forward_mine, made["got"].astype(F32))
    up_sums = jnp.concatenate([half[0] for half in forward_sums], axis=1)
    down_sums = jnp.concatenate([jnp.transpose(half[1]) for half in forward_sums], axis=0)

    terms = [attention_keep[0]] + [got[0].astype(F32) for got in attention_got]
    halves = choose(low, tree_sum([term[:rows] for term in terms[::2]]), tree_sum([term[:rows] for term in terms[1::2]]))
    small = tree_sum([term[rows:] for term in terms])
    fields = [
        jnp.concatenate([half[:, i * extent : (i + 1) * extent] for half in halves], axis=1) for i in range(4)
    ]
    norm_sums = small[:4] + swap(small[:4], "tp", 1)
    pre_sums = small[5:7, : 3 * extent].reshape(2, 3, extent)
    return (
        outputs,
        input_grad,
        norm_sums[0],
        norm_sums[1],
        norm_sums[2],
        norm_sums[3],
        jnp.stack(fields[:3]),
        jnp.concatenate([pre_sums[0], pre_sums[1]], axis=1),
        jnp.transpose(fields[3]),
        small[4],
        up_sums,
        small[7:9].reshape(-1),
        down_sums,
        small[4],
    )


def solution(mesh):
    placed = (
        P(None, "ctx", "fsdp", None),
        P(None, "fsdp", None),
        P(),
        P(),
        P(),
        P(),
        P(None, ("fsdp", "ctx"), "tp"),
        P(None, "tp"),
        P("tp", ("fsdp", "ctx")),
        P(),
        P(("fsdp", "ctx"), "tp"),
        P("tp"),
        P("tp", ("fsdp", "ctx")),
        P(),
        P(None, "ctx", "fsdp", None),
    )
    return jax.shard_map(
        local,
        mesh=mesh,
        in_specs=placed,
        out_specs=(
            P(None, "ctx", "fsdp", None),
            P(None, "ctx", "fsdp", None),
            P(),
            P(),
            P(),
            P(),
            P(None, ("fsdp", "ctx"), "tp"),
            P(None, "tp"),
            P("tp", ("fsdp", "ctx")),
            P(),
            P(("fsdp", "ctx"), "tp"),
            P("tp"),
            P("tp", ("fsdp", "ctx")),
            P(),
        ),
        check_vma=False,
    )
```

```python
import math

import jax
import jax.numpy as jnp
from jax import lax
from jax.experimental import pallas as pl
from jax.experimental.pallas import tpu as pltpu
from jax.sharding import PartitionSpec as P

HD = 64
ROT = 16
LANES = 128
F32 = jnp.float32
BF16 = jnp.bfloat16
MIB = 1024 * 1024
EPSILON = 1e-05
TASKS = (
    "finish_a",
    "weights_a",
    "forward_first",
    "finish_b",
    "weights_b",
    "sums",
    "forward_second",
    "attention_first",
    "totals",
    "close",
)
SMALL_ROWS = 16
SHARE = 1 / 0.6


def swap(value, axis, bit):
    size = lax.axis_size(axis)
    return lax.ppermute(value, axis, [(i, i ^ bit) for i in range(size)])


def choose(bit, first, second):
    return jnp.where(bit == 0, first, second), jnp.where(bit == 0, second, first)


def gather_column(own, other):
    return [own] + [swap(other if j & 1 else own, "ctx", j) for j in range(1, lax.axis_size("ctx"))]


def gather_pieces(column):
    return [column] + [swap(column, "fsdp", j) for j in range(1, lax.axis_size("fsdp"))]


def launch(kernel, scalars, operands, waits, us, *, grid, in_specs, out_specs, out_shape, scratch_shapes=(), mib=24, **more):
    count = (scalars is not None) + len(operands)

    def body(*refs):
        kernel(*refs[:count], *refs[count + len(waits) :])

    return pl.pallas_call(
        body,
        out_shape=out_shape,
        grid_spec=pltpu.PrefetchScalarGridSpec(
            num_scalar_prefetch=0 if scalars is None else 1,
            grid=grid,
            in_specs=[*in_specs] + [pl.BlockSpec(memory_space=pl.ANY)] * len(waits),
            out_specs=out_specs,
            scratch_shapes=scratch_shapes,
        ),
        compiler_params=pltpu.CompilerParams(vmem_limit_bytes=mib * MIB),
        cost_estimate=pl.CostEstimate(flops=int(us * SHARE * 1.1e9), bytes_accessed=1024, transcendentals=0),
        **more,
    )(*([] if scalars is None else [scalars]), *operands, *waits)


def matmul(lhs, rhs):
    return jnp.dot(lhs, rhs, preferred_element_type=F32)


def against(lhs, rhs):
    return lax.dot_general(lhs, rhs, (((1,), (1,)), ((), ())), preferred_element_type=F32)


def exchanged(load, width, index, rows):
    shift = index * rows
    high, low = shift // LANES, lax.rem(shift, LANES)
    blocks = []
    for block in range(width // LANES):
        start = pl.multiple_of((block ^ high) * LANES, LANES)
        value = load(pl.ds(start, LANES)).astype(F32)
        step = rows
        while step < LANES:
            lane = lax.broadcasted_iota(jnp.int32, value.shape, 1)
            turned = pltpu.roll(value, step, 1)
            if 2 * step != LANES:
                turned = jnp.where((lane & step) != 0, turned, pltpu.roll(value, LANES - step, 1))
            value = jnp.where((low & step) != 0, turned, value)
            step *= 2
        blocks.append(value)
    return jnp.concatenate(blocks, axis=1)


def normal_of(values):
    centre = jnp.mean(values, axis=-1, keepdims=True)
    offset = values - centre
    spread = lax.rsqrt(jnp.mean(offset * offset, axis=-1, keepdims=True) + EPSILON)
    return offset * spread, spread


def prepare_block(rows, index, load_x, load_g, gains_ref, outs):
    x_out, g_out, one_out = outs
    width = x_out.shape[1]
    values = exchanged(load_x, width, index, rows)
    gains = exchanged(lambda lanes: gains_ref[:, lanes], width, index, rows)
    normal, _ = normal_of(values)
    x_out[...] = values.astype(BF16)
    g_out[...] = exchanged(load_g, width, index, rows).astype(BF16)
    one_out[...] = (normal * gains[0:1] + gains[1:2]).astype(BF16)


def prepare_own_kernel(rows, index_ref, x_ref, g_ref, gains_ref, *refs):
    outs, sum_out = refs[:3], refs[3]
    prepare_block(rows, index_ref[0], lambda lanes: x_ref[:, lanes], lambda lanes: g_ref[:, lanes], gains_ref, outs)

    @pl.when(pl.program_id(0) == 0)
    def _():
        sum_out[...] = jnp.zeros_like(sum_out)

    sum_out[...] += jnp.sum(g_ref[...].astype(F32), axis=0, keepdims=True)


def prepare_pair_kernel(rows, count, index_ref, mine_ref, other_ref, gains_ref, *refs):
    half = mine_ref.shape[2]

    def loader(field):
        def load(lanes):
            inside = pl.ds(pl.multiple_of(lax.rem(lanes.start, half), LANES), lanes.size)
            mine, other = mine_ref[field, :, inside].astype(F32), other_ref[field, :, inside].astype(F32)
            return jnp.where(lanes.start // half == index_ref[1], mine, other)

        return load

    own_refs, out_refs = refs[:3], refs[3:]
    step = pl.program_id(0)

    @pl.when(step < count)
    def _():
        for own, out in zip(own_refs, out_refs):
            out[...] = own[...]

    @pl.when(step >= count)
    def _():
        prepare_block(rows, index_ref[0], loader(0), loader(1), gains_ref, out_refs)


def prepare_late_kernel(rows, index_ref, x_ref, g_ref, one_ref, gains_ref, two_out, one_t, two_t, g_t):
    normal, _ = normal_of(x_ref[...].astype(F32))
    gains = exchanged(lambda lanes: gains_ref[:, lanes], x_ref.shape[1], index_ref[0], rows)
    two = (normal * gains[2:3] + gains[3:4]).astype(BF16)
    two_out[...] = two
    one_t[...] = one_ref[...].T
    two_t[...] = two.T
    g_t[...] = g_ref[...].T


def prepare_own(index, x, g, gains, rows, block_rows, waits=()):
    tokens, width = x.shape
    row_spec = pl.BlockSpec((block_rows, width), lambda m, *_: (m, 0))
    *outs, grad_sum = launch(
        lambda *refs: prepare_own_kernel(rows, *refs),
        index,
        [x, g, gains],
        waits,
        2.100,
        out_shape=[jax.ShapeDtypeStruct((tokens, width), BF16)] * 3 + [jax.ShapeDtypeStruct((1, width), F32)],
        grid=(tokens // block_rows,),
        in_specs=[row_spec, row_spec, pl.BlockSpec(gains.shape, lambda m, *_: (0, 0))],
        out_specs=[row_spec] * 3 + [pl.BlockSpec((1, width), lambda m, *_: (0, 0))],
        name="prepare_own",
    )
    return outs, grad_sum


def prepare_pair(index, arrived, gains, own, rows, block_rows, first_part, waits=()):
    _, tokens, half = arrived[0].shape
    width = 2 * half
    count = tokens // block_rows

    def place(step):
        m, side = lax.rem(step, count), step // count
        return m + jnp.where(m < first_part, side * first_part, first_part + side * (count - first_part))

    half_spec = pl.BlockSpec((2, block_rows, half), lambda m, *_: (0, jnp.maximum(m - count, 0), 0))
    own_spec = pl.BlockSpec((block_rows, width), lambda m, *_: (jnp.minimum(m, count - 1), 0))
    return launch(
        lambda *refs: prepare_pair_kernel(rows, count, *refs),
        index,
        [*arrived, gains, *own],
        waits,
        2.100,
        out_shape=[jax.ShapeDtypeStruct((2 * tokens, width), BF16)] * 3,
        grid=(2 * count,),
        in_specs=[half_spec, half_spec, pl.BlockSpec(gains.shape, lambda m, *_: (0, 0))] + [own_spec] * 3,
        out_specs=[pl.BlockSpec((block_rows, width), lambda m, *_: (place(m), 0))] * 3,
        name="prepare_pair",
    )


def prepare_late(index, x, g, one, gains, rows, block_rows, waits=()):
    tokens, width = x.shape
    row_spec = pl.BlockSpec((block_rows, width), lambda m, *_: (m, 0))
    column_spec = pl.BlockSpec((width, block_rows), lambda m, *_: (0, m))
    plain, turned = jax.ShapeDtypeStruct((tokens, width), BF16), jax.ShapeDtypeStruct((width, tokens), BF16)
    return launch(
        lambda *refs: prepare_late_kernel(rows, *refs),
        index,
        [x, g, one, gains],
        waits,
        3.600,
        out_shape=[plain, turned, turned, turned],
        grid=(tokens // block_rows,),
        in_specs=[row_spec, row_spec, row_spec, pl.BlockSpec(gains.shape, lambda m, *_: (0, 0))],
        out_specs=[row_spec, column_spec, column_spec, column_spec],
        name="prepare_late",
        mib=24,
    )


def turn(values, cosine, sine):
    lane = lax.broadcasted_iota(jnp.int32, values.shape, 1) % HD
    ahead = pltpu.roll(values, LANES - ROT // 2, 1)
    behind = pltpu.roll(values, ROT // 2, 1)
    return values * cosine + jnp.where(lane < ROT // 2, ahead, behind) * sine


def gather_weight(piece_refs, weight_s):
    @pl.when(pl.program_id(0) == 0)
    def _():
        start = 0
        for ref in piece_refs:
            weight_s[start : start + ref.shape[0], :] = ref[...]
            start += ref.shape[0]


def pick(place, first, second):
    return jnp.where(place == 0, first, second), jnp.where(place == 0, second, first)


def project_kernel(fsdp, block_rows, scalar_ref, one_ref, g_ref, table_ref, bias_ref, *refs):
    piece_refs, (local_ref, remote_ref, weight_s) = refs[:fsdp], refs[fsdp:]
    tokens, width = one_ref.shape
    gather_weight(piece_refs, weight_s)
    pre = matmul(one_ref[...], weight_s[:, : 6 * LANES]) + bias_ref[...]
    back = matmul(g_ref[...], weight_s[:, 6 * LANES :])
    for block in range(tokens // block_rows):
        rows = slice(block * block_rows, (block + 1) * block_rows)
        rank = scalar_ref[1 + pl.program_id(0) * (tokens // block_rows) + block]
        places = pl.ds(pl.multiple_of(rank * block_rows, block_rows), block_rows)
        cosine, sine = table_ref[0, places, :], table_ref[1, places, :]
        for field in range(4):
            source = pre[rows] if field < 3 else back[rows]
            start = 2 * field * LANES if field < 3 else 0
            both = [source[:, start + group * LANES : start + (group + 1) * LANES] for group in range(2)]
            if field < 2:
                both = [turn(item, cosine, sine) for item in both]
            here = slice(field * LANES, (field + 1) * LANES)
            mine, other = pick(scalar_ref[0], *both)
            local_ref[rows, here] = mine.astype(BF16)
            remote_ref[rows, here] = other.astype(BF16)


def project(place, ranks, one, g, first, count, table, bias, pieces, block_rows, waits=()):
    width = one.shape[1]
    fsdp = len(pieces)
    tokens = count * block_rows
    tile = 2 * block_rows
    base = first // 2
    side = pl.BlockSpec((tile, width), lambda t, *_: (base + t, 0))
    once = pl.Buffered(1)
    out = pl.BlockSpec((tile, 4 * LANES), lambda t, *_: (t, 0))
    return launch(
        lambda *refs: project_kernel(fsdp, block_rows, *refs),
        jnp.concatenate([place, ranks]),
        [one, g, table, bias, *pieces],
        waits,
        tokens / 500.000,
        out_shape=[jax.ShapeDtypeStruct((tokens, 4 * LANES), BF16)] * 2,
        grid=(tokens // tile,),
        in_specs=[
            side,
            side,
            pl.BlockSpec(table.shape, lambda t, *_: (0, 0, 0), pipeline_mode=once),
            pl.BlockSpec(bias.shape, lambda t, *_: (0, 0)),
        ]
        + [pl.BlockSpec(piece.shape, lambda t, *_: (0, 0), pipeline_mode=once) for piece in pieces],
        out_specs=[out, out],
        scratch_shapes=[pltpu.VMEM((width, 8 * LANES), BF16)],
        name="project",
        mib=28,
    )


def attend_kernel(blocks, block_rows, scale, rank_ref, table_ref, *refs):
    count = blocks // 2
    chunk_refs, out_refs = refs[:count], refs[count : 2 * count]
    q_s, k_s, v_s, d_s, kt_s, vt_s, ot_s, qt_s, dk_s, dv_s = refs[2 * count :]
    item = pl.program_id(0)

    def rows_of(index):
        return pl.ds(pl.multiple_of(rank_ref[item * blocks + index] * block_rows, block_rows), block_rows)

    for index in range(blocks):
        rows, chunk, side = rows_of(index), chunk_refs[index // 2], index % 2
        q_s[rows, :] = chunk[side, 0, :, :LANES]
        k_s[rows, :] = chunk[side, 0, :, LANES : 2 * LANES]
        v_s[rows, :] = chunk[side, 0, :, 2 * LANES : 3 * LANES]
        d_s[rows, :] = chunk[side, 0, :, 3 * LANES :]
    kt_s[...] = k_s[...].T
    vt_s[...] = v_s[...].T
    lane = lax.broadcasted_iota(jnp.int32, (block_rows, LANES), 1)
    for rank in reversed(range(blocks)):
        rows = slice(rank * block_rows, (rank + 1) * block_rows)
        keys = slice(0, (rank + 1) * block_rows)
        dk, dv = None, None
        for head in range(LANES // HD):
            inside = (lane // HD) == head
            heads = slice(head * HD, (head + 1) * HD)
            q_h = jnp.where(inside, q_s[rows, :], 0).astype(BF16)
            d_h = jnp.where(inside, d_s[rows, :], 0).astype(BF16)
            scores = against(k_s[keys, :], q_h) * scale
            weights = jnp.exp(scores - jnp.max(scores, axis=0, keepdims=True))
            weights = weights * (1.0 / jnp.sum(weights, axis=0, keepdims=True))
            low = weights.astype(BF16)
            ot_s[heads, rows] = matmul(vt_s[heads, keys], low)
            dv_part = matmul(low, d_h)
            slope = against(v_s[keys, :], d_h)
            delta = jnp.sum(weights * slope, axis=0, keepdims=True)
            slope = (weights * (slope - delta)).astype(BF16)
            qt_s[heads, rows] = matmul(kt_s[heads, keys], slope)
            dk_part = matmul(slope, q_h)
            dk, dv = (dk_part, dv_part) if dk is None else (dk + dk_part, dv + dv_part)
        if rank == blocks - 1:
            dk_s[...], dv_s[...] = dk, dv
        else:
            dk_s[keys, :] += dk
            dv_s[keys, :] += dv
    for index in range(blocks):
        rows, out, side = rows_of(index), out_refs[index // 2], index % 2
        cosine, sine = table_ref[0, rows, :], -table_ref[1, rows, :]
        out[side, 0, :, :LANES] = turn(qt_s[:, rows].T * scale, cosine, sine).astype(BF16)
        out[side, 0, :, LANES : 2 * LANES] = turn(dk_s[rows, :] * scale, cosine, sine).astype(BF16)
        out[side, 0, :, 2 * LANES : 3 * LANES] = dv_s[rows, :].astype(BF16)
        out[side, 0, :, 3 * LANES :] = ot_s[:, rows].T.astype(BF16)


def attend(ranks, table, chunks, waits=()):
    sides, count, block_rows, _ = chunks[0].shape
    blocks = sides * len(chunks)
    length = blocks * block_rows
    spec = pl.BlockSpec((sides, 1, block_rows, 4 * LANES), lambda m, *_: (0, m, 0, 0))
    pairs = count * blocks * (blocks + 1) // 2 * block_rows * block_rows
    return launch(
        lambda *refs: attend_kernel(blocks, block_rows, HD ** (-0.5), *refs),
        ranks,
        [table, *chunks],
        waits,
        11 * count,
        out_shape=[jax.ShapeDtypeStruct(chunk.shape, BF16) for chunk in chunks],
        grid=(count,),
        in_specs=[pl.BlockSpec(table.shape, lambda m, *_: (0, 0, 0))] + [spec] * len(chunks),
        out_specs=[spec] * len(chunks),
        scratch_shapes=[pltpu.VMEM((length, LANES), BF16)] * 4
        + [pltpu.VMEM((LANES, length), BF16)] * 2
        + [pltpu.VMEM((LANES, length), F32)] * 2
        + [pltpu.VMEM((length, LANES), F32)] * 2,
        name="attend",
        mib=24,
    )


def forward_kernel(fsdp, two_ref, g_ref, two_t, g_t, bias_ref, *refs):
    up_refs, down_refs = refs[:fsdp], refs[fsdp : 2 * fsdp]
    branch_ref, slope_ref, sum_ref = refs[2 * fsdp : 2 * fsdp + 3]
    out_refs, (up_s, down_s) = refs[2 * fsdp + 3 : -2], refs[-2:]
    width = two_ref.shape[1]
    span = width // fsdp
    lanes = [slice(offset * span, (offset + 1) * span) for offset in range(fsdp)]
    for offset in range(fsdp):
        up_s[lanes[offset], :] = up_refs[offset][...]
        down_s[lanes[offset], :] = down_refs[offset][...]
    pre = matmul(two_ref[...], up_s[...]) + bias_ref[...]
    back = matmul(g_ref[...], down_s[...])
    gate = 0.5 * (1.0 + lax.erf(pre * math.sqrt(0.5)))
    bell = jnp.exp(-0.5 * pre * pre) * (1.0 / math.sqrt(2.0 * math.pi))
    hidden = (pre * gate).astype(BF16)
    pre_grad = (back * (gate + pre * bell)).astype(BF16)
    sum_ref[...] = jnp.sum(pre_grad.astype(F32), axis=0, keepdims=True)

    @pl.when(pl.program_id(0) == 0)
    def _():
        branch_ref[...] = against(hidden, down_s[...])
        slope_ref[...] = against(pre_grad, up_s[...])

    @pl.when(pl.program_id(0) != 0)
    def _():
        branch_ref[...] += against(hidden, down_s[...])
        slope_ref[...] += against(pre_grad, up_s[...])

    for offset in range(fsdp):
        out = out_refs[offset]
        out[0] = matmul(two_t[lanes[offset], :], pre_grad).astype(out.dtype)
        out[1] = matmul(g_t[lanes[offset], :], hidden).astype(out.dtype)


def feed_forward(two, g, two_t, g_t, bias, pieces, waits=()):
    tokens, width = two.shape
    fsdp = len(pieces)
    span, hidden = pieces[0].shape[0], pieces[0].shape[1] // 2
    tile = 256
    tiles = hidden // tile
    once = pl.Buffered(1)
    whole = pl.BlockSpec((tokens, width), lambda n: (0, 0), pipeline_mode=once)
    whole_t = pl.BlockSpec((width, tokens), lambda n: (0, 0), pipeline_mode=once)
    piece = pl.BlockSpec((span, tile), lambda n: (0, n))
    later = pl.BlockSpec((span, tile), lambda n: (0, n + tiles))
    line = pl.BlockSpec((1, tile), lambda n: (0, n))
    grads = [jax.ShapeDtypeStruct((2, span, hidden), BF16 if offset else F32) for offset in range(fsdp)]
    grad = pl.BlockSpec((2, span, tile), lambda n: (0, 0, n))
    branch, slope, sums, *grads = launch(
        lambda *refs: forward_kernel(fsdp, *refs),
        None,
        [two, g, two_t, g_t, bias, *pieces, *pieces],
        waits,
        34,
        out_shape=[jax.ShapeDtypeStruct((tokens, width), F32)] * 2
        + [jax.ShapeDtypeStruct((1, hidden), F32)]
        + grads,
        grid=(tiles,),
        in_specs=[whole, whole, whole_t, whole_t, line] + [piece] * fsdp + [later] * fsdp,
        out_specs=[whole, whole, line] + [grad] * fsdp,
        scratch_shapes=[pltpu.VMEM((width, tile), BF16)] * 2,
        name="feed_forward",
        mib=60,
    )
    return branch, slope, sums, grads


def collect(place, local_ref, remote_ref, stack_s):
    for ref, group in ((local_ref, place), (remote_ref, 1 - place)):
        for field in range(4):
            here = pl.ds(pl.multiple_of((2 * field + group) * LANES, LANES), LANES)
            stack_s[:, here] = ref[:, field * LANES : (field + 1) * LANES]


def weights_kernel(fsdp, last, place_ref, one_t, g_t, local_ref, remote_ref, *refs):
    before_ref, small_ref = refs[:2] if last else (None, None)
    out_refs, stack_s = refs[2 if last else 0 : -1], refs[-1]
    step = pl.program_id(0)
    span = one_t.shape[0]

    @pl.when(step == 0)
    def _():
        collect(place_ref[0], local_ref, remote_ref, stack_s)

    pre_part = matmul(one_t[...], stack_s[:, : 6 * LANES])
    out_part = matmul(g_t[...], stack_s[:, 6 * LANES :])
    if not last:
        out_refs[0][0, :, : 6 * LANES] = pre_part
        out_refs[0][0, :, 6 * LANES :] = out_part
    else:
        pre_part = pre_part + before_ref[0, :, : 6 * LANES]
        out_part = out_part + before_ref[0, :, 6 * LANES :]
        small = small_ref[...].astype(BF16)
        for offset in range(fsdp):

            @pl.when(step == offset)
            def _():
                out = out_refs[offset]
                out[0, :span, : 6 * LANES] = pre_part.astype(out.dtype)
                out[0, :span, 6 * LANES :] = out_part.astype(out.dtype)
                out[0, span:, :] = small.astype(out.dtype)


def attention_weights(place, one_t, g_t, first, local, remote, before, fsdp, waits=()):
    width = one_t.shape[0]
    tokens = local.shape[0]
    span = width // fsdp
    columns = 8 * LANES
    last = before is not None
    stack = jax.ShapeDtypeStruct((fsdp, span, columns), F32)
    grads = [
        jax.ShapeDtypeStruct((1, span + SMALL_ROWS, columns), BF16 if offset else F32) for offset in range(fsdp)
    ]
    piece = pl.BlockSpec((span, tokens), lambda o, *_: (o, first // tokens))
    slab = pl.BlockSpec((1, span, columns), lambda o, *_: (o, 0, 0))
    whole = lambda item: pl.BlockSpec(item.shape, lambda o, *_: (0,) * len(item.shape))
    grads = launch(
        lambda *refs: weights_kernel(fsdp, last, *refs),
        place,
        [one_t, g_t, local, remote, *(before if last else [])],
        waits,
        7 if last else 0.5,
        out_shape=grads if last else [stack],
        grid=(fsdp,),
        in_specs=[piece, piece, whole(local), whole(remote)] + ([slab, whole(before[1])] if last else []),
        out_specs=[whole(item) for item in grads] if last else [slab],
        scratch_shapes=[pltpu.VMEM((tokens, columns), BF16)],
        name="attention_weights",
    )
    return list(grads) if last else grads[0]


def finish_kernel(fsdp, rows, scalar_ref, x_ref, gains_ref, branch_ref, slope_ref, local_ref, remote_ref, before_ref, *refs):
    piece_refs, (mine_ref, theirs_ref, small_ref, stack_s, one_s, branch_s, out_s, norm_s) = refs[:fsdp], refs[fsdp:]
    half, width = x_ref.shape
    span = width // fsdp
    step = pl.program_id(0)
    index = scalar_ref[0]
    gains = exchanged(lambda item: gains_ref[:, item], width, index, rows)

    @pl.when(step == 0)
    def _():
        norm_s[...] = jnp.zeros_like(norm_s)
        collect(scalar_ref[1], local_ref, remote_ref, stack_s)
        for offset in range(fsdp):
            lanes = slice(offset * span, (offset + 1) * span)
            one_s[:, lanes] = against(stack_s[:, : 6 * LANES], piece_refs[offset][:, : 6 * LANES])
            branch_s[:, lanes] = against(stack_s[:, 6 * LANES :], piece_refs[offset][:, 6 * LANES :])

    here = pl.ds(pl.multiple_of((2 * lax.rem(step, 2) + ((step // 2) ^ scalar_ref[3])) * half, half), half)
    one, two = one_s[here, :], slope_ref[...]
    normal, _ = normal_of(x_ref[...].astype(F32))
    norm_s[0:1, :] += jnp.sum(one * normal, axis=0, keepdims=True)
    norm_s[1:2, :] += jnp.sum(one, axis=0, keepdims=True)
    norm_s[2:3, :] += jnp.sum(two * normal, axis=0, keepdims=True)
    norm_s[3:4, :] += jnp.sum(two, axis=0, keepdims=True)
    plain = []
    for value in (branch_ref[...] + branch_s[here, :], one * gains[0:1] + two * gains[2:3]):
        out_s[...] = value
        plain.append(exchanged(lambda item: out_s[:, item], width, index, rows).astype(BF16))

    for which, ref in enumerate((mine_ref, theirs_ref)):

        @pl.when(step // 2 == which)
        def _():
            ref[0, 0], ref[0, 1] = plain

    @pl.when(step == 3)
    def _():
        small_ref[...] = before_ref[...]
        small_ref[0:4, :] += exchanged(lambda item: norm_s[0:4, item], width, index, rows)
        small_ref[pl.ds(5 + scalar_ref[2], 1), : 6 * LANES] += jnp.sum(
            stack_s[:, : 6 * LANES].astype(F32), axis=0, keepdims=True
        )


def finish(scalars, x, gains, branch, slope, first, local, remote, small, pieces, rows, waits=()):
    width = x.shape[1]
    fsdp = len(pieces)
    half = local.shape[0] // 4
    base = first // half
    once = pl.Buffered(1)
    fixed = lambda item: pl.BlockSpec(item.shape, lambda t, *_: (0, 0))
    place = lambda t, scalars: 2 * lax.rem(t, 2) + ((t // 2) ^ scalars[3])
    row_spec = pl.BlockSpec((half, width), lambda t, scalars: (base + place(t, scalars), 0))
    back_spec = pl.BlockSpec(local.shape, lambda t, *_: (0, 0), pipeline_mode=once)
    mine_spec = pl.BlockSpec((1, 2, half, width), lambda t, *_: (jnp.minimum(t, 1), 0, 0, 0))
    theirs_spec = pl.BlockSpec((1, 2, half, width), lambda t, *_: (jnp.maximum(t - 2, 0), 0, 0, 0))
    sums = jax.ShapeDtypeStruct((2, 2, half, width), BF16)
    return launch(
        lambda *refs: finish_kernel(fsdp, rows, *refs),
        scalars,
        [x, gains, branch, slope, local, remote, small, *pieces],
        waits,
        half / 20 if first else 0.5,
        out_shape=[sums, sums, jax.ShapeDtypeStruct(small.shape, F32)],
        grid=(4,),
        in_specs=[row_spec, fixed(gains), row_spec, row_spec, back_spec, back_spec, fixed(small)]
        + [pl.BlockSpec(piece.shape, lambda t, *_: (0, 0), pipeline_mode=once) for piece in pieces],
        out_specs=[mine_spec, theirs_spec, fixed(small)],
        scratch_shapes=[
            pltpu.VMEM((4 * half, 8 * LANES), BF16),
            pltpu.VMEM((4 * half, width), F32),
            pltpu.VMEM((4 * half, width), F32),
            pltpu.VMEM((half, width), F32),
            pltpu.VMEM((8, width), F32),
        ],
        name="finish",
        mib=40,
    )


def sums_kernel(parts, *refs):
    terms, out = refs[:-1], refs[-1]
    start = 0
    for number in range(parts):
        mine, other = terms[2 * number : 2 * number + 2]
        rows = slice(start, start + mine.shape[2])
        total = mine[0, 0].astype(F32) + other[0, 0].astype(F32)
        if len(terms) > 2 * parts:
            total = total + terms[-1][0, rows, :].astype(F32)
        out[0, rows, :] = total.astype(BF16)
        start += mine.shape[2]


def core_sums(side, terms, more=(), waits=(), us=2):
    fields, width = terms[0].shape[1], terms[0].shape[3]
    rows = sum(item.shape[2] for item in terms[::2])
    field = pl.BlockSpec((1, rows, width), lambda n: (n, 0, 0))
    return launch(
        lambda *refs: sums_kernel(len(terms) // 2, *refs),
        None,
        [*terms, *more],
        waits,
        us,
        out_shape=jax.ShapeDtypeStruct((fields, rows, width), BF16),
        grid=(fields,),
        in_specs=[pl.BlockSpec((1, 1, item.shape[2], width), lambda n: (side, n, 0, 0)) for item in terms]
        + [field] * len(more),
        out_specs=field,
        name="core_sums",
    )


def tree_sum(terms):
    while len(terms) > 1:
        terms = [first + second for first, second in zip(terms[::2], terms[1::2])]
    return terms[0]


def reduce_kernel(body, cuts, *refs):
    in_refs, out_refs = refs[: -len(cuts)], refs[-len(cuts) :]
    extra = in_refs[0].shape[1] - body
    for (start, count, _), out in zip(cuts, out_refs):
        rows = slice(start, start + count)
        out[0, :count, :] = tree_sum([ref[0, rows, :].astype(F32) for ref in in_refs]).astype(out.dtype)
    if extra:
        small = tree_sum([ref[0, body:, :].astype(F32) for ref in in_refs]).astype(BF16)
        for (_, count, _), out in zip(cuts, out_refs):
            out[0, count:, :] = small.astype(out.dtype)


def reduce_and_cut(terms, cuts, waits=(), extra=0, us=3):
    stacks, rows, columns = terms[0].shape
    tile = min(columns, 512)
    spec = lambda count: pl.BlockSpec((1, count, tile), lambda a, b: (a, 0, b))
    return launch(
        lambda *refs: reduce_kernel(rows - extra, cuts, *refs),
        None,
        terms,
        waits,
        us,
        out_shape=[jax.ShapeDtypeStruct((stacks, count + extra, columns), dtype) for _, count, dtype in cuts],
        grid=(stacks, columns // tile),
        in_specs=[spec(rows)] * len(terms),
        out_specs=[spec(count + extra) for _, count, _ in cuts],
        name="reduce_and_cut",
    )


def scatter(stack):
    return [stack[0]] + [swap(piece, "fsdp", j) for j, piece in enumerate(stack) if j > 0]


def close_kernel(source, core_ref, x_ref, g_ref, mine_ref, other_ref, shift_ref, out_ref, grad_ref):
    core, _ = source(pl.program_id(0))
    values = x_ref[...].astype(F32)
    normal, spread = normal_of(values)
    total, slope = (
        jnp.where(core == core_ref[0], mine_ref[field].astype(F32), other_ref[field].astype(F32)) for field in range(2)
    )
    out_ref[...] = (values + total + shift_ref[...]).astype(BF16)
    slope_mean = jnp.mean(slope, axis=-1, keepdims=True)
    slope_dot = jnp.mean(slope * normal, axis=-1, keepdims=True)
    grad_ref[...] = (g_ref[...].astype(F32) + spread * (slope - slope_mean - normal * slope_dot)).astype(BF16)


def close(core, x, g, mine, other, shift, first_rows, waits=()):
    tokens, width = x.shape
    block = math.gcd(math.gcd(first_rows // 2, (tokens - first_rows) // 2), 128)
    first, rest = first_rows // (2 * block), (tokens - first_rows) // (2 * block)

    def source(m):
        late = m >= 2 * first
        local = m - jnp.where(late, 2 * first, 0)
        count = jnp.where(late, rest, first)
        core = jnp.where(local >= count, 1, 0)
        return core, local - core * count + jnp.where(late, first, 0)

    row_spec = pl.BlockSpec((block, width), lambda m, *_: (m, 0))
    total_spec = pl.BlockSpec((2, block, width), lambda m, *_: (0, source(m)[1], 0))
    return launch(
        lambda *refs: close_kernel(source, *refs),
        core,
        [x, g, mine, other, shift],
        waits,
        3,
        out_shape=[jax.ShapeDtypeStruct((tokens, width), BF16)] * 2,
        grid=(tokens // block,),
        in_specs=[row_spec, row_spec, total_spec, total_spec, pl.BlockSpec((1, width), lambda m, *_: (0, 0))],
        out_specs=[row_spec] * 2,
        name="close",
    )


def ranks_of(order, offsets):
    sources = lax.axis_index("ctx") ^ jnp.array(offsets, dtype=jnp.int32)
    match = sources[:, None] == jnp.arange(order.shape[1], dtype=jnp.int32)[None, :]
    return jnp.sum(jnp.where(match, order[:, None, :], 0), axis=-1)


def exchange_attention(local, remote, order, table, block_rows, waits):
    shape = (2, order.shape[0], block_rows, 4 * LANES)
    ranks = ranks_of(order, range(4)).reshape(-1)
    outs = attend(ranks, table, [local.reshape(shape), remote.reshape(shape)], waits)
    mine, theirs = (out.reshape(local.shape) for out in outs)
    return mine, swap(theirs, "ctx", 2)


def gathered_attention(local, remote, order, table, block_rows, waits):
    groups, micro = 2, order.shape[0]
    ctx = lax.axis_size("ctx")
    heads = groups * LANES // HD
    scale = HD ** (-0.5)
    packed = jnp.stack([local, remote]).reshape(groups, 2, micro, block_rows, 4 * LANES)
    packed = jnp.transpose(packed, (0, 2, 1, 3, 4))
    ranks = ranks_of(order, range(ctx))

    def split(array):
        array = array.reshape(groups, 2 * block_rows, LANES // HD, HD)
        return jnp.transpose(array, (1, 0, 2, 3)).reshape(2 * block_rows, heads, HD)

    def join(array):
        return jnp.transpose(array.reshape(2, block_rows, groups, LANES), (2, 0, 1, 3))

    def everywhere(array):
        return jnp.stack([array] + [swap(array, "ctx", j) for j in range(2, ctx, 2)])

    def home(array):
        total = array[0].astype(F32)
        for j in range(2, ctx, 2):
            total = total + swap(array[j // 2], "ctx", j).astype(F32)
        return total

    results = []
    for m in range(micro):
        parted = packed[:, m].reshape(groups, 2 * block_rows, 4, LANES)
        queries, keys, values, douts = (split(parted[:, :, i]) for i in range(4))
        all_keys, all_values = everywhere(keys), everywhere(values)
        key_ranks = jnp.repeat(ranks[m].reshape(-1, 2), block_rows, axis=1)
        query_ranks = key_ranks[0]
        allowed = (key_ranks[:, None, :] <= query_ranks[None, :, None])[:, None]

        def peak_step(state, item):
            key, value, ok = item
            peak, total, sums = state
            scores = jnp.einsum("bhe,rhe->hbr", queries, key, preferred_element_type=F32) * scale
            scores = jnp.where(ok, scores, -1e30)
            new = jnp.maximum(peak, jnp.max(scores, axis=-1))
            weights = jnp.where(ok, jnp.exp(scores - new[..., None]), 0.0)
            fade = jnp.exp(peak - new)
            part = jnp.einsum("hbr,rhe->hbe", weights.astype(BF16), value, preferred_element_type=F32)
            return (new, total * fade + jnp.sum(weights, axis=-1), sums * fade[..., None] + part), None

        start = (
            jnp.full((heads, 2 * block_rows), -1e30, F32),
            jnp.zeros((heads, 2 * block_rows), F32),
            jnp.zeros((heads, 2 * block_rows, HD), F32),
        )
        (peak, total, sums), _ = lax.scan(peak_step, start, (all_keys, all_values, allowed))
        attended = jnp.transpose(sums / total[..., None], (1, 0, 2))
        level = peak + jnp.log(total)
        delta = jnp.transpose(jnp.sum(douts.astype(F32) * attended, axis=-1))

        def back_step(query_sum, item):
            key, value, ok = item
            scores = jnp.einsum("bhe,rhe->hbr", queries, key, preferred_element_type=F32) * scale
            weights = jnp.where(ok, jnp.exp(scores - level[..., None]), 0.0)
            value_grad = jnp.einsum("hbr,bhe->rhe", weights.astype(BF16), douts, preferred_element_type=F32)
            slope = jnp.einsum("bhe,rhe->hbr", douts, value, preferred_element_type=F32)
            slope = (weights * (slope - delta[..., None])).astype(BF16)
            query_part = jnp.einsum("hbr,rhe->bhe", slope, key, preferred_element_type=F32) * scale
            key_grad = jnp.einsum("hbr,bhe->rhe", slope, queries, preferred_element_type=F32) * scale
            return query_sum + query_part, (key_grad.astype(BF16), value_grad.astype(BF16))

        query_grad, (key_grads, value_grads) = lax.scan(
            back_step, jnp.zeros(queries.shape, F32), (all_keys, all_values, allowed)
        )
        rows = [
            lax.dynamic_slice(table, (0, ranks[m, side] * block_rows, 0), (2, block_rows, LANES)) for side in range(2)
        ]
        rows = jnp.concatenate(rows, axis=1)

        def unturn(array):
            half = ROT // 2
            cosine, sine = rows[0, :, :half][:, None], rows[1, :, half:ROT][:, None]
            first, second = array[..., :half], array[..., half:ROT]
            return jnp.concatenate(
                [first * cosine + second * sine, second * cosine - first * sine, array[..., ROT:]], axis=-1
            )

        fields = (unturn(query_grad), unturn(home(key_grads)), home(value_grads), attended)
        results.append(jnp.concatenate([join(field.astype(BF16)) for field in fields], axis=-1))
    results = jnp.transpose(jnp.stack(results, axis=1), (0, 2, 1, 3, 4))
    mine, theirs = results.reshape(groups, *local.shape)
    return mine, theirs


def rotation_table(length):
    lane = jnp.arange(LANES, dtype=jnp.int32) % HD
    halves = ROT // 2
    frequency = jnp.exp((lane % halves).astype(F32) * (-2.0 * math.log(10000.0) / ROT))
    frequency = jnp.where(lane < ROT, frequency, 0.0)
    angles = jnp.arange(length, dtype=F32)[:, None] * frequency
    return jnp.stack([jnp.cos(angles), jnp.where(lane < halves, -1.0, 1.0) * jnp.sin(angles)])


def local(
    inputs,
    block_order,
    first_gain,
    first_shift,
    second_gain,
    second_shift,
    qkv_weight,
    qkv_bias,
    out_weight,
    out_bias,
    up_weight,
    up_bias,
    down_weight,
    down_bias,
    out_grad,
):
    micro, block_rows, _, width = inputs.shape
    ctx = lax.axis_size("ctx")
    f, z, core = lax.axis_index("fsdp"), lax.axis_index("ctx"), lax.axis_index("tp")
    low = z & 1
    rows = up_weight.shape[0]
    groups, hidden = 2, up_weight.shape[1] // 2
    tokens = micro * block_rows
    order = block_order[:, 0]
    first_part = micro - 1
    parts = ((0, first_part), (first_part, micro))
    exchanging = ctx == 2 * groups

    fields = [qkv_weight[0], qkv_weight[1], qkv_weight[2], jnp.transpose(out_weight)]
    extent = groups * LANES
    halves = [jnp.concatenate([field[:, i * extent : (i + 1) * extent] for field in fields], axis=1) for i in range(2)]
    shard = jnp.stack(halves)

    x, g = inputs.reshape(tokens, width), out_grad.reshape(tokens, width)
    fields = [up_weight, jnp.transpose(down_weight)]
    halves = [jnp.concatenate([field[:, i * hidden : (i + 1) * hidden] for field in fields], axis=1) for i in range(2)]
    forward_shard, both, shard = lax.optimization_barrier((jnp.stack(halves), jnp.stack([x, g]), shard))
    column = gather_column(*choose(low, shard[0], shard[1]))
    own, other = choose(low, forward_shard[0], forward_shard[1])
    forward_pair = jnp.concatenate([own, swap(other, "ctx", 1)], axis=0)
    lanes, _ = choose(core, both[:, :, : width // 2], both[:, :, width // 2 :])
    lanes, column[1] = lax.optimization_barrier((lanes, column[1]))
    lanes = swap(lanes, "ctx", 1)
    column = jnp.concatenate(column, axis=0)
    pieces = gather_pieces(column)

    table = rotation_table(ctx * block_rows)
    index = jnp.stack([f * ctx + z, core]).astype(jnp.int32)
    gains = jnp.stack([first_gain, first_shift, second_gain, second_shift]).astype(F32)
    prepared, grad_sum = prepare_own(
        index, x, g, gains, rows, block_rows, (column, forward_pair, table)
    )
    forward_column = [forward_pair] + [swap(forward_pair, "ctx", j) for j in range(2, ctx, 2)]
    lanes, grad_sum, *pieces = lax.optimization_barrier((lanes, grad_sum, *pieces))
    arrived = (lanes, swap(lanes, "tp", 1))
    x_both, g_both, one = prepare_pair(
        index, arrived, gains, prepared, rows, block_rows, first_part
    )

    place = ((z >> 1) if exchanging else jnp.zeros_like(z)).astype(jnp.int32).reshape(1)
    bias = qkv_bias.astype(F32)
    bias = choose(low, bias[:, :extent], bias[:, extent:])[0].reshape(1, -1)
    attention = exchange_attention if exchanging else gathered_attention
    send = (lambda item: swap(item, "ctx", 2)) if exchanging else (lambda item: item)
    packed, first_block = [], 0
    for begin, end in parts:
        ranks = jnp.transpose(ranks_of(order[begin:end], (0, 1))).reshape(-1)
        count = 2 * (end - begin)
        waits = [forward_column] if packed else []
        mine, other = project(
            place, ranks, one, g_both, first_block, count, table, bias, pieces, block_rows, waits
        )
        if not packed:
            forward_column[0], mine = lax.optimization_barrier((forward_column[0], mine))
            forward_column = jnp.concatenate(forward_column, axis=0)
            forward_pieces = gather_pieces(forward_column)
        packed.append((first_block * block_rows, mine, other))
        first_block += count

    two, one_t, two_t, g_t = prepare_late(index, x_both, g_both, one, gains, rows, block_rows, (packed[1][1],))
    up_shift = up_bias.astype(F32).reshape(2, 1, hidden)
    up_shift = choose(low, up_shift[0], up_shift[1])[0]
    arrivals = [send(theirs) for _, _, theirs in packed]
    returned = [attention(packed[0][1], arrivals[0], order[: parts[0][1]], table, block_rows, (g_t,))]
    branch, slope, up_sum, forward_grads = feed_forward(
        two, g_both, two_t, g_t, up_shift, forward_pieces, (returned[0][0],)
    )
    returned.append(attention(packed[1][1], arrivals[1], order[parts[1][0] :], table, block_rows, (up_sum,)))

    scalars = jnp.stack([f * ctx + z, place[0], low, core]).astype(jnp.int32)
    end_shift = (out_bias.astype(F32) + down_bias.astype(F32)).reshape(1, width)
    forward_terms = scatter(forward_grads)
    pairs = range(2, ctx, 2)

    def finish_part(number, small, waits):
        first, (local, remote) = packed[number][0], returned[number]
        mine, theirs, small = finish(
            scalars, x_both, gains, branch, slope, first, local, remote, small, pieces, rows, waits
        )
        return (mine, swap(theirs, "tp", 1)), small

    def weights_part(number, before, waits):
        first, (local, remote) = packed[number][0], returned[number]
        return attention_weights(place, one_t, g_t, first, local, remote, before, len(pieces), waits)

    zero = jnp.zeros((1, width), F32)
    small = jnp.concatenate([zero] * 4 + [grad_sum, zero, zero, *choose(low, up_sum, zero)] + [zero] * (SMALL_ROWS - 9))
    made = {}

    def run(task, wait):
        if task == "finish_a":
            made["a"], made["small"] = finish_part(0, small, (wait,))
            return made["small"]
        if task == "weights_a":
            made["grads_a"] = weights_part(0, None, (wait,))
            return made["grads_a"]
        if task == "forward_first":
            keep, *send = reduce_and_cut(
                forward_terms, [(0, 2 * rows, F32)] + [(j * rows, 2 * rows, BF16) for j in pairs], (wait,)
            )
            made["forward"] = [keep] + [swap(item, "ctx", j) for j, item in zip(pairs, send)]
            return keep
        if task == "finish_b":
            made["b"], made["small"] = finish_part(1, made["small"], (wait,))
            return made["small"]
        if task == "weights_b":
            grads = weights_part(1, (made["grads_a"], made["small"]), (wait,))
            made["attention"] = scatter(grads)
            return grads[0]
        if task == "forward_second":
            made["mine"], made["send"] = reduce_and_cut(
                made["forward"], [(0, rows, F32), (rows, rows, BF16)], (wait,)
            )
            return made["mine"]
        if task == "attention_first":
            made["keep"], *send = reduce_and_cut(
                made["attention"],
                [(0, rows, F32)] + [(j * rows, rows, BF16) for j in range(1, ctx)],
                (wait,),
                SMALL_ROWS,
            )
            made["sent"] = [swap(item, "ctx", j) for j, item in enumerate(send, 1)]
            return made["keep"]
        if task == "sums":
            sums = core_sums(1, [*made["a"], *made["b"]], (), (wait,))
            made["pair"] = swap(sums, "ctx", 1)
            return sums
        if task == "totals":
            totals = core_sums(0, [*made["a"], *made["b"]], [made["pair"]], (wait, *made["sent"]))
            made["totals"] = (totals, swap(totals, "tp", 1))
            return totals
        core_place = core.astype(jnp.int32).reshape(1)
        made["results"] = close(core_place, x, g, *made["totals"], end_shift, packed[1][0] // 2, (wait,))
        return made["results"][0]

    wait = returned[1][0]
    for task in TASKS:
        wait = run(task, wait)
    forward_mine, forward_send, attention_keep, results = (made[key] for key in ("mine", "send", "keep", "results"))
    attention_got = made["sent"]
    forward_got, done = lax.optimization_barrier((swap(forward_send, "ctx", 1), results[0]))
    results = [done, results[1]]
    outputs, input_grad = (item.reshape(inputs.shape) for item in results)
    forward_sums = choose(low, forward_mine, forward_got.astype(F32))
    up_sums = jnp.concatenate([half[0] for half in forward_sums], axis=1)
    down_sums = jnp.concatenate([jnp.transpose(half[1]) for half in forward_sums], axis=0)

    terms = [attention_keep[0]] + [got[0].astype(F32) for got in attention_got]
    halves = choose(low, tree_sum([term[:rows] for term in terms[::2]]), tree_sum([term[:rows] for term in terms[1::2]]))
    small = tree_sum([term[rows:] for term in terms])
    fields = [
        jnp.concatenate([half[:, i * extent : (i + 1) * extent] for half in halves], axis=1) for i in range(4)
    ]
    norm_sums = small[:4] + swap(small[:4], "tp", 1)
    pre_sums = small[5:7, : 3 * extent].reshape(2, 3, extent)
    return (
        outputs,
        input_grad,
        norm_sums[0],
        norm_sums[1],
        norm_sums[2],
        norm_sums[3],
        jnp.stack(fields[:3]),
        jnp.concatenate([pre_sums[0], pre_sums[1]], axis=1),
        jnp.transpose(fields[3]),
        small[4],
        up_sums,
        small[7:9].reshape(-1),
        down_sums,
        small[4],
    )


def solution(mesh):
    placed = (
        P(None, "ctx", "fsdp", None),
        P(None, "fsdp", None),
        P(),
        P(),
        P(),
        P(),
        P(None, ("fsdp", "ctx"), "tp"),
        P(None, "tp"),
        P("tp", ("fsdp", "ctx")),
        P(),
        P(("fsdp", "ctx"), "tp"),
        P("tp"),
        P("tp", ("fsdp", "ctx")),
        P(),
        P(None, "ctx", "fsdp", None),
    )
    return jax.shard_map(
        local,
        mesh=mesh,
        in_specs=placed,
        out_specs=(
            P(None, "ctx", "fsdp", None),
            P(None, "ctx", "fsdp", None),
            P(),
            P(),
            P(),
            P(),
            P(None, ("fsdp", "ctx"), "tp"),
            P(None, "tp"),
            P("tp", ("fsdp", "ctx")),
            P(),
            P(("fsdp", "ctx"), "tp"),
            P("tp"),
            P("tp", ("fsdp", "ctx")),
            P(),
        ),
        check_vma=False,
    )
```

```python
import math

import jax
import jax.numpy as jnp
from jax import lax
from jax.experimental import pallas as pl
from jax.experimental.pallas import tpu as pltpu
from jax.sharding import PartitionSpec as P

HD = 64
ROT = 16
LANES = 128
F32 = jnp.float32
BF16 = jnp.bfloat16
MIB = 1024 * 1024
EPSILON = 1e-05
TASKS = (
    "finish_a",
    "weights_a",
    "forward_first",
    "finish_b",
    "weights_b",
    "sums",
    "forward_second",
    "attention_first",
    "totals",
    "close",
)
SMALL_ROWS = 16
SHARE = 1 / 0.6


def swap(value, axis, bit):
    size = lax.axis_size(axis)
    return lax.ppermute(value, axis, [(i, i ^ bit) for i in range(size)])


def choose(bit, first, second):
    return jnp.where(bit == 0, first, second), jnp.where(bit == 0, second, first)


def gather_column(own, other):
    return [own] + [swap(other if j & 1 else own, "ctx", j) for j in range(1, lax.axis_size("ctx"))]


def gather_pieces(column):
    return [column] + [swap(column, "fsdp", j) for j in range(1, lax.axis_size("fsdp"))]


def launch(kernel, scalars, operands, waits, us, *, grid, in_specs, out_specs, out_shape, scratch_shapes=(), mib=24, **more):
    count = (scalars is not None) + len(operands)

    def body(*refs):
        kernel(*refs[:count], *refs[count + len(waits) :])

    return pl.pallas_call(
        body,
        out_shape=out_shape,
        grid_spec=pltpu.PrefetchScalarGridSpec(
            num_scalar_prefetch=0 if scalars is None else 1,
            grid=grid,
            in_specs=[*in_specs] + [pl.BlockSpec(memory_space=pl.ANY)] * len(waits),
            out_specs=out_specs,
            scratch_shapes=scratch_shapes,
        ),
        compiler_params=pltpu.CompilerParams(vmem_limit_bytes=mib * MIB),
        cost_estimate=pl.CostEstimate(flops=int(us * SHARE * 1.1e9), bytes_accessed=1024, transcendentals=0),
        **more,
    )(*([] if scalars is None else [scalars]), *operands, *waits)


def matmul(lhs, rhs):
    return jnp.dot(lhs, rhs, preferred_element_type=F32)


def against(lhs, rhs):
    return lax.dot_general(lhs, rhs, (((1,), (1,)), ((), ())), preferred_element_type=F32)


def exchanged(load, width, index, rows):
    shift = index * rows
    high, low = shift // LANES, lax.rem(shift, LANES)
    blocks = []
    for block in range(width // LANES):
        start = pl.multiple_of((block ^ high) * LANES, LANES)
        value = load(pl.ds(start, LANES)).astype(F32)
        step = rows
        while step < LANES:
            lane = lax.broadcasted_iota(jnp.int32, value.shape, 1)
            turned = pltpu.roll(value, step, 1)
            if 2 * step != LANES:
                turned = jnp.where((lane & step) != 0, turned, pltpu.roll(value, LANES - step, 1))
            value = jnp.where((low & step) != 0, turned, value)
            step *= 2
        blocks.append(value)
    return jnp.concatenate(blocks, axis=1)


def normal_of(values):
    centre = jnp.mean(values, axis=-1, keepdims=True)
    offset = values - centre
    spread = lax.rsqrt(jnp.mean(offset * offset, axis=-1, keepdims=True) + EPSILON)
    return offset * spread, spread


def prepare_block(rows, index, load_x, load_g, gains_ref, outs):
    x_out, g_out, one_out = outs
    width = x_out.shape[1]
    values = exchanged(load_x, width, index, rows)
    gains = exchanged(lambda lanes: gains_ref[:, lanes], width, index, rows)
    normal, _ = normal_of(values)
    x_out[...] = values.astype(BF16)
    g_out[...] = exchanged(load_g, width, index, rows).astype(BF16)
    one_out[...] = (normal * gains[0:1] + gains[1:2]).astype(BF16)


def prepare_own_kernel(rows, index_ref, x_ref, g_ref, gains_ref, *refs):
    outs, sum_out = refs[:3], refs[3]
    prepare_block(rows, index_ref[0], lambda lanes: x_ref[:, lanes], lambda lanes: g_ref[:, lanes], gains_ref, outs)

    @pl.when(pl.program_id(0) == 0)
    def _():
        sum_out[...] = jnp.zeros_like(sum_out)

    sum_out[...] += jnp.sum(g_ref[...].astype(F32), axis=0, keepdims=True)


def prepare_pair_kernel(rows, count, index_ref, mine_ref, other_ref, gains_ref, *refs):
    half = mine_ref.shape[2]

    def loader(field):
        def load(lanes):
            inside = pl.ds(pl.multiple_of(lax.rem(lanes.start, half), LANES), lanes.size)
            mine, other = mine_ref[field, :, inside].astype(F32), other_ref[field, :, inside].astype(F32)
            return jnp.where(lanes.start // half == index_ref[1], mine, other)

        return load

    own_refs, out_refs = refs[:3], refs[3:]
    step = pl.program_id(0)

    @pl.when(step < count)
    def _():
        for own, out in zip(own_refs, out_refs):
            out[...] = own[...]

    @pl.when(step >= count)
    def _():
        prepare_block(rows, index_ref[0], loader(0), loader(1), gains_ref, out_refs)


def prepare_late_kernel(rows, index_ref, x_ref, g_ref, one_ref, gains_ref, two_out, one_t, two_t, g_t):
    normal, _ = normal_of(x_ref[...].astype(F32))
    gains = exchanged(lambda lanes: gains_ref[:, lanes], x_ref.shape[1], index_ref[0], rows)
    two = (normal * gains[2:3] + gains[3:4]).astype(BF16)
    two_out[...] = two
    one_t[...] = one_ref[...].T
    two_t[...] = two.T
    g_t[...] = g_ref[...].T


def prepare_own(index, x, g, gains, rows, block_rows, waits=()):
    tokens, width = x.shape
    row_spec = pl.BlockSpec((block_rows, width), lambda m, *_: (m, 0))
    *outs, grad_sum = launch(
        lambda *refs: prepare_own_kernel(rows, *refs),
        index,
        [x, g, gains],
        waits,
        2.100,
        out_shape=[jax.ShapeDtypeStruct((tokens, width), BF16)] * 3 + [jax.ShapeDtypeStruct((1, width), F32)],
        grid=(tokens // block_rows,),
        in_specs=[row_spec, row_spec, pl.BlockSpec(gains.shape, lambda m, *_: (0, 0))],
        out_specs=[row_spec] * 3 + [pl.BlockSpec((1, width), lambda m, *_: (0, 0))],
        name="prepare_own",
    )
    return outs, grad_sum


def prepare_pair(index, arrived, gains, own, rows, block_rows, first_part, waits=()):
    _, tokens, half = arrived[0].shape
    width = 2 * half
    count = tokens // block_rows

    def place(step):
        m, side = lax.rem(step, count), step // count
        return m + jnp.where(m < first_part, side * first_part, first_part + side * (count - first_part))

    half_spec = pl.BlockSpec((2, block_rows, half), lambda m, *_: (0, jnp.maximum(m - count, 0), 0))
    own_spec = pl.BlockSpec((block_rows, width), lambda m, *_: (jnp.minimum(m, count - 1), 0))
    return launch(
        lambda *refs: prepare_pair_kernel(rows, count, *refs),
        index,
        [*arrived, gains, *own],
        waits,
        2.100,
        out_shape=[jax.ShapeDtypeStruct((2 * tokens, width), BF16)] * 3,
        grid=(2 * count,),
        in_specs=[half_spec, half_spec, pl.BlockSpec(gains.shape, lambda m, *_: (0, 0))] + [own_spec] * 3,
        out_specs=[pl.BlockSpec((block_rows, width), lambda m, *_: (place(m), 0))] * 3,
        name="prepare_pair",
    )


def prepare_late(index, x, g, one, gains, rows, block_rows, waits=()):
    tokens, width = x.shape
    row_spec = pl.BlockSpec((block_rows, width), lambda m, *_: (m, 0))
    column_spec = pl.BlockSpec((width, block_rows), lambda m, *_: (0, m))
    plain, turned = jax.ShapeDtypeStruct((tokens, width), BF16), jax.ShapeDtypeStruct((width, tokens), BF16)
    return launch(
        lambda *refs: prepare_late_kernel(rows, *refs),
        index,
        [x, g, one, gains],
        waits,
        3.600,
        out_shape=[plain, turned, turned, turned],
        grid=(tokens // block_rows,),
        in_specs=[row_spec, row_spec, row_spec, pl.BlockSpec(gains.shape, lambda m, *_: (0, 0))],
        out_specs=[row_spec, column_spec, column_spec, column_spec],
        name="prepare_late",
        mib=24,
    )


def turn(values, cosine, sine):
    lane = lax.broadcasted_iota(jnp.int32, values.shape, 1) % HD
    ahead = pltpu.roll(values, LANES - ROT // 2, 1)
    behind = pltpu.roll(values, ROT // 2, 1)
    return values * cosine + jnp.where(lane < ROT // 2, ahead, behind) * sine


def gather_weight(piece_refs, weight_s):
    @pl.when(pl.program_id(0) == 0)
    def _():
        start = 0
        for ref in piece_refs:
            weight_s[start : start + ref.shape[0], :] = ref[...]
            start += ref.shape[0]


def pick(place, first, second):
    return jnp.where(place == 0, first, second), jnp.where(place == 0, second, first)


def project_kernel(fsdp, block_rows, scalar_ref, one_ref, g_ref, table_ref, bias_ref, *refs):
    piece_refs, (local_ref, remote_ref, weight_s) = refs[:fsdp], refs[fsdp:]
    tokens, width = one_ref.shape
    gather_weight(piece_refs, weight_s)
    pre = matmul(one_ref[...], weight_s[:, : 6 * LANES]) + bias_ref[...]
    back = matmul(g_ref[...], weight_s[:, 6 * LANES :])
    for block in range(tokens // block_rows):
        rows = slice(block * block_rows, (block + 1) * block_rows)
        rank = scalar_ref[1 + pl.program_id(0) * (tokens // block_rows) + block]
        places = pl.ds(pl.multiple_of(rank * block_rows, block_rows), block_rows)
        cosine, sine = table_ref[0, places, :], table_ref[1, places, :]
        for field in range(4):
            source = pre[rows] if field < 3 else back[rows]
            start = 2 * field * LANES if field < 3 else 0
            both = [source[:, start + group * LANES : start + (group + 1) * LANES] for group in range(2)]
            if field < 2:
                both = [turn(item, cosine, sine) for item in both]
            here = slice(field * LANES, (field + 1) * LANES)
            mine, other = pick(scalar_ref[0], *both)
            local_ref[rows, here] = mine.astype(BF16)
            remote_ref[rows, here] = other.astype(BF16)


def project(place, ranks, one, g, first, count, table, bias, pieces, block_rows, waits=()):
    width = one.shape[1]
    fsdp = len(pieces)
    tokens = count * block_rows
    tile = 2 * block_rows
    base = first // 2
    side = pl.BlockSpec((tile, width), lambda t, *_: (base + t, 0))
    once = pl.Buffered(1)
    out = pl.BlockSpec((tile, 4 * LANES), lambda t, *_: (t, 0))
    return launch(
        lambda *refs: project_kernel(fsdp, block_rows, *refs),
        jnp.concatenate([place, ranks]),
        [one, g, table, bias, *pieces],
        waits,
        tokens / 500.000,
        out_shape=[jax.ShapeDtypeStruct((tokens, 4 * LANES), BF16)] * 2,
        grid=(tokens // tile,),
        in_specs=[
            side,
            side,
            pl.BlockSpec(table.shape, lambda t, *_: (0, 0, 0), pipeline_mode=once),
            pl.BlockSpec(bias.shape, lambda t, *_: (0, 0)),
        ]
        + [pl.BlockSpec(piece.shape, lambda t, *_: (0, 0), pipeline_mode=once) for piece in pieces],
        out_specs=[out, out],
        scratch_shapes=[pltpu.VMEM((width, 8 * LANES), BF16)],
        name="project",
        mib=28,
    )


def attend_kernel(blocks, block_rows, scale, rank_ref, table_ref, *refs):
    count = blocks // 2
    chunk_refs, out_refs = refs[:count], refs[count : 2 * count]
    q_s, k_s, v_s, d_s, kt_s, vt_s, ot_s, qt_s, dk_s, dv_s = refs[2 * count :]
    item = pl.program_id(0)

    def rows_of(index):
        return pl.ds(pl.multiple_of(rank_ref[item * blocks + index] * block_rows, block_rows), block_rows)

    for index in range(blocks):
        rows, chunk, side = rows_of(index), chunk_refs[index // 2], index % 2
        q_s[rows, :] = chunk[side, 0, :, :LANES]
        k_s[rows, :] = chunk[side, 0, :, LANES : 2 * LANES]
        v_s[rows, :] = chunk[side, 0, :, 2 * LANES : 3 * LANES]
        d_s[rows, :] = chunk[side, 0, :, 3 * LANES :]
    kt_s[...] = k_s[...].T
    vt_s[...] = v_s[...].T
    lane = lax.broadcasted_iota(jnp.int32, (block_rows, LANES), 1)
    dk_s[...] = jnp.zeros_like(dk_s)
    dv_s[...] = jnp.zeros_like(dv_s)

    def head_step(head, carry):
        inside = (lane // HD) == head
        heads = pl.ds(pl.multiple_of(head * HD, HD), HD)
        for rank in range(blocks):
            rows = slice(rank * block_rows, (rank + 1) * block_rows)
            keys = slice(0, (rank + 1) * block_rows)
            q_h = jnp.where(inside, q_s[rows, :], 0).astype(BF16)
            d_h = jnp.where(inside, d_s[rows, :], 0).astype(BF16)
            scores = against(k_s[keys, :], q_h) * scale
            weights = jnp.exp(scores - jnp.max(scores, axis=0, keepdims=True))
            weights = weights * (1.0 / jnp.sum(weights, axis=0, keepdims=True))
            low = weights.astype(BF16)
            ot_s[heads, rows] = matmul(vt_s[heads, keys], low)
            dv_s[keys, :] += matmul(low, d_h)
            slope = against(v_s[keys, :], d_h)
            delta = jnp.sum(weights * slope, axis=0, keepdims=True)
            slope = (weights * (slope - delta)).astype(BF16)
            qt_s[heads, rows] = matmul(kt_s[heads, keys], slope)
            dk_s[keys, :] += matmul(slope, q_h)
        return carry

    lax.fori_loop(0, LANES // HD, head_step, 0)
    for index in range(blocks):
        rows, out, side = rows_of(index), out_refs[index // 2], index % 2
        cosine, sine = table_ref[0, rows, :], -table_ref[1, rows, :]
        out[side, 0, :, :LANES] = turn(qt_s[:, rows].T * scale, cosine, sine).astype(BF16)
        out[side, 0, :, LANES : 2 * LANES] = turn(dk_s[rows, :] * scale, cosine, sine).astype(BF16)
        out[side, 0, :, 2 * LANES : 3 * LANES] = dv_s[rows, :].astype(BF16)
        out[side, 0, :, 3 * LANES :] = ot_s[:, rows].T.astype(BF16)


def attend(ranks, table, chunks, waits=()):
    sides, count, block_rows, _ = chunks[0].shape
    blocks = sides * len(chunks)
    length = blocks * block_rows
    spec = pl.BlockSpec((sides, 1, block_rows, 4 * LANES), lambda m, *_: (0, m, 0, 0))
    pairs = count * blocks * (blocks + 1) // 2 * block_rows * block_rows
    return launch(
        lambda *refs: attend_kernel(blocks, block_rows, HD ** (-0.5), *refs),
        ranks,
        [table, *chunks],
        waits,
        11 * count,
        out_shape=[jax.ShapeDtypeStruct(chunk.shape, BF16) for chunk in chunks],
        grid=(count,),
        in_specs=[pl.BlockSpec(table.shape, lambda m, *_: (0, 0, 0))] + [spec] * len(chunks),
        out_specs=[spec] * len(chunks),
        scratch_shapes=[pltpu.VMEM((length, LANES), BF16)] * 4
        + [pltpu.VMEM((LANES, length), BF16)] * 2
        + [pltpu.VMEM((LANES, length), F32)] * 2
        + [pltpu.VMEM((length, LANES), F32)] * 2,
        name="attend",
        mib=24,
    )


def forward_kernel(fsdp, two_ref, g_ref, two_t, g_t, bias_ref, *refs):
    up_refs, down_refs = refs[:fsdp], refs[fsdp : 2 * fsdp]
    branch_ref, slope_ref, sum_ref = refs[2 * fsdp : 2 * fsdp + 3]
    out_refs, (up_s, down_s) = refs[2 * fsdp + 3 : -2], refs[-2:]
    width = two_ref.shape[1]
    span = width // fsdp
    lanes = [slice(offset * span, (offset + 1) * span) for offset in range(fsdp)]
    for offset in range(fsdp):
        up_s[lanes[offset], :] = up_refs[offset][...]
        down_s[lanes[offset], :] = down_refs[offset][...]
    pre = matmul(two_ref[...], up_s[...]) + bias_ref[...]
    back = matmul(g_ref[...], down_s[...])
    gate = 0.5 * (1.0 + lax.erf(pre * math.sqrt(0.5)))
    bell = jnp.exp(-0.5 * pre * pre) * (1.0 / math.sqrt(2.0 * math.pi))
    hidden = (pre * gate).astype(BF16)
    pre_grad = (back * (gate + pre * bell)).astype(BF16)
    sum_ref[...] = jnp.sum(pre_grad.astype(F32), axis=0, keepdims=True)

    @pl.when(pl.program_id(0) == 0)
    def _():
        branch_ref[...] = against(hidden, down_s[...])
        slope_ref[...] = against(pre_grad, up_s[...])

    @pl.when(pl.program_id(0) != 0)
    def _():
        branch_ref[...] += against(hidden, down_s[...])
        slope_ref[...] += against(pre_grad, up_s[...])

    for offset in range(fsdp):
        out = out_refs[offset]
        out[0] = matmul(two_t[lanes[offset], :], pre_grad).astype(out.dtype)
        out[1] = matmul(g_t[lanes[offset], :], hidden).astype(out.dtype)


def feed_forward(two, g, two_t, g_t, bias, pieces, waits=()):
    tokens, width = two.shape
    fsdp = len(pieces)
    span, hidden = pieces[0].shape[0], pieces[0].shape[1] // 2
    tile = 512
    tiles = hidden // tile
    once = pl.Buffered(1)
    whole = pl.BlockSpec((tokens, width), lambda n: (0, 0), pipeline_mode=once)
    whole_t = pl.BlockSpec((width, tokens), lambda n: (0, 0), pipeline_mode=once)
    piece = pl.BlockSpec((span, tile), lambda n: (0, n))
    later = pl.BlockSpec((span, tile), lambda n: (0, n + tiles))
    line = pl.BlockSpec((1, tile), lambda n: (0, n))
    grads = [jax.ShapeDtypeStruct((2, span, hidden), BF16 if offset else F32) for offset in range(fsdp)]
    grad = pl.BlockSpec((2, span, tile), lambda n: (0, 0, n))
    branch, slope, sums, *grads = launch(
        lambda *refs: forward_kernel(fsdp, *refs),
        None,
        [two, g, two_t, g_t, bias, *pieces, *pieces],
        waits,
        34,
        out_shape=[jax.ShapeDtypeStruct((tokens, width), F32)] * 2
        + [jax.ShapeDtypeStruct((1, hidden), F32)]
        + grads,
        grid=(tiles,),
        in_specs=[whole, whole, whole_t, whole_t, line] + [piece] * fsdp + [later] * fsdp,
        out_specs=[whole, whole, line] + [grad] * fsdp,
        scratch_shapes=[pltpu.VMEM((width, tile), BF16)] * 2,
        name="feed_forward",
        mib=60,
    )
    return branch, slope, sums, grads


def collect(place, local_ref, remote_ref, stack_s):
    for ref, group in ((local_ref, place), (remote_ref, 1 - place)):
        for field in range(4):
            here = pl.ds(pl.multiple_of((2 * field + group) * LANES, LANES), LANES)
            stack_s[:, here] = ref[:, field * LANES : (field + 1) * LANES]


def weights_kernel(fsdp, last, place_ref, one_t, g_t, local_ref, remote_ref, *refs):
    before_ref, small_ref = refs[:2] if last else (None, None)
    out_refs, stack_s = refs[2 if last else 0 : -1], refs[-1]
    step = pl.program_id(0)
    span = one_t.shape[0]

    @pl.when(step == 0)
    def _():
        collect(place_ref[0], local_ref, remote_ref, stack_s)

    pre_part = matmul(one_t[...], stack_s[:, : 6 * LANES])
    out_part = matmul(g_t[...], stack_s[:, 6 * LANES :])
    if not last:
        out_refs[0][0, :, : 6 * LANES] = pre_part
        out_refs[0][0, :, 6 * LANES :] = out_part
    else:
        pre_part = pre_part + before_ref[0, :, : 6 * LANES]
        out_part = out_part + before_ref[0, :, 6 * LANES :]
        small = small_ref[...].astype(BF16)
        for offset in range(fsdp):

            @pl.when(step == offset)
            def _():
                out = out_refs[offset]
                out[0, :span, : 6 * LANES] = pre_part.astype(out.dtype)
                out[0, :span, 6 * LANES :] = out_part.astype(out.dtype)
                out[0, span:, :] = small.astype(out.dtype)


def attention_weights(place, one_t, g_t, first, local, remote, before, fsdp, waits=()):
    width = one_t.shape[0]
    tokens = local.shape[0]
    span = width // fsdp
    columns = 8 * LANES
    last = before is not None
    stack = jax.ShapeDtypeStruct((fsdp, span, columns), F32)
    grads = [
        jax.ShapeDtypeStruct((1, span + SMALL_ROWS, columns), BF16 if offset else F32) for offset in range(fsdp)
    ]
    piece = pl.BlockSpec((span, tokens), lambda o, *_: (o, first // tokens))
    slab = pl.BlockSpec((1, span, columns), lambda o, *_: (o, 0, 0))
    whole = lambda item: pl.BlockSpec(item.shape, lambda o, *_: (0,) * len(item.shape))
    grads = launch(
        lambda *refs: weights_kernel(fsdp, last, *refs),
        place,
        [one_t, g_t, local, remote, *(before if last else [])],
        waits,
        7 if last else 0.5,
        out_shape=grads if last else [stack],
        grid=(fsdp,),
        in_specs=[piece, piece, whole(local), whole(remote)] + ([slab, whole(before[1])] if last else []),
        out_specs=[whole(item) for item in grads] if last else [slab],
        scratch_shapes=[pltpu.VMEM((tokens, columns), BF16)],
        name="attention_weights",
    )
    return list(grads) if last else grads[0]


def finish_kernel(fsdp, rows, scalar_ref, x_ref, gains_ref, branch_ref, slope_ref, local_ref, remote_ref, before_ref, *refs):
    piece_refs, (mine_ref, theirs_ref, small_ref, stack_s, one_s, branch_s, out_s, norm_s) = refs[:fsdp], refs[fsdp:]
    half, width = x_ref.shape
    span = width // fsdp
    step = pl.program_id(0)
    index = scalar_ref[0]
    gains = exchanged(lambda item: gains_ref[:, item], width, index, rows)

    @pl.when(step == 0)
    def _():
        norm_s[...] = jnp.zeros_like(norm_s)
        collect(scalar_ref[1], local_ref, remote_ref, stack_s)
        for offset in range(fsdp):
            lanes = slice(offset * span, (offset + 1) * span)
            one_s[:, lanes] = against(stack_s[:, : 6 * LANES], piece_refs[offset][:, : 6 * LANES])
            branch_s[:, lanes] = against(stack_s[:, 6 * LANES :], piece_refs[offset][:, 6 * LANES :])

    here = pl.ds(pl.multiple_of((2 * lax.rem(step, 2) + ((step // 2) ^ scalar_ref[3])) * half, half), half)
    one, two = one_s[here, :], slope_ref[...]
    normal, _ = normal_of(x_ref[...].astype(F32))
    norm_s[0:1, :] += jnp.sum(one * normal, axis=0, keepdims=True)
    norm_s[1:2, :] += jnp.sum(one, axis=0, keepdims=True)
    norm_s[2:3, :] += jnp.sum(two * normal, axis=0, keepdims=True)
    norm_s[3:4, :] += jnp.sum(two, axis=0, keepdims=True)
    plain = []
    for value in (branch_ref[...] + branch_s[here, :], one * gains[0:1] + two * gains[2:3]):
        out_s[...] = value
        plain.append(exchanged(lambda item: out_s[:, item], width, index, rows).astype(BF16))

    for which, ref in enumerate((mine_ref, theirs_ref)):

        @pl.when(step // 2 == which)
        def _():
            ref[0, 0], ref[0, 1] = plain

    @pl.when(step == 3)
    def _():
        small_ref[...] = before_ref[...]
        small_ref[0:4, :] += exchanged(lambda item: norm_s[0:4, item], width, index, rows)
        small_ref[pl.ds(5 + scalar_ref[2], 1), : 6 * LANES] += jnp.sum(
            stack_s[:, : 6 * LANES].astype(F32), axis=0, keepdims=True
        )


def finish(scalars, x, gains, branch, slope, first, local, remote, small, pieces, rows, waits=()):
    width = x.shape[1]
    fsdp = len(pieces)
    half = local.shape[0] // 4
    base = first // half
    once = pl.Buffered(1)
    fixed = lambda item: pl.BlockSpec(item.shape, lambda t, *_: (0, 0))
    place = lambda t, scalars: 2 * lax.rem(t, 2) + ((t // 2) ^ scalars[3])
    row_spec = pl.BlockSpec((half, width), lambda t, scalars: (base + place(t, scalars), 0))
    back_spec = pl.BlockSpec(local.shape, lambda t, *_: (0, 0), pipeline_mode=once)
    mine_spec = pl.BlockSpec((1, 2, half, width), lambda t, *_: (jnp.minimum(t, 1), 0, 0, 0))
    theirs_spec = pl.BlockSpec((1, 2, half, width), lambda t, *_: (jnp.maximum(t - 2, 0), 0, 0, 0))
    sums = jax.ShapeDtypeStruct((2, 2, half, width), BF16)
    return launch(
        lambda *refs: finish_kernel(fsdp, rows, *refs),
        scalars,
        [x, gains, branch, slope, local, remote, small, *pieces],
        waits,
        half / 20 if first else 0.5,
        out_shape=[sums, sums, jax.ShapeDtypeStruct(small.shape, F32)],
        grid=(4,),
        in_specs=[row_spec, fixed(gains), row_spec, row_spec, back_spec, back_spec, fixed(small)]
        + [pl.BlockSpec(piece.shape, lambda t, *_: (0, 0), pipeline_mode=once) for piece in pieces],
        out_specs=[mine_spec, theirs_spec, fixed(small)],
        scratch_shapes=[
            pltpu.VMEM((4 * half, 8 * LANES), BF16),
            pltpu.VMEM((4 * half, width), F32),
            pltpu.VMEM((4 * half, width), F32),
            pltpu.VMEM((half, width), F32),
            pltpu.VMEM((8, width), F32),
        ],
        name="finish",
        mib=40,
    )


def sums_kernel(parts, *refs):
    terms, out = refs[:-1], refs[-1]
    start = 0
    for number in range(parts):
        mine, other = terms[2 * number : 2 * number + 2]
        rows = slice(start, start + mine.shape[2])
        total = mine[0, 0].astype(F32) + other[0, 0].astype(F32)
        if len(terms) > 2 * parts:
            total = total + terms[-1][0, rows, :].astype(F32)
        out[0, rows, :] = total.astype(BF16)
        start += mine.shape[2]


def core_sums(side, terms, more=(), waits=(), us=2):
    fields, width = terms[0].shape[1], terms[0].shape[3]
    rows = sum(item.shape[2] for item in terms[::2])
    field = pl.BlockSpec((1, rows, width), lambda n: (n, 0, 0))
    return launch(
        lambda *refs: sums_kernel(len(terms) // 2, *refs),
        None,
        [*terms, *more],
        waits,
        us,
        out_shape=jax.ShapeDtypeStruct((fields, rows, width), BF16),
        grid=(fields,),
        in_specs=[pl.BlockSpec((1, 1, item.shape[2], width), lambda n: (side, n, 0, 0)) for item in terms]
        + [field] * len(more),
        out_specs=field,
        name="core_sums",
    )


def tree_sum(terms):
    while len(terms) > 1:
        terms = [first + second for first, second in zip(terms[::2], terms[1::2])]
    return terms[0]


def reduce_kernel(body, cuts, *refs):
    in_refs, out_refs = refs[: -len(cuts)], refs[-len(cuts) :]
    extra = in_refs[0].shape[1] - body
    for (start, count, _), out in zip(cuts, out_refs):
        rows = slice(start, start + count)
        out[0, :count, :] = tree_sum([ref[0, rows, :].astype(F32) for ref in in_refs]).astype(out.dtype)
    if extra:
        small = tree_sum([ref[0, body:, :].astype(F32) for ref in in_refs]).astype(BF16)
        for (_, count, _), out in zip(cuts, out_refs):
            out[0, count:, :] = small.astype(out.dtype)


def reduce_and_cut(terms, cuts, waits=(), extra=0, us=3):
    stacks, rows, columns = terms[0].shape
    tile = min(columns, 512)
    spec = lambda count: pl.BlockSpec((1, count, tile), lambda a, b: (a, 0, b))
    return launch(
        lambda *refs: reduce_kernel(rows - extra, cuts, *refs),
        None,
        terms,
        waits,
        us,
        out_shape=[jax.ShapeDtypeStruct((stacks, count + extra, columns), dtype) for _, count, dtype in cuts],
        grid=(stacks, columns // tile),
        in_specs=[spec(rows)] * len(terms),
        out_specs=[spec(count + extra) for _, count, _ in cuts],
        name="reduce_and_cut",
    )


def scatter(stack):
    return [stack[0]] + [swap(piece, "fsdp", j) for j, piece in enumerate(stack) if j > 0]


def close_kernel(source, core_ref, x_ref, g_ref, mine_ref, other_ref, shift_ref, out_ref, grad_ref):
    core, _ = source(pl.program_id(0))
    values = x_ref[...].astype(F32)
    normal, spread = normal_of(values)
    total, slope = (
        jnp.where(core == core_ref[0], mine_ref[field].astype(F32), other_ref[field].astype(F32)) for field in range(2)
    )
    out_ref[...] = (values + total + shift_ref[...]).astype(BF16)
    slope_mean = jnp.mean(slope, axis=-1, keepdims=True)
    slope_dot = jnp.mean(slope * normal, axis=-1, keepdims=True)
    grad_ref[...] = (g_ref[...].astype(F32) + spread * (slope - slope_mean - normal * slope_dot)).astype(BF16)


def close(core, x, g, mine, other, shift, first_rows, waits=()):
    tokens, width = x.shape
    block = math.gcd(math.gcd(first_rows // 2, (tokens - first_rows) // 2), 128)
    first, rest = first_rows // (2 * block), (tokens - first_rows) // (2 * block)

    def source(m):
        late = m >= 2 * first
        local = m - jnp.where(late, 2 * first, 0)
        count = jnp.where(late, rest, first)
        core = jnp.where(local >= count, 1, 0)
        return core, local - core * count + jnp.where(late, first, 0)

    row_spec = pl.BlockSpec((block, width), lambda m, *_: (m, 0))
    total_spec = pl.BlockSpec((2, block, width), lambda m, *_: (0, source(m)[1], 0))
    return launch(
        lambda *refs: close_kernel(source, *refs),
        core,
        [x, g, mine, other, shift],
        waits,
        3,
        out_shape=[jax.ShapeDtypeStruct((tokens, width), BF16)] * 2,
        grid=(tokens // block,),
        in_specs=[row_spec, row_spec, total_spec, total_spec, pl.BlockSpec((1, width), lambda m, *_: (0, 0))],
        out_specs=[row_spec] * 2,
        name="close",
    )


def ranks_of(order, offsets):
    sources = lax.axis_index("ctx") ^ jnp.array(offsets, dtype=jnp.int32)
    match = sources[:, None] == jnp.arange(order.shape[1], dtype=jnp.int32)[None, :]
    return jnp.sum(jnp.where(match, order[:, None, :], 0), axis=-1)


def exchange_attention(local, remote, order, table, block_rows, waits):
    shape = (2, order.shape[0], block_rows, 4 * LANES)
    ranks = ranks_of(order, range(4)).reshape(-1)
    outs = attend(ranks, table, [local.reshape(shape), remote.reshape(shape)], waits)
    mine, theirs = (out.reshape(local.shape) for out in outs)
    return mine, swap(theirs, "ctx", 2)


def gathered_attention(local, remote, order, table, block_rows, waits):
    groups, micro = 2, order.shape[0]
    ctx = lax.axis_size("ctx")
    heads = groups * LANES // HD
    scale = HD ** (-0.5)
    packed = jnp.stack([local, remote]).reshape(groups, 2, micro, block_rows, 4 * LANES)
    packed = jnp.transpose(packed, (0, 2, 1, 3, 4))
    ranks = ranks_of(order, range(ctx))

    def split(array):
        array = array.reshape(groups, 2 * block_rows, LANES // HD, HD)
        return jnp.transpose(array, (1, 0, 2, 3)).reshape(2 * block_rows, heads, HD)

    def join(array):
        return jnp.transpose(array.reshape(2, block_rows, groups, LANES), (2, 0, 1, 3))

    def everywhere(array):
        return jnp.stack([array] + [swap(array, "ctx", j) for j in range(2, ctx, 2)])

    def home(array):
        total = array[0].astype(F32)
        for j in range(2, ctx, 2):
            total = total + swap(array[j // 2], "ctx", j).astype(F32)
        return total

    results = []
    for m in range(micro):
        parted = packed[:, m].reshape(groups, 2 * block_rows, 4, LANES)
        queries, keys, values, douts = (split(parted[:, :, i]) for i in range(4))
        all_keys, all_values = everywhere(keys), everywhere(values)
        key_ranks = jnp.repeat(ranks[m].reshape(-1, 2), block_rows, axis=1)
        query_ranks = key_ranks[0]
        allowed = (key_ranks[:, None, :] <= query_ranks[None, :, None])[:, None]

        def peak_step(state, item):
            key, value, ok = item
            peak, total, sums = state
            scores = jnp.einsum("bhe,rhe->hbr", queries, key, preferred_element_type=F32) * scale
            scores = jnp.where(ok, scores, -1e30)
            new = jnp.maximum(peak, jnp.max(scores, axis=-1))
            weights = jnp.where(ok, jnp.exp(scores - new[..., None]), 0.0)
            fade = jnp.exp(peak - new)
            part = jnp.einsum("hbr,rhe->hbe", weights.astype(BF16), value, preferred_element_type=F32)
            return (new, total * fade + jnp.sum(weights, axis=-1), sums * fade[..., None] + part), None

        start = (
            jnp.full((heads, 2 * block_rows), -1e30, F32),
            jnp.zeros((heads, 2 * block_rows), F32),
            jnp.zeros((heads, 2 * block_rows, HD), F32),
        )
        (peak, total, sums), _ = lax.scan(peak_step, start, (all_keys, all_values, allowed))
        attended = jnp.transpose(sums / total[..., None], (1, 0, 2))
        level = peak + jnp.log(total)
        delta = jnp.transpose(jnp.sum(douts.astype(F32) * attended, axis=-1))

        def back_step(query_sum, item):
            key, value, ok = item
            scores = jnp.einsum("bhe,rhe->hbr", queries, key, preferred_element_type=F32) * scale
            weights = jnp.where(ok, jnp.exp(scores - level[..., None]), 0.0)
            value_grad = jnp.einsum("hbr,bhe->rhe", weights.astype(BF16), douts, preferred_element_type=F32)
            slope = jnp.einsum("bhe,rhe->hbr", douts, value, preferred_element_type=F32)
            slope = (weights * (slope - delta[..., None])).astype(BF16)
            query_part = jnp.einsum("hbr,rhe->bhe", slope, key, preferred_element_type=F32) * scale
            key_grad = jnp.einsum("hbr,bhe->rhe", slope, queries, preferred_element_type=F32) * scale
            return query_sum + query_part, (key_grad.astype(BF16), value_grad.astype(BF16))

        query_grad, (key_grads, value_grads) = lax.scan(
            back_step, jnp.zeros(queries.shape, F32), (all_keys, all_values, allowed)
        )
        rows = [
            lax.dynamic_slice(table, (0, ranks[m, side] * block_rows, 0), (2, block_rows, LANES)) for side in range(2)
        ]
        rows = jnp.concatenate(rows, axis=1)

        def unturn(array):
            half = ROT // 2
            cosine, sine = rows[0, :, :half][:, None], rows[1, :, half:ROT][:, None]
            first, second = array[..., :half], array[..., half:ROT]
            return jnp.concatenate(
                [first * cosine + second * sine, second * cosine - first * sine, array[..., ROT:]], axis=-1
            )

        fields = (unturn(query_grad), unturn(home(key_grads)), home(value_grads), attended)
        results.append(jnp.concatenate([join(field.astype(BF16)) for field in fields], axis=-1))
    results = jnp.transpose(jnp.stack(results, axis=1), (0, 2, 1, 3, 4))
    mine, theirs = results.reshape(groups, *local.shape)
    return mine, theirs


def rotation_table(length):
    lane = jnp.arange(LANES, dtype=jnp.int32) % HD
    halves = ROT // 2
    frequency = jnp.exp((lane % halves).astype(F32) * (-2.0 * math.log(10000.0) / ROT))
    frequency = jnp.where(lane < ROT, frequency, 0.0)
    angles = jnp.arange(length, dtype=F32)[:, None] * frequency
    return jnp.stack([jnp.cos(angles), jnp.where(lane < halves, -1.0, 1.0) * jnp.sin(angles)])


def local(
    inputs,
    block_order,
    first_gain,
    first_shift,
    second_gain,
    second_shift,
    qkv_weight,
    qkv_bias,
    out_weight,
    out_bias,
    up_weight,
    up_bias,
    down_weight,
    down_bias,
    out_grad,
):
    micro, block_rows, _, width = inputs.shape
    ctx = lax.axis_size("ctx")
    f, z, core = lax.axis_index("fsdp"), lax.axis_index("ctx"), lax.axis_index("tp")
    low = z & 1
    rows = up_weight.shape[0]
    groups, hidden = 2, up_weight.shape[1] // 2
    tokens = micro * block_rows
    order = block_order[:, 0]
    first_part = micro - 1
    parts = ((0, first_part), (first_part, micro))
    exchanging = ctx == 2 * groups

    fields = [qkv_weight[0], qkv_weight[1], qkv_weight[2], jnp.transpose(out_weight)]
    extent = groups * LANES
    halves = [jnp.concatenate([field[:, i * extent : (i + 1) * extent] for field in fields], axis=1) for i in range(2)]
    shard = jnp.stack(halves)

    x, g = inputs.reshape(tokens, width), out_grad.reshape(tokens, width)
    fields = [up_weight, jnp.transpose(down_weight)]
    halves = [jnp.concatenate([field[:, i * hidden : (i + 1) * hidden] for field in fields], axis=1) for i in range(2)]
    forward_shard, both, shard = lax.optimization_barrier((jnp.stack(halves), jnp.stack([x, g]), shard))
    column = gather_column(*choose(low, shard[0], shard[1]))
    own, other = choose(low, forward_shard[0], forward_shard[1])
    forward_pair = jnp.concatenate([own, swap(other, "ctx", 1)], axis=0)
    lanes, _ = choose(core, both[:, :, : width // 2], both[:, :, width // 2 :])
    lanes, column[1] = lax.optimization_barrier((lanes, column[1]))
    lanes = swap(lanes, "ctx", 1)
    column = jnp.concatenate(column, axis=0)
    pieces = gather_pieces(column)

    table = rotation_table(ctx * block_rows)
    index = jnp.stack([f * ctx + z, core]).astype(jnp.int32)
    gains = jnp.stack([first_gain, first_shift, second_gain, second_shift]).astype(F32)
    prepared, grad_sum = prepare_own(
        index, x, g, gains, rows, block_rows, (column, forward_pair, table)
    )
    forward_column = [forward_pair] + [swap(forward_pair, "ctx", j) for j in range(2, ctx, 2)]
    lanes, grad_sum, *pieces = lax.optimization_barrier((lanes, grad_sum, *pieces))
    arrived = (lanes, swap(lanes, "tp", 1))
    x_both, g_both, one = prepare_pair(
        index, arrived, gains, prepared, rows, block_rows, first_part
    )

    place = ((z >> 1) if exchanging else jnp.zeros_like(z)).astype(jnp.int32).reshape(1)
    bias = qkv_bias.astype(F32)
    bias = choose(low, bias[:, :extent], bias[:, extent:])[0].reshape(1, -1)
    attention = exchange_attention if exchanging else gathered_attention
    send = (lambda item: swap(item, "ctx", 2)) if exchanging else (lambda item: item)
    packed, first_block = [], 0
    for begin, end in parts:
        ranks = jnp.transpose(ranks_of(order[begin:end], (0, 1))).reshape(-1)
        count = 2 * (end - begin)
        waits = [forward_column] if packed else []
        mine, other = project(
            place, ranks, one, g_both, first_block, count, table, bias, pieces, block_rows, waits
        )
        if not packed:
            forward_column[0], mine = lax.optimization_barrier((forward_column[0], mine))
            forward_column = jnp.concatenate(forward_column, axis=0)
            forward_pieces = gather_pieces(forward_column)
        packed.append((first_block * block_rows, mine, other))
        first_block += count

    two, one_t, two_t, g_t = prepare_late(index, x_both, g_both, one, gains, rows, block_rows, (packed[1][1],))
    up_shift = up_bias.astype(F32).reshape(2, 1, hidden)
    up_shift = choose(low, up_shift[0], up_shift[1])[0]
    arrivals = [send(theirs) for _, _, theirs in packed]
    returned = [attention(packed[0][1], arrivals[0], order[: parts[0][1]], table, block_rows, (g_t,))]
    branch, slope, up_sum, forward_grads = feed_forward(
        two, g_both, two_t, g_t, up_shift, forward_pieces, (returned[0][0],)
    )
    returned.append(attention(packed[1][1], arrivals[1], order[parts[1][0] :], table, block_rows, (up_sum,)))

    scalars = jnp.stack([f * ctx + z, place[0], low, core]).astype(jnp.int32)
    end_shift = (out_bias.astype(F32) + down_bias.astype(F32)).reshape(1, width)
    forward_terms = scatter(forward_grads)
    pairs = range(2, ctx, 2)

    def finish_part(number, small, waits):
        first, (local, remote) = packed[number][0], returned[number]
        mine, theirs, small = finish(
            scalars, x_both, gains, branch, slope, first, local, remote, small, pieces, rows, waits
        )
        return (mine, swap(theirs, "tp", 1)), small

    def weights_part(number, before, waits):
        first, (local, remote) = packed[number][0], returned[number]
        return attention_weights(place, one_t, g_t, first, local, remote, before, len(pieces), waits)

    zero = jnp.zeros((1, width), F32)
    small = jnp.concatenate([zero] * 4 + [grad_sum, zero, zero, *choose(low, up_sum, zero)] + [zero] * (SMALL_ROWS - 9))
    made = {}

    def run(task, wait):
        if task == "finish_a":
            made["a"], made["small"] = finish_part(0, small, (wait,))
            return made["small"]
        if task == "weights_a":
            made["grads_a"] = weights_part(0, None, (wait,))
            return made["grads_a"]
        if task == "forward_first":
            keep, *send = reduce_and_cut(
                forward_terms, [(0, 2 * rows, F32)] + [(j * rows, 2 * rows, BF16) for j in pairs], (wait,)
            )
            made["forward"] = [keep] + [swap(item, "ctx", j) for j, item in zip(pairs, send)]
            return keep
        if task == "finish_b":
            made["b"], made["small"] = finish_part(1, made["small"], (wait,))
            return made["small"]
        if task == "weights_b":
            grads = weights_part(1, (made["grads_a"], made["small"]), (wait,))
            made["attention"] = scatter(grads)
            return grads[0]
        if task == "forward_second":
            made["mine"], made["send"] = reduce_and_cut(
                made["forward"], [(0, rows, F32), (rows, rows, BF16)], (wait,)
            )
            return made["mine"]
        if task == "attention_first":
            made["keep"], *send = reduce_and_cut(
                made["attention"],
                [(0, rows, F32)] + [(j * rows, rows, BF16) for j in range(1, ctx)],
                (wait,),
                SMALL_ROWS,
            )
            made["sent"] = [swap(item, "ctx", j) for j, item in enumerate(send, 1)]
            return made["keep"]
        if task == "sums":
            sums = core_sums(1, [*made["a"], *made["b"]], (), (wait,))
            made["pair"] = swap(sums, "ctx", 1)
            return sums
        if task == "totals":
            totals = core_sums(0, [*made["a"], *made["b"]], [made["pair"]], (wait, *made["sent"]))
            made["totals"] = (totals, swap(totals, "tp", 1))
            return totals
        core_place = core.astype(jnp.int32).reshape(1)
        made["results"] = close(core_place, x, g, *made["totals"], end_shift, packed[1][0] // 2, (wait,))
        return made["results"][0]

    wait = returned[1][0]
    for task in TASKS:
        wait = run(task, wait)
    forward_mine, forward_send, attention_keep, results = (made[key] for key in ("mine", "send", "keep", "results"))
    attention_got = made["sent"]
    forward_got, done = lax.optimization_barrier((swap(forward_send, "ctx", 1), results[0]))
    results = [done, results[1]]
    outputs, input_grad = (item.reshape(inputs.shape) for item in results)
    forward_sums = choose(low, forward_mine, forward_got.astype(F32))
    up_sums = jnp.concatenate([half[0] for half in forward_sums], axis=1)
    down_sums = jnp.concatenate([jnp.transpose(half[1]) for half in forward_sums], axis=0)

    terms = [attention_keep[0]] + [got[0].astype(F32) for got in attention_got]
    halves = choose(low, tree_sum([term[:rows] for term in terms[::2]]), tree_sum([term[:rows] for term in terms[1::2]]))
    small = tree_sum([term[rows:] for term in terms])
    fields = [
        jnp.concatenate([half[:, i * extent : (i + 1) * extent] for half in halves], axis=1) for i in range(4)
    ]
    norm_sums = small[:4] + swap(small[:4], "tp", 1)
    pre_sums = small[5:7, : 3 * extent].reshape(2, 3, extent)
    return (
        outputs,
        input_grad,
        norm_sums[0],
        norm_sums[1],
        norm_sums[2],
        norm_sums[3],
        jnp.stack(fields[:3]),
        jnp.concatenate([pre_sums[0], pre_sums[1]], axis=1),
        jnp.transpose(fields[3]),
        small[4],
        up_sums,
        small[7:9].reshape(-1),
        down_sums,
        small[4],
    )


def solution(mesh):
    placed = (
        P(None, "ctx", "fsdp", None),
        P(None, "fsdp", None),
        P(),
        P(),
        P(),
        P(),
        P(None, ("fsdp", "ctx"), "tp"),
        P(None, "tp"),
        P("tp", ("fsdp", "ctx")),
        P(),
        P(("fsdp", "ctx"), "tp"),
        P("tp"),
        P("tp", ("fsdp", "ctx")),
        P(),
        P(None, "ctx", "fsdp", None),
    )
    return jax.shard_map(
        local,
        mesh=mesh,
        in_specs=placed,
        out_specs=(
            P(None, "ctx", "fsdp", None),
            P(None, "ctx", "fsdp", None),
            P(),
            P(),
            P(),
            P(),
            P(None, ("fsdp", "ctx"), "tp"),
            P(None, "tp"),
            P("tp", ("fsdp", "ctx")),
            P(),
            P(("fsdp", "ctx"), "tp"),
            P("tp"),
            P("tp", ("fsdp", "ctx")),
            P(),
        ),
        check_vma=False,
    )
```

```python
import math

import jax
import jax.numpy as jnp
from jax import lax
from jax.experimental import pallas as pl
from jax.experimental.pallas import tpu as pltpu
from jax.sharding import PartitionSpec as P

HD = 64
ROT = 16
LANES = 128
F32 = jnp.float32
BF16 = jnp.bfloat16
MIB = 1024 * 1024
EPSILON = 1e-05
TASKS = (
    "finish_a",
    "weights_a",
    "forward_first",
    "finish_b",
    "weights_b",
    "sums",
    "forward_second",
    "attention_first",
    "totals",
    "close",
)
SMALL_ROWS = 16
SHARE = 1 / 0.6


def swap(value, axis, bit):
    size = lax.axis_size(axis)
    return lax.ppermute(value, axis, [(i, i ^ bit) for i in range(size)])


def choose(bit, first, second):
    return jnp.where(bit == 0, first, second), jnp.where(bit == 0, second, first)


def gather_column(own, other):
    return [own] + [swap(other if j & 1 else own, "ctx", j) for j in range(1, lax.axis_size("ctx"))]


def gather_pieces(column):
    return [column] + [swap(column, "fsdp", j) for j in range(1, lax.axis_size("fsdp"))]


def launch(kernel, scalars, operands, waits, us, *, grid, in_specs, out_specs, out_shape, scratch_shapes=(), mib=24, **more):
    count = (scalars is not None) + len(operands)

    def body(*refs):
        kernel(*refs[:count], *refs[count + len(waits) :])

    return pl.pallas_call(
        body,
        out_shape=out_shape,
        grid_spec=pltpu.PrefetchScalarGridSpec(
            num_scalar_prefetch=0 if scalars is None else 1,
            grid=grid,
            in_specs=[*in_specs] + [pl.BlockSpec(memory_space=pl.ANY)] * len(waits),
            out_specs=out_specs,
            scratch_shapes=scratch_shapes,
        ),
        compiler_params=pltpu.CompilerParams(vmem_limit_bytes=mib * MIB),
        cost_estimate=pl.CostEstimate(flops=int(us * SHARE * 1.1e9), bytes_accessed=1024, transcendentals=0),
        **more,
    )(*([] if scalars is None else [scalars]), *operands, *waits)


def matmul(lhs, rhs):
    return jnp.dot(lhs, rhs, preferred_element_type=F32)


def against(lhs, rhs):
    return lax.dot_general(lhs, rhs, (((1,), (1,)), ((), ())), preferred_element_type=F32)


def exchanged(load, width, index, rows):
    shift = index * rows
    high, low = shift // LANES, lax.rem(shift, LANES)
    blocks = []
    for block in range(width // LANES):
        start = pl.multiple_of((block ^ high) * LANES, LANES)
        value = load(pl.ds(start, LANES)).astype(F32)
        step = rows
        while step < LANES:
            lane = lax.broadcasted_iota(jnp.int32, value.shape, 1)
            turned = pltpu.roll(value, step, 1)
            if 2 * step != LANES:
                turned = jnp.where((lane & step) != 0, turned, pltpu.roll(value, LANES - step, 1))
            value = jnp.where((low & step) != 0, turned, value)
            step *= 2
        blocks.append(value)
    return jnp.concatenate(blocks, axis=1)


def normal_of(values):
    centre = jnp.mean(values, axis=-1, keepdims=True)
    offset = values - centre
    spread = lax.rsqrt(jnp.mean(offset * offset, axis=-1, keepdims=True) + EPSILON)
    return offset * spread, spread


def prepare_block(rows, index, load_x, load_g, gains_ref, outs):
    x_out, g_out, one_out = outs
    width = x_out.shape[1]
    values = exchanged(load_x, width, index, rows)
    gains = exchanged(lambda lanes: gains_ref[:, lanes], width, index, rows)
    normal, _ = normal_of(values)
    x_out[...] = values.astype(BF16)
    g_out[...] = exchanged(load_g, width, index, rows).astype(BF16)
    one_out[...] = (normal * gains[0:1] + gains[1:2]).astype(BF16)


def prepare_own_kernel(rows, index_ref, x_ref, g_ref, gains_ref, *refs):
    outs, sum_out = refs[:3], refs[3]
    prepare_block(rows, index_ref[0], lambda lanes: x_ref[:, lanes], lambda lanes: g_ref[:, lanes], gains_ref, outs)

    @pl.when(pl.program_id(0) == 0)
    def _():
        sum_out[...] = jnp.zeros_like(sum_out)

    sum_out[...] += jnp.sum(g_ref[...].astype(F32), axis=0, keepdims=True)


def prepare_pair_kernel(rows, count, index_ref, mine_ref, other_ref, gains_ref, *refs):
    half = mine_ref.shape[2]

    def loader(field):
        def load(lanes):
            inside = pl.ds(pl.multiple_of(lax.rem(lanes.start, half), LANES), lanes.size)
            mine, other = mine_ref[field, :, inside].astype(F32), other_ref[field, :, inside].astype(F32)
            return jnp.where(lanes.start // half == index_ref[1], mine, other)

        return load

    own_refs, out_refs = refs[:3], refs[3:]
    step = pl.program_id(0)

    @pl.when(step < count)
    def _():
        for own, out in zip(own_refs, out_refs):
            out[...] = own[...]

    @pl.when(step >= count)
    def _():
        prepare_block(rows, index_ref[0], loader(0), loader(1), gains_ref, out_refs)


def prepare_late_kernel(rows, index_ref, x_ref, g_ref, one_ref, gains_ref, two_out, one_t, two_t, g_t):
    normal, _ = normal_of(x_ref[...].astype(F32))
    gains = exchanged(lambda lanes: gains_ref[:, lanes], x_ref.shape[1], index_ref[0], rows)
    two = (normal * gains[2:3] + gains[3:4]).astype(BF16)
    two_out[...] = two
    one_t[...] = one_ref[...].T
    two_t[...] = two.T
    g_t[...] = g_ref[...].T


def prepare_own(index, x, g, gains, rows, block_rows, waits=()):
    tokens, width = x.shape
    row_spec = pl.BlockSpec((block_rows, width), lambda m, *_: (m, 0))
    *outs, grad_sum = launch(
        lambda *refs: prepare_own_kernel(rows, *refs),
        index,
        [x, g, gains],
        waits,
        2.100,
        out_shape=[jax.ShapeDtypeStruct((tokens, width), BF16)] * 3 + [jax.ShapeDtypeStruct((1, width), F32)],
        grid=(tokens // block_rows,),
        in_specs=[row_spec, row_spec, pl.BlockSpec(gains.shape, lambda m, *_: (0, 0))],
        out_specs=[row_spec] * 3 + [pl.BlockSpec((1, width), lambda m, *_: (0, 0))],
        name="prepare_own",
    )
    return outs, grad_sum


def prepare_pair(index, arrived, gains, own, rows, block_rows, first_part, waits=()):
    _, tokens, half = arrived[0].shape
    width = 2 * half
    count = tokens // block_rows

    def place(step):
        m, side = lax.rem(step, count), step // count
        return m + jnp.where(m < first_part, side * first_part, first_part + side * (count - first_part))

    half_spec = pl.BlockSpec((2, block_rows, half), lambda m, *_: (0, jnp.maximum(m - count, 0), 0))
    own_spec = pl.BlockSpec((block_rows, width), lambda m, *_: (jnp.minimum(m, count - 1), 0))
    return launch(
        lambda *refs: prepare_pair_kernel(rows, count, *refs),
        index,
        [*arrived, gains, *own],
        waits,
        2.100,
        out_shape=[jax.ShapeDtypeStruct((2 * tokens, width), BF16)] * 3,
        grid=(2 * count,),
        in_specs=[half_spec, half_spec, pl.BlockSpec(gains.shape, lambda m, *_: (0, 0))] + [own_spec] * 3,
        out_specs=[pl.BlockSpec((block_rows, width), lambda m, *_: (place(m), 0))] * 3,
        name="prepare_pair",
    )


def prepare_late(index, x, g, one, gains, rows, block_rows, waits=()):
    tokens, width = x.shape
    row_spec = pl.BlockSpec((block_rows, width), lambda m, *_: (m, 0))
    column_spec = pl.BlockSpec((width, block_rows), lambda m, *_: (0, m))
    plain, turned = jax.ShapeDtypeStruct((tokens, width), BF16), jax.ShapeDtypeStruct((width, tokens), BF16)
    return launch(
        lambda *refs: prepare_late_kernel(rows, *refs),
        index,
        [x, g, one, gains],
        waits,
        3.600,
        out_shape=[plain, turned, turned, turned],
        grid=(tokens // block_rows,),
        in_specs=[row_spec, row_spec, row_spec, pl.BlockSpec(gains.shape, lambda m, *_: (0, 0))],
        out_specs=[row_spec, column_spec, column_spec, column_spec],
        name="prepare_late",
        mib=24,
    )


def turn(values, cosine, sine):
    lane = lax.broadcasted_iota(jnp.int32, values.shape, 1) % HD
    ahead = pltpu.roll(values, LANES - ROT // 2, 1)
    behind = pltpu.roll(values, ROT // 2, 1)
    return values * cosine + jnp.where(lane < ROT // 2, ahead, behind) * sine


def gather_weight(piece_refs, weight_s):
    @pl.when(pl.program_id(0) == 0)
    def _():
        start = 0
        for ref in piece_refs:
            weight_s[start : start + ref.shape[0], :] = ref[...]
            start += ref.shape[0]


def pick(place, first, second):
    return jnp.where(place == 0, first, second), jnp.where(place == 0, second, first)


def project_kernel(fsdp, block_rows, scalar_ref, one_ref, g_ref, table_ref, bias_ref, *refs):
    piece_refs, (local_ref, remote_ref, weight_s) = refs[:fsdp], refs[fsdp:]
    tokens, width = one_ref.shape
    gather_weight(piece_refs, weight_s)
    pre = matmul(one_ref[...], weight_s[:, : 6 * LANES]) + bias_ref[...]
    back = matmul(g_ref[...], weight_s[:, 6 * LANES :])
    for block in range(tokens // block_rows):
        rows = slice(block * block_rows, (block + 1) * block_rows)
        rank = scalar_ref[1 + pl.program_id(0) * (tokens // block_rows) + block]
        places = pl.ds(pl.multiple_of(rank * block_rows, block_rows), block_rows)
        cosine, sine = table_ref[0, places, :], table_ref[1, places, :]
        for field in range(4):
            source = pre[rows] if field < 3 else back[rows]
            start = 2 * field * LANES if field < 3 else 0
            both = [source[:, start + group * LANES : start + (group + 1) * LANES] for group in range(2)]
            if field < 2:
                both = [turn(item, cosine, sine) for item in both]
            here = slice(field * LANES, (field + 1) * LANES)
            mine, other = pick(scalar_ref[0], *both)
            local_ref[rows, here] = mine.astype(BF16)
            remote_ref[rows, here] = other.astype(BF16)


def project(place, ranks, one, g, first, count, table, bias, pieces, block_rows, waits=()):
    width = one.shape[1]
    fsdp = len(pieces)
    tokens = count * block_rows
    tile = 2 * block_rows
    base = first // 2
    side = pl.BlockSpec((tile, width), lambda t, *_: (base + t, 0))
    once = pl.Buffered(1)
    out = pl.BlockSpec((tile, 4 * LANES), lambda t, *_: (t, 0))
    return launch(
        lambda *refs: project_kernel(fsdp, block_rows, *refs),
        jnp.concatenate([place, ranks]),
        [one, g, table, bias, *pieces],
        waits,
        tokens / 500.000,
        out_shape=[jax.ShapeDtypeStruct((tokens, 4 * LANES), BF16)] * 2,
        grid=(tokens // tile,),
        in_specs=[
            side,
            side,
            pl.BlockSpec(table.shape, lambda t, *_: (0, 0, 0), pipeline_mode=once),
            pl.BlockSpec(bias.shape, lambda t, *_: (0, 0)),
        ]
        + [pl.BlockSpec(piece.shape, lambda t, *_: (0, 0), pipeline_mode=once) for piece in pieces],
        out_specs=[out, out],
        scratch_shapes=[pltpu.VMEM((width, 8 * LANES), BF16)],
        name="project",
        mib=28,
    )


def attend_kernel(blocks, block_rows, scale, rank_ref, table_ref, *refs):
    count = blocks // 2
    chunk_refs, out_refs = refs[:count], refs[count : 2 * count]
    q_s, k_s, v_s, d_s, kt_s, vt_s, ot_s, qt_s, dk_s, dv_s = refs[2 * count :]
    item = pl.program_id(0)

    def rows_of(index):
        return pl.ds(pl.multiple_of(rank_ref[item * blocks + index] * block_rows, block_rows), block_rows)

    for index in range(blocks):
        rows, chunk, side = rows_of(index), chunk_refs[index // 2], index % 2
        q_s[rows, :] = chunk[side, 0, :, :LANES]
        k_s[rows, :] = chunk[side, 0, :, LANES : 2 * LANES]
        v_s[rows, :] = chunk[side, 0, :, 2 * LANES : 3 * LANES]
        d_s[rows, :] = chunk[side, 0, :, 3 * LANES :]
    kt_s[...] = k_s[...].T
    vt_s[...] = v_s[...].T
    lane = lax.broadcasted_iota(jnp.int32, (block_rows, LANES), 1)
    dk_s[...] = jnp.zeros_like(dk_s)
    dv_s[...] = jnp.zeros_like(dv_s)

    def head_step(head, carry):
        inside = (lane // HD) == head
        heads = pl.ds(pl.multiple_of(head * HD, HD), HD)
        for rank in range(blocks):
            rows = slice(rank * block_rows, (rank + 1) * block_rows)
            keys = slice(0, (rank + 1) * block_rows)
            q_h = jnp.where(inside, q_s[rows, :], 0).astype(BF16)
            d_h = jnp.where(inside, d_s[rows, :], 0).astype(BF16)
            scores = against(k_s[keys, :], q_h) * scale
            weights = jnp.exp(scores - jnp.max(scores, axis=0, keepdims=True))
            weights = weights * (1.0 / jnp.sum(weights, axis=0, keepdims=True))
            low = weights.astype(BF16)
            ot_s[heads, rows] = matmul(vt_s[heads, keys], low)
            dv_s[keys, :] += matmul(low, d_h)
            slope = against(v_s[keys, :], d_h)
            delta = jnp.sum(weights * slope, axis=0, keepdims=True)
            slope = (weights * (slope - delta)).astype(BF16)
            qt_s[heads, rows] = matmul(kt_s[heads, keys], slope)
            dk_s[keys, :] += matmul(slope, q_h)
        return carry

    lax.fori_loop(0, LANES // HD, head_step, 0)
    for index in range(blocks):
        rows, out, side = rows_of(index), out_refs[index // 2], index % 2
        cosine, sine = table_ref[0, rows, :], -table_ref[1, rows, :]
        out[side, 0, :, :LANES] = turn(qt_s[:, rows].T * scale, cosine, sine).astype(BF16)
        out[side, 0, :, LANES : 2 * LANES] = turn(dk_s[rows, :] * scale, cosine, sine).astype(BF16)
        out[side, 0, :, 2 * LANES : 3 * LANES] = dv_s[rows, :].astype(BF16)
        out[side, 0, :, 3 * LANES :] = ot_s[:, rows].T.astype(BF16)


def attend(ranks, table, chunks, waits=()):
    sides, count, block_rows, _ = chunks[0].shape
    blocks = sides * len(chunks)
    length = blocks * block_rows
    spec = pl.BlockSpec((sides, 1, block_rows, 4 * LANES), lambda m, *_: (0, m, 0, 0))
    pairs = count * blocks * (blocks + 1) // 2 * block_rows * block_rows
    return launch(
        lambda *refs: attend_kernel(blocks, block_rows, HD ** (-0.5), *refs),
        ranks,
        [table, *chunks],
        waits,
        11 * count,
        out_shape=[jax.ShapeDtypeStruct(chunk.shape, BF16) for chunk in chunks],
        grid=(count,),
        in_specs=[pl.BlockSpec(table.shape, lambda m, *_: (0, 0, 0))] + [spec] * len(chunks),
        out_specs=[spec] * len(chunks),
        scratch_shapes=[pltpu.VMEM((length, LANES), BF16)] * 4
        + [pltpu.VMEM((LANES, length), BF16)] * 2
        + [pltpu.VMEM((LANES, length), F32)] * 2
        + [pltpu.VMEM((length, LANES), F32)] * 2,
        name="attend",
        mib=24,
    )


def forward_kernel(fsdp, two_ref, g_ref, two_t, g_t, bias_ref, *refs):
    up_refs, down_refs = refs[:fsdp], refs[fsdp : 2 * fsdp]
    branch_ref, slope_ref, sum_ref = refs[2 * fsdp : 2 * fsdp + 3]
    out_refs, (up_s, down_s) = refs[2 * fsdp + 3 : -2], refs[-2:]
    width = two_ref.shape[1]
    span = width // fsdp
    lanes = [slice(offset * span, (offset + 1) * span) for offset in range(fsdp)]
    for offset in range(fsdp):
        up_s[lanes[offset], :] = up_refs[offset][...]
        down_s[lanes[offset], :] = down_refs[offset][...]
    pre = matmul(two_ref[...], up_s[...]) + bias_ref[...]
    back = matmul(g_ref[...], down_s[...])
    gate = 0.5 * (1.0 + lax.erf(pre * math.sqrt(0.5)))
    bell = jnp.exp(-0.5 * pre * pre) * (1.0 / math.sqrt(2.0 * math.pi))
    hidden = (pre * gate).astype(BF16)
    pre_grad = (back * (gate + pre * bell)).astype(BF16)
    sum_ref[...] = jnp.sum(pre_grad.astype(F32), axis=0, keepdims=True)

    @pl.when(pl.program_id(0) == 0)
    def _():
        branch_ref[...] = against(hidden, down_s[...])
        slope_ref[...] = against(pre_grad, up_s[...])

    @pl.when(pl.program_id(0) != 0)
    def _():
        branch_ref[...] += against(hidden, down_s[...])
        slope_ref[...] += against(pre_grad, up_s[...])

    for offset in range(fsdp):
        out = out_refs[offset]
        out[0] = matmul(two_t[lanes[offset], :], pre_grad).astype(out.dtype)
        out[1] = matmul(g_t[lanes[offset], :], hidden).astype(out.dtype)


def feed_forward(two, g, two_t, g_t, bias, pieces, waits=()):
    tokens, width = two.shape
    fsdp = len(pieces)
    span, hidden = pieces[0].shape[0], pieces[0].shape[1] // 2
    tile = 512
    tiles = hidden // tile
    once = pl.Buffered(1)
    whole = pl.BlockSpec((tokens, width), lambda n: (0, 0), pipeline_mode=once)
    whole_t = pl.BlockSpec((width, tokens), lambda n: (0, 0), pipeline_mode=once)
    piece = pl.BlockSpec((span, tile), lambda n: (0, n))
    later = pl.BlockSpec((span, tile), lambda n: (0, n + tiles))
    line = pl.BlockSpec((1, tile), lambda n: (0, n))
    grads = [jax.ShapeDtypeStruct((2, span, hidden), BF16 if offset else F32) for offset in range(fsdp)]
    grad = pl.BlockSpec((2, span, tile), lambda n: (0, 0, n))
    branch, slope, sums, *grads = launch(
        lambda *refs: forward_kernel(fsdp, *refs),
        None,
        [two, g, two_t, g_t, bias, *pieces, *pieces],
        waits,
        34,
        out_shape=[jax.ShapeDtypeStruct((tokens, width), F32)] * 2
        + [jax.ShapeDtypeStruct((1, hidden), F32)]
        + grads,
        grid=(tiles,),
        in_specs=[whole, whole, whole_t, whole_t, line] + [piece] * fsdp + [later] * fsdp,
        out_specs=[whole, whole, line] + [grad] * fsdp,
        scratch_shapes=[pltpu.VMEM((width, tile), BF16)] * 2,
        name="feed_forward",
        mib=60,
    )
    return branch, slope, sums, grads


def collect(place, local_ref, remote_ref, stack_s):
    for ref, group in ((local_ref, place), (remote_ref, 1 - place)):
        for field in range(4):
            here = pl.ds(pl.multiple_of((2 * field + group) * LANES, LANES), LANES)
            stack_s[:, here] = ref[:, field * LANES : (field + 1) * LANES]


def weights_kernel(fsdp, last, place_ref, one_t, g_t, local_ref, remote_ref, *refs):
    before_ref, small_ref = refs[:2] if last else (None, None)
    out_refs, stack_s = refs[2 if last else 0 : -1], refs[-1]
    step = pl.program_id(0)
    span = one_t.shape[0]

    @pl.when(step == 0)
    def _():
        collect(place_ref[0], local_ref, remote_ref, stack_s)

    pre_part = matmul(one_t[...], stack_s[:, : 6 * LANES])
    out_part = matmul(g_t[...], stack_s[:, 6 * LANES :])
    if not last:
        out_refs[0][0, :, : 6 * LANES] = pre_part
        out_refs[0][0, :, 6 * LANES :] = out_part
    else:
        pre_part = pre_part + before_ref[0, :, : 6 * LANES]
        out_part = out_part + before_ref[0, :, 6 * LANES :]
        small = small_ref[...].astype(BF16)
        for offset in range(fsdp):

            @pl.when(step == offset)
            def _():
                out = out_refs[offset]
                out[0, :span, : 6 * LANES] = pre_part.astype(out.dtype)
                out[0, :span, 6 * LANES :] = out_part.astype(out.dtype)
                out[0, span:, :] = small.astype(out.dtype)


def attention_weights(place, one_t, g_t, first, local, remote, before, fsdp, waits=()):
    width = one_t.shape[0]
    tokens = local.shape[0]
    span = width // fsdp
    columns = 8 * LANES
    last = before is not None
    stack = jax.ShapeDtypeStruct((fsdp, span, columns), F32)
    grads = [
        jax.ShapeDtypeStruct((1, span + SMALL_ROWS, columns), BF16 if offset else F32) for offset in range(fsdp)
    ]
    piece = pl.BlockSpec((span, tokens), lambda o, *_: (o, first // tokens))
    slab = pl.BlockSpec((1, span, columns), lambda o, *_: (o, 0, 0))
    whole = lambda item: pl.BlockSpec(item.shape, lambda o, *_: (0,) * len(item.shape))
    grads = launch(
        lambda *refs: weights_kernel(fsdp, last, *refs),
        place,
        [one_t, g_t, local, remote, *(before if last else [])],
        waits,
        7 if last else 0.5,
        out_shape=grads if last else [stack],
        grid=(fsdp,),
        in_specs=[piece, piece, whole(local), whole(remote)] + ([slab, whole(before[1])] if last else []),
        out_specs=[whole(item) for item in grads] if last else [slab],
        scratch_shapes=[pltpu.VMEM((tokens, columns), BF16)],
        name="attention_weights",
    )
    return list(grads) if last else grads[0]


def finish_kernel(fsdp, rows, scalar_ref, x_ref, gains_ref, branch_ref, slope_ref, local_ref, remote_ref, before_ref, *refs):
    piece_refs, (mine_ref, theirs_ref, small_ref, stack_s, one_s, branch_s, out_s, norm_s) = refs[:fsdp], refs[fsdp:]
    half, width = x_ref.shape
    span = width // fsdp
    step = pl.program_id(0)
    index = scalar_ref[0]
    gains = exchanged(lambda item: gains_ref[:, item], width, index, rows)

    @pl.when(step == 0)
    def _():
        norm_s[...] = jnp.zeros_like(norm_s)
        collect(scalar_ref[1], local_ref, remote_ref, stack_s)
        for offset in range(fsdp):
            lanes = slice(offset * span, (offset + 1) * span)
            one_s[:, lanes] = against(stack_s[:, : 6 * LANES], piece_refs[offset][:, : 6 * LANES])
            branch_s[:, lanes] = against(stack_s[:, 6 * LANES :], piece_refs[offset][:, 6 * LANES :])

    here = pl.ds(pl.multiple_of((2 * lax.rem(step, 2) + ((step // 2) ^ scalar_ref[3])) * half, half), half)
    one, two = one_s[here, :], slope_ref[...]
    normal, _ = normal_of(x_ref[...].astype(F32))
    norm_s[0:1, :] += jnp.sum(one * normal, axis=0, keepdims=True)
    norm_s[1:2, :] += jnp.sum(one, axis=0, keepdims=True)
    norm_s[2:3, :] += jnp.sum(two * normal, axis=0, keepdims=True)
    norm_s[3:4, :] += jnp.sum(two, axis=0, keepdims=True)
    plain = []
    for value in (branch_ref[...] + branch_s[here, :], one * gains[0:1] + two * gains[2:3]):
        out_s[...] = value
        plain.append(exchanged(lambda item: out_s[:, item], width, index, rows).astype(BF16))

    for which, ref in enumerate((mine_ref, theirs_ref)):

        @pl.when(step // 2 == which)
        def _():
            ref[0, 0], ref[0, 1] = plain

    @pl.when(step == 3)
    def _():
        small_ref[...] = before_ref[...]
        small_ref[0:4, :] += exchanged(lambda item: norm_s[0:4, item], width, index, rows)
        small_ref[pl.ds(5 + scalar_ref[2], 1), : 6 * LANES] += jnp.sum(
            stack_s[:, : 6 * LANES].astype(F32), axis=0, keepdims=True
        )


def finish(scalars, x, gains, branch, slope, first, local, remote, small, pieces, rows, waits=()):
    width = x.shape[1]
    fsdp = len(pieces)
    half = local.shape[0] // 4
    base = first // half
    once = pl.Buffered(1)
    fixed = lambda item: pl.BlockSpec(item.shape, lambda t, *_: (0, 0))
    place = lambda t, scalars: 2 * lax.rem(t, 2) + ((t // 2) ^ scalars[3])
    row_spec = pl.BlockSpec((half, width), lambda t, scalars: (base + place(t, scalars), 0))
    back_spec = pl.BlockSpec(local.shape, lambda t, *_: (0, 0), pipeline_mode=once)
    mine_spec = pl.BlockSpec((1, 2, half, width), lambda t, *_: (jnp.minimum(t, 1), 0, 0, 0))
    theirs_spec = pl.BlockSpec((1, 2, half, width), lambda t, *_: (jnp.maximum(t - 2, 0), 0, 0, 0))
    sums = jax.ShapeDtypeStruct((2, 2, half, width), BF16)
    return launch(
        lambda *refs: finish_kernel(fsdp, rows, *refs),
        scalars,
        [x, gains, branch, slope, local, remote, small, *pieces],
        waits,
        half / 20 if first else 0.5,
        out_shape=[sums, sums, jax.ShapeDtypeStruct(small.shape, F32)],
        grid=(4,),
        in_specs=[row_spec, fixed(gains), row_spec, row_spec, back_spec, back_spec, fixed(small)]
        + [pl.BlockSpec(piece.shape, lambda t, *_: (0, 0), pipeline_mode=once) for piece in pieces],
        out_specs=[mine_spec, theirs_spec, fixed(small)],
        scratch_shapes=[
            pltpu.VMEM((4 * half, 8 * LANES), BF16),
            pltpu.VMEM((4 * half, width), F32),
            pltpu.VMEM((4 * half, width), F32),
            pltpu.VMEM((half, width), F32),
            pltpu.VMEM((8, width), F32),
        ],
        name="finish",
        mib=60 if first == 0 else 40,
    )


def sums_kernel(parts, *refs):
    terms, out = refs[:-1], refs[-1]
    start = 0
    for number in range(parts):
        mine, other = terms[2 * number : 2 * number + 2]
        rows = slice(start, start + mine.shape[2])
        total = mine[0, 0].astype(F32) + other[0, 0].astype(F32)
        if len(terms) > 2 * parts:
            total = total + terms[-1][0, rows, :].astype(F32)
        out[0, rows, :] = total.astype(BF16)
        start += mine.shape[2]


def core_sums(side, terms, more=(), waits=(), us=2):
    fields, width = terms[0].shape[1], terms[0].shape[3]
    rows = sum(item.shape[2] for item in terms[::2])
    field = pl.BlockSpec((1, rows, width), lambda n: (n, 0, 0))
    return launch(
        lambda *refs: sums_kernel(len(terms) // 2, *refs),
        None,
        [*terms, *more],
        waits,
        us,
        out_shape=jax.ShapeDtypeStruct((fields, rows, width), BF16),
        grid=(fields,),
        in_specs=[pl.BlockSpec((1, 1, item.shape[2], width), lambda n: (side, n, 0, 0)) for item in terms]
        + [field] * len(more),
        out_specs=field,
        name="core_sums",
    )


def tree_sum(terms):
    while len(terms) > 1:
        terms = [first + second for first, second in zip(terms[::2], terms[1::2])]
    return terms[0]


def reduce_kernel(body, cuts, *refs):
    in_refs, out_refs = refs[: -len(cuts)], refs[-len(cuts) :]
    extra = in_refs[0].shape[1] - body
    for (start, count, _), out in zip(cuts, out_refs):
        rows = slice(start, start + count)
        out[0, :count, :] = tree_sum([ref[0, rows, :].astype(F32) for ref in in_refs]).astype(out.dtype)
    if extra:
        small = tree_sum([ref[0, body:, :].astype(F32) for ref in in_refs]).astype(BF16)
        for (_, count, _), out in zip(cuts, out_refs):
            out[0, count:, :] = small.astype(out.dtype)


def reduce_and_cut(terms, cuts, waits=(), extra=0, us=3):
    stacks, rows, columns = terms[0].shape
    tile = min(columns, 512)
    spec = lambda count: pl.BlockSpec((1, count, tile), lambda a, b: (a, 0, b))
    return launch(
        lambda *refs: reduce_kernel(rows - extra, cuts, *refs),
        None,
        terms,
        waits,
        us,
        out_shape=[jax.ShapeDtypeStruct((stacks, count + extra, columns), dtype) for _, count, dtype in cuts],
        grid=(stacks, columns // tile),
        in_specs=[spec(rows)] * len(terms),
        out_specs=[spec(count + extra) for _, count, _ in cuts],
        name="reduce_and_cut",
    )


def scatter(stack):
    return [stack[0]] + [swap(piece, "fsdp", j) for j, piece in enumerate(stack) if j > 0]


def close_kernel(source, core_ref, x_ref, g_ref, mine_ref, other_ref, shift_ref, out_ref, grad_ref):
    core, _ = source(pl.program_id(0))
    values = x_ref[...].astype(F32)
    normal, spread = normal_of(values)
    total, slope = (
        jnp.where(core == core_ref[0], mine_ref[field].astype(F32), other_ref[field].astype(F32)) for field in range(2)
    )
    out_ref[...] = (values + total + shift_ref[...]).astype(BF16)
    slope_mean = jnp.mean(slope, axis=-1, keepdims=True)
    slope_dot = jnp.mean(slope * normal, axis=-1, keepdims=True)
    grad_ref[...] = (g_ref[...].astype(F32) + spread * (slope - slope_mean - normal * slope_dot)).astype(BF16)


def close(core, x, g, mine, other, shift, first_rows, waits=()):
    tokens, width = x.shape
    block = math.gcd(math.gcd(first_rows // 2, (tokens - first_rows) // 2), 128)
    first, rest = first_rows // (2 * block), (tokens - first_rows) // (2 * block)

    def source(m):
        late = m >= 2 * first
        local = m - jnp.where(late, 2 * first, 0)
        count = jnp.where(late, rest, first)
        core = jnp.where(local >= count, 1, 0)
        return core, local - core * count + jnp.where(late, first, 0)

    row_spec = pl.BlockSpec((block, width), lambda m, *_: (m, 0))
    total_spec = pl.BlockSpec((2, block, width), lambda m, *_: (0, source(m)[1], 0))
    return launch(
        lambda *refs: close_kernel(source, *refs),
        core,
        [x, g, mine, other, shift],
        waits,
        3,
        out_shape=[jax.ShapeDtypeStruct((tokens, width), BF16)] * 2,
        grid=(tokens // block,),
        in_specs=[row_spec, row_spec, total_spec, total_spec, pl.BlockSpec((1, width), lambda m, *_: (0, 0))],
        out_specs=[row_spec] * 2,
        name="close",
    )


def ranks_of(order, offsets):
    sources = lax.axis_index("ctx") ^ jnp.array(offsets, dtype=jnp.int32)
    match = sources[:, None] == jnp.arange(order.shape[1], dtype=jnp.int32)[None, :]
    return jnp.sum(jnp.where(match, order[:, None, :], 0), axis=-1)


def exchange_attention(local, remote, order, table, block_rows, waits):
    shape = (2, order.shape[0], block_rows, 4 * LANES)
    ranks = ranks_of(order, range(4)).reshape(-1)
    outs = attend(ranks, table, [local.reshape(shape), remote.reshape(shape)], waits)
    mine, theirs = (out.reshape(local.shape) for out in outs)
    return mine, swap(theirs, "ctx", 2)


def gathered_attention(local, remote, order, table, block_rows, waits):
    groups, micro = 2, order.shape[0]
    ctx = lax.axis_size("ctx")
    heads = groups * LANES // HD
    scale = HD ** (-0.5)
    packed = jnp.stack([local, remote]).reshape(groups, 2, micro, block_rows, 4 * LANES)
    packed = jnp.transpose(packed, (0, 2, 1, 3, 4))
    ranks = ranks_of(order, range(ctx))

    def split(array):
        array = array.reshape(groups, 2 * block_rows, LANES // HD, HD)
        return jnp.transpose(array, (1, 0, 2, 3)).reshape(2 * block_rows, heads, HD)

    def join(array):
        return jnp.transpose(array.reshape(2, block_rows, groups, LANES), (2, 0, 1, 3))

    def everywhere(array):
        return jnp.stack([array] + [swap(array, "ctx", j) for j in range(2, ctx, 2)])

    def home(array):
        total = array[0].astype(F32)
        for j in range(2, ctx, 2):
            total = total + swap(array[j // 2], "ctx", j).astype(F32)
        return total

    results = []
    for m in range(micro):
        parted = packed[:, m].reshape(groups, 2 * block_rows, 4, LANES)
        queries, keys, values, douts = (split(parted[:, :, i]) for i in range(4))
        all_keys, all_values = everywhere(keys), everywhere(values)
        key_ranks = jnp.repeat(ranks[m].reshape(-1, 2), block_rows, axis=1)
        query_ranks = key_ranks[0]
        allowed = (key_ranks[:, None, :] <= query_ranks[None, :, None])[:, None]

        def peak_step(state, item):
            key, value, ok = item
            peak, total, sums = state
            scores = jnp.einsum("bhe,rhe->hbr", queries, key, preferred_element_type=F32) * scale
            scores = jnp.where(ok, scores, -1e30)
            new = jnp.maximum(peak, jnp.max(scores, axis=-1))
            weights = jnp.where(ok, jnp.exp(scores - new[..., None]), 0.0)
            fade = jnp.exp(peak - new)
            part = jnp.einsum("hbr,rhe->hbe", weights.astype(BF16), value, preferred_element_type=F32)
            return (new, total * fade + jnp.sum(weights, axis=-1), sums * fade[..., None] + part), None

        start = (
            jnp.full((heads, 2 * block_rows), -1e30, F32),
            jnp.zeros((heads, 2 * block_rows), F32),
            jnp.zeros((heads, 2 * block_rows, HD), F32),
        )
        (peak, total, sums), _ = lax.scan(peak_step, start, (all_keys, all_values, allowed))
        attended = jnp.transpose(sums / total[..., None], (1, 0, 2))
        level = peak + jnp.log(total)
        delta = jnp.transpose(jnp.sum(douts.astype(F32) * attended, axis=-1))

        def back_step(query_sum, item):
            key, value, ok = item
            scores = jnp.einsum("bhe,rhe->hbr", queries, key, preferred_element_type=F32) * scale
            weights = jnp.where(ok, jnp.exp(scores - level[..., None]), 0.0)
            value_grad = jnp.einsum("hbr,bhe->rhe", weights.astype(BF16), douts, preferred_element_type=F32)
            slope = jnp.einsum("bhe,rhe->hbr", douts, value, preferred_element_type=F32)
            slope = (weights * (slope - delta[..., None])).astype(BF16)
            query_part = jnp.einsum("hbr,rhe->bhe", slope, key, preferred_element_type=F32) * scale
            key_grad = jnp.einsum("hbr,bhe->rhe", slope, queries, preferred_element_type=F32) * scale
            return query_sum + query_part, (key_grad.astype(BF16), value_grad.astype(BF16))

        query_grad, (key_grads, value_grads) = lax.scan(
            back_step, jnp.zeros(queries.shape, F32), (all_keys, all_values, allowed)
        )
        rows = [
            lax.dynamic_slice(table, (0, ranks[m, side] * block_rows, 0), (2, block_rows, LANES)) for side in range(2)
        ]
        rows = jnp.concatenate(rows, axis=1)

        def unturn(array):
            half = ROT // 2
            cosine, sine = rows[0, :, :half][:, None], rows[1, :, half:ROT][:, None]
            first, second = array[..., :half], array[..., half:ROT]
            return jnp.concatenate(
                [first * cosine + second * sine, second * cosine - first * sine, array[..., ROT:]], axis=-1
            )

        fields = (unturn(query_grad), unturn(home(key_grads)), home(value_grads), attended)
        results.append(jnp.concatenate([join(field.astype(BF16)) for field in fields], axis=-1))
    results = jnp.transpose(jnp.stack(results, axis=1), (0, 2, 1, 3, 4))
    mine, theirs = results.reshape(groups, *local.shape)
    return mine, theirs


def rotation_table(length):
    lane = jnp.arange(LANES, dtype=jnp.int32) % HD
    halves = ROT // 2
    frequency = jnp.exp((lane % halves).astype(F32) * (-2.0 * math.log(10000.0) / ROT))
    frequency = jnp.where(lane < ROT, frequency, 0.0)
    angles = jnp.arange(length, dtype=F32)[:, None] * frequency
    return jnp.stack([jnp.cos(angles), jnp.where(lane < halves, -1.0, 1.0) * jnp.sin(angles)])


def local(
    inputs,
    block_order,
    first_gain,
    first_shift,
    second_gain,
    second_shift,
    qkv_weight,
    qkv_bias,
    out_weight,
    out_bias,
    up_weight,
    up_bias,
    down_weight,
    down_bias,
    out_grad,
):
    micro, block_rows, _, width = inputs.shape
    ctx = lax.axis_size("ctx")
    f, z, core = lax.axis_index("fsdp"), lax.axis_index("ctx"), lax.axis_index("tp")
    low = z & 1
    rows = up_weight.shape[0]
    groups, hidden = 2, up_weight.shape[1] // 2
    tokens = micro * block_rows
    order = block_order[:, 0]
    first_part = micro - 1
    parts = ((0, first_part), (first_part, micro))
    exchanging = ctx == 2 * groups

    fields = [qkv_weight[0], qkv_weight[1], qkv_weight[2], jnp.transpose(out_weight)]
    extent = groups * LANES
    halves = [jnp.concatenate([field[:, i * extent : (i + 1) * extent] for field in fields], axis=1) for i in range(2)]
    shard = jnp.stack(halves)

    x, g = inputs.reshape(tokens, width), out_grad.reshape(tokens, width)
    fields = [up_weight, jnp.transpose(down_weight)]
    halves = [jnp.concatenate([field[:, i * hidden : (i + 1) * hidden] for field in fields], axis=1) for i in range(2)]
    forward_shard, both, shard = lax.optimization_barrier((jnp.stack(halves), jnp.stack([x, g]), shard))
    column = gather_column(*choose(low, shard[0], shard[1]))
    own, other = choose(low, forward_shard[0], forward_shard[1])
    forward_pair = jnp.concatenate([own, swap(other, "ctx", 1)], axis=0)
    lanes, _ = choose(core, both[:, :, : width // 2], both[:, :, width // 2 :])
    lanes, column[1] = lax.optimization_barrier((lanes, column[1]))
    lanes = swap(lanes, "ctx", 1)
    column = jnp.concatenate(column, axis=0)
    pieces = gather_pieces(column)

    table = rotation_table(ctx * block_rows)
    index = jnp.stack([f * ctx + z, core]).astype(jnp.int32)
    gains = jnp.stack([first_gain, first_shift, second_gain, second_shift]).astype(F32)
    prepared, grad_sum = prepare_own(
        index, x, g, gains, rows, block_rows, (column, forward_pair, table)
    )
    forward_column = [forward_pair] + [swap(forward_pair, "ctx", j) for j in range(2, ctx, 2)]
    lanes, grad_sum, *pieces = lax.optimization_barrier((lanes, grad_sum, *pieces))
    arrived = (lanes, swap(lanes, "tp", 1))
    x_both, g_both, one = prepare_pair(
        index, arrived, gains, prepared, rows, block_rows, first_part
    )

    place = ((z >> 1) if exchanging else jnp.zeros_like(z)).astype(jnp.int32).reshape(1)
    bias = qkv_bias.astype(F32)
    bias = choose(low, bias[:, :extent], bias[:, extent:])[0].reshape(1, -1)
    attention = exchange_attention if exchanging else gathered_attention
    send = (lambda item: swap(item, "ctx", 2)) if exchanging else (lambda item: item)
    packed, first_block = [], 0
    for begin, end in parts:
        ranks = jnp.transpose(ranks_of(order[begin:end], (0, 1))).reshape(-1)
        count = 2 * (end - begin)
        waits = [forward_column] if packed else []
        mine, other = project(
            place, ranks, one, g_both, first_block, count, table, bias, pieces, block_rows, waits
        )
        if not packed:
            forward_column[0], mine = lax.optimization_barrier((forward_column[0], mine))
            forward_column = jnp.concatenate(forward_column, axis=0)
            forward_pieces = gather_pieces(forward_column)
        packed.append((first_block * block_rows, mine, other))
        first_block += count

    two, one_t, two_t, g_t = prepare_late(index, x_both, g_both, one, gains, rows, block_rows, (packed[1][1],))
    up_shift = up_bias.astype(F32).reshape(2, 1, hidden)
    up_shift = choose(low, up_shift[0], up_shift[1])[0]
    arrivals = [send(theirs) for _, _, theirs in packed]
    returned = [attention(packed[0][1], arrivals[0], order[: parts[0][1]], table, block_rows, (g_t,))]
    branch, slope, up_sum, forward_grads = feed_forward(
        two, g_both, two_t, g_t, up_shift, forward_pieces, (returned[0][0],)
    )
    returned.append(attention(packed[1][1], arrivals[1], order[parts[1][0] :], table, block_rows, (up_sum,)))

    scalars = jnp.stack([f * ctx + z, place[0], low, core]).astype(jnp.int32)
    end_shift = (out_bias.astype(F32) + down_bias.astype(F32)).reshape(1, width)
    forward_terms = scatter(forward_grads)
    pairs = range(2, ctx, 2)

    def finish_part(number, small, waits):
        first, (local, remote) = packed[number][0], returned[number]
        mine, theirs, small = finish(
            scalars, x_both, gains, branch, slope, first, local, remote, small, pieces, rows, waits
        )
        return (mine, swap(theirs, "tp", 1)), small

    def weights_part(number, before, waits):
        first, (local, remote) = packed[number][0], returned[number]
        return attention_weights(place, one_t, g_t, first, local, remote, before, len(pieces), waits)

    zero = jnp.zeros((1, width), F32)
    small = jnp.concatenate([zero] * 4 + [grad_sum, zero, zero, *choose(low, up_sum, zero)] + [zero] * (SMALL_ROWS - 9))
    made = {}

    def run(task, wait):
        if task == "finish_a":
            made["a"], made["small"] = finish_part(0, small, (wait,))
            return made["small"]
        if task == "weights_a":
            made["grads_a"] = weights_part(0, None, (wait,))
            return made["grads_a"]
        if task == "forward_first":
            keep, *send = reduce_and_cut(
                forward_terms, [(0, 2 * rows, F32)] + [(j * rows, 2 * rows, BF16) for j in pairs], (wait,)
            )
            made["forward"] = [keep] + [swap(item, "ctx", j) for j, item in zip(pairs, send)]
            return keep
        if task == "finish_b":
            made["b"], made["small"] = finish_part(1, made["small"], (wait,))
            return made["small"]
        if task == "weights_b":
            grads = weights_part(1, (made["grads_a"], made["small"]), (wait,))
            made["attention"] = scatter(grads)
            return grads[0]
        if task == "forward_second":
            made["mine"], made["send"] = reduce_and_cut(
                made["forward"], [(0, rows, F32), (rows, rows, BF16)], (wait,)
            )
            return made["mine"]
        if task == "attention_first":
            made["keep"], *send = reduce_and_cut(
                made["attention"],
                [(0, rows, F32)] + [(j * rows, rows, BF16) for j in range(1, ctx)],
                (wait,),
                SMALL_ROWS,
            )
            made["sent"] = [swap(item, "ctx", j) for j, item in enumerate(send, 1)]
            return made["keep"]
        if task == "sums":
            sums = core_sums(1, [*made["a"], *made["b"]], (), (wait,))
            made["pair"] = swap(sums, "ctx", 1)
            return sums
        if task == "totals":
            totals = core_sums(0, [*made["a"], *made["b"]], [made["pair"]], (wait, *made["sent"]))
            made["totals"] = (totals, swap(totals, "tp", 1))
            return totals
        core_place = core.astype(jnp.int32).reshape(1)
        made["results"] = close(core_place, x, g, *made["totals"], end_shift, packed[1][0] // 2, (wait,))
        return made["results"][0]

    wait = returned[1][0]
    for task in TASKS:
        wait = run(task, wait)
    forward_mine, forward_send, attention_keep, results = (made[key] for key in ("mine", "send", "keep", "results"))
    attention_got = made["sent"]
    forward_got, done = lax.optimization_barrier((swap(forward_send, "ctx", 1), results[0]))
    results = [done, results[1]]
    outputs, input_grad = (item.reshape(inputs.shape) for item in results)
    forward_sums = choose(low, forward_mine, forward_got.astype(F32))
    up_sums = jnp.concatenate([half[0] for half in forward_sums], axis=1)
    down_sums = jnp.concatenate([jnp.transpose(half[1]) for half in forward_sums], axis=0)

    terms = [attention_keep[0]] + [got[0].astype(F32) for got in attention_got]
    halves = choose(low, tree_sum([term[:rows] for term in terms[::2]]), tree_sum([term[:rows] for term in terms[1::2]]))
    small = tree_sum([term[rows:] for term in terms])
    fields = [
        jnp.concatenate([half[:, i * extent : (i + 1) * extent] for half in halves], axis=1) for i in range(4)
    ]
    norm_sums = small[:4] + swap(small[:4], "tp", 1)
    pre_sums = small[5:7, : 3 * extent].reshape(2, 3, extent)
    return (
        outputs,
        input_grad,
        norm_sums[0],
        norm_sums[1],
        norm_sums[2],
        norm_sums[3],
        jnp.stack(fields[:3]),
        jnp.concatenate([pre_sums[0], pre_sums[1]], axis=1),
        jnp.transpose(fields[3]),
        small[4],
        up_sums,
        small[7:9].reshape(-1),
        down_sums,
        small[4],
    )


def solution(mesh):
    placed = (
        P(None, "ctx", "fsdp", None),
        P(None, "fsdp", None),
        P(),
        P(),
        P(),
        P(),
        P(None, ("fsdp", "ctx"), "tp"),
        P(None, "tp"),
        P("tp", ("fsdp", "ctx")),
        P(),
        P(("fsdp", "ctx"), "tp"),
        P("tp"),
        P("tp", ("fsdp", "ctx")),
        P(),
        P(None, "ctx", "fsdp", None),
    )
    return jax.shard_map(
        local,
        mesh=mesh,
        in_specs=placed,
        out_specs=(
            P(None, "ctx", "fsdp", None),
            P(None, "ctx", "fsdp", None),
            P(),
            P(),
            P(),
            P(),
            P(None, ("fsdp", "ctx"), "tp"),
            P(None, "tp"),
            P("tp", ("fsdp", "ctx")),
            P(),
            P(("fsdp", "ctx"), "tp"),
            P("tp"),
            P("tp", ("fsdp", "ctx")),
            P(),
        ),
        check_vma=False,
    )
```

```python
import math

import jax
import jax.numpy as jnp
from jax import lax
from jax.experimental import pallas as pl
from jax.experimental.pallas import tpu as pltpu
from jax.sharding import PartitionSpec as P

HD = 64
ROT = 16
LANES = 128
F32 = jnp.float32
BF16 = jnp.bfloat16
MIB = 1024 * 1024
EPSILON = 1e-05
TASKS = (
    "finish_a",
    "weights_a",
    "forward_first",
    "finish_b",
    "weights_b",
    "sums",
    "forward_second",
    "attention_first",
    "totals",
    "close",
)
SMALL_ROWS = 16
SHARE = 1 / 0.6


def swap(value, axis, bit):
    size = lax.axis_size(axis)
    return lax.ppermute(value, axis, [(i, i ^ bit) for i in range(size)])


def choose(bit, first, second):
    return jnp.where(bit == 0, first, second), jnp.where(bit == 0, second, first)


def gather_column(own, other):
    return [own] + [swap(other if j & 1 else own, "ctx", j) for j in range(1, lax.axis_size("ctx"))]


def gather_pieces(column):
    return [column] + [swap(column, "fsdp", j) for j in range(1, lax.axis_size("fsdp"))]


def launch(kernel, scalars, operands, waits, us, *, grid, in_specs, out_specs, out_shape, scratch_shapes=(), mib=24, **more):
    count = (scalars is not None) + len(operands)

    def body(*refs):
        kernel(*refs[:count], *refs[count + len(waits) :])

    return pl.pallas_call(
        body,
        out_shape=out_shape,
        grid_spec=pltpu.PrefetchScalarGridSpec(
            num_scalar_prefetch=0 if scalars is None else 1,
            grid=grid,
            in_specs=[*in_specs] + [pl.BlockSpec(memory_space=pl.ANY)] * len(waits),
            out_specs=out_specs,
            scratch_shapes=scratch_shapes,
        ),
        compiler_params=pltpu.CompilerParams(vmem_limit_bytes=mib * MIB),
        cost_estimate=pl.CostEstimate(flops=int(us * SHARE * 1.1e9), bytes_accessed=1024, transcendentals=0),
        **more,
    )(*([] if scalars is None else [scalars]), *operands, *waits)


def matmul(lhs, rhs):
    return jnp.dot(lhs, rhs, preferred_element_type=F32)


def against(lhs, rhs):
    return lax.dot_general(lhs, rhs, (((1,), (1,)), ((), ())), preferred_element_type=F32)


def exchanged(load, width, index, rows):
    shift = index * rows
    high, low = shift // LANES, lax.rem(shift, LANES)
    blocks = []
    for block in range(width // LANES):
        start = pl.multiple_of((block ^ high) * LANES, LANES)
        value = load(pl.ds(start, LANES)).astype(F32)
        step = rows
        while step < LANES:
            lane = lax.broadcasted_iota(jnp.int32, value.shape, 1)
            turned = pltpu.roll(value, step, 1)
            if 2 * step != LANES:
                turned = jnp.where((lane & step) != 0, turned, pltpu.roll(value, LANES - step, 1))
            value = jnp.where((low & step) != 0, turned, value)
            step *= 2
        blocks.append(value)
    return jnp.concatenate(blocks, axis=1)


def normal_of(values):
    centre = jnp.mean(values, axis=-1, keepdims=True)
    offset = values - centre
    spread = lax.rsqrt(jnp.mean(offset * offset, axis=-1, keepdims=True) + EPSILON)
    return offset * spread, spread


def prepare_block(rows, index, load_x, load_g, gains_ref, outs):
    x_out, g_out, one_out = outs
    width = x_out.shape[1]
    values = exchanged(load_x, width, index, rows)
    gains = exchanged(lambda lanes: gains_ref[:, lanes], width, index, rows)
    normal, _ = normal_of(values)
    x_out[...] = values.astype(BF16)
    g_out[...] = exchanged(load_g, width, index, rows).astype(BF16)
    one_out[...] = (normal * gains[0:1] + gains[1:2]).astype(BF16)


def prepare_own_kernel(rows, index_ref, x_ref, g_ref, gains_ref, *refs):
    outs, sum_out = refs[:3], refs[3]
    prepare_block(rows, index_ref[0], lambda lanes: x_ref[:, lanes], lambda lanes: g_ref[:, lanes], gains_ref, outs)

    @pl.when(pl.program_id(0) == 0)
    def _():
        sum_out[...] = jnp.zeros_like(sum_out)

    sum_out[...] += jnp.sum(g_ref[...].astype(F32), axis=0, keepdims=True)


def prepare_pair_kernel(rows, count, index_ref, mine_ref, other_ref, gains_ref, *refs):
    half = mine_ref.shape[2]

    def loader(field):
        def load(lanes):
            inside = pl.ds(pl.multiple_of(lax.rem(lanes.start, half), LANES), lanes.size)
            mine, other = mine_ref[field, :, inside].astype(F32), other_ref[field, :, inside].astype(F32)
            return jnp.where(lanes.start // half == index_ref[1], mine, other)

        return load

    own_refs, out_refs = refs[:3], refs[3:]
    step = pl.program_id(0)

    @pl.when(step < count)
    def _():
        for own, out in zip(own_refs, out_refs):
            out[...] = own[...]

    @pl.when(step >= count)
    def _():
        prepare_block(rows, index_ref[0], loader(0), loader(1), gains_ref, out_refs)


def prepare_late_kernel(rows, index_ref, x_ref, g_ref, one_ref, gains_ref, two_out, one_t, two_t, g_t):
    normal, _ = normal_of(x_ref[...].astype(F32))
    gains = exchanged(lambda lanes: gains_ref[:, lanes], x_ref.shape[1], index_ref[0], rows)
    two = (normal * gains[2:3] + gains[3:4]).astype(BF16)
    two_out[...] = two
    one_t[...] = one_ref[...].T
    two_t[...] = two.T
    g_t[...] = g_ref[...].T


def prepare_own(index, x, g, gains, rows, block_rows, waits=()):
    tokens, width = x.shape
    row_spec = pl.BlockSpec((block_rows, width), lambda m, *_: (m, 0))
    *outs, grad_sum = launch(
        lambda *refs: prepare_own_kernel(rows, *refs),
        index,
        [x, g, gains],
        waits,
        2.100,
        out_shape=[jax.ShapeDtypeStruct((tokens, width), BF16)] * 3 + [jax.ShapeDtypeStruct((1, width), F32)],
        grid=(tokens // block_rows,),
        in_specs=[row_spec, row_spec, pl.BlockSpec(gains.shape, lambda m, *_: (0, 0))],
        out_specs=[row_spec] * 3 + [pl.BlockSpec((1, width), lambda m, *_: (0, 0))],
        name="prepare_own",
    )
    return outs, grad_sum


def prepare_pair(index, arrived, gains, own, rows, block_rows, first_part, waits=()):
    _, tokens, half = arrived[0].shape
    width = 2 * half
    count = tokens // block_rows

    def place(step):
        m, side = lax.rem(step, count), step // count
        return m + jnp.where(m < first_part, side * first_part, first_part + side * (count - first_part))

    half_spec = pl.BlockSpec((2, block_rows, half), lambda m, *_: (0, jnp.maximum(m - count, 0), 0))
    own_spec = pl.BlockSpec((block_rows, width), lambda m, *_: (jnp.minimum(m, count - 1), 0))
    return launch(
        lambda *refs: prepare_pair_kernel(rows, count, *refs),
        index,
        [*arrived, gains, *own],
        waits,
        2.100,
        out_shape=[jax.ShapeDtypeStruct((2 * tokens, width), BF16)] * 3,
        grid=(2 * count,),
        in_specs=[half_spec, half_spec, pl.BlockSpec(gains.shape, lambda m, *_: (0, 0))] + [own_spec] * 3,
        out_specs=[pl.BlockSpec((block_rows, width), lambda m, *_: (place(m), 0))] * 3,
        name="prepare_pair",
    )


def prepare_late(index, x, g, one, gains, rows, block_rows, waits=()):
    tokens, width = x.shape
    row_spec = pl.BlockSpec((block_rows, width), lambda m, *_: (m, 0))
    column_spec = pl.BlockSpec((width, block_rows), lambda m, *_: (0, m))
    plain, turned = jax.ShapeDtypeStruct((tokens, width), BF16), jax.ShapeDtypeStruct((width, tokens), BF16)
    return launch(
        lambda *refs: prepare_late_kernel(rows, *refs),
        index,
        [x, g, one, gains],
        waits,
        3.600,
        out_shape=[plain, turned, turned, turned],
        grid=(tokens // block_rows,),
        in_specs=[row_spec, row_spec, row_spec, pl.BlockSpec(gains.shape, lambda m, *_: (0, 0))],
        out_specs=[row_spec, column_spec, column_spec, column_spec],
        name="prepare_late",
        mib=24,
    )


def turn(values, cosine, sine):
    lane = lax.broadcasted_iota(jnp.int32, values.shape, 1) % HD
    ahead = pltpu.roll(values, LANES - ROT // 2, 1)
    behind = pltpu.roll(values, ROT // 2, 1)
    return values * cosine + jnp.where(lane < ROT // 2, ahead, behind) * sine


def gather_weight(piece_refs, weight_s):
    @pl.when(pl.program_id(0) == 0)
    def _():
        start = 0
        for ref in piece_refs:
            weight_s[start : start + ref.shape[0], :] = ref[...]
            start += ref.shape[0]


def pick(place, first, second):
    return jnp.where(place == 0, first, second), jnp.where(place == 0, second, first)


def project_kernel(fsdp, block_rows, scalar_ref, one_ref, g_ref, table_ref, bias_ref, *refs):
    piece_refs, (local_ref, remote_ref, weight_s) = refs[:fsdp], refs[fsdp:]
    tokens, width = one_ref.shape
    gather_weight(piece_refs, weight_s)
    pre = matmul(one_ref[...], weight_s[:, : 6 * LANES]) + bias_ref[...]
    back = matmul(g_ref[...], weight_s[:, 6 * LANES :])
    for block in range(tokens // block_rows):
        rows = slice(block * block_rows, (block + 1) * block_rows)
        rank = scalar_ref[1 + pl.program_id(0) * (tokens // block_rows) + block]
        places = pl.ds(pl.multiple_of(rank * block_rows, block_rows), block_rows)
        cosine, sine = table_ref[0, places, :], table_ref[1, places, :]
        for field in range(4):
            source = pre[rows] if field < 3 else back[rows]
            start = 2 * field * LANES if field < 3 else 0
            both = [source[:, start + group * LANES : start + (group + 1) * LANES] for group in range(2)]
            if field < 2:
                both = [turn(item, cosine, sine) for item in both]
            here = slice(field * LANES, (field + 1) * LANES)
            mine, other = pick(scalar_ref[0], *both)
            local_ref[rows, here] = mine.astype(BF16)
            remote_ref[rows, here] = other.astype(BF16)


def project(place, ranks, one, g, first, count, table, bias, pieces, block_rows, waits=()):
    width = one.shape[1]
    fsdp = len(pieces)
    tokens = count * block_rows
    tile = 2 * block_rows
    base = first // 2
    side = pl.BlockSpec((tile, width), lambda t, *_: (base + t, 0))
    once = pl.Buffered(1)
    out = pl.BlockSpec((tile, 4 * LANES), lambda t, *_: (t, 0))
    return launch(
        lambda *refs: project_kernel(fsdp, block_rows, *refs),
        jnp.concatenate([place, ranks]),
        [one, g, table, bias, *pieces],
        waits,
        tokens / 500.000,
        out_shape=[jax.ShapeDtypeStruct((tokens, 4 * LANES), BF16)] * 2,
        grid=(tokens // tile,),
        in_specs=[
            side,
            side,
            pl.BlockSpec(table.shape, lambda t, *_: (0, 0, 0), pipeline_mode=once),
            pl.BlockSpec(bias.shape, lambda t, *_: (0, 0)),
        ]
        + [pl.BlockSpec(piece.shape, lambda t, *_: (0, 0), pipeline_mode=once) for piece in pieces],
        out_specs=[out, out],
        scratch_shapes=[pltpu.VMEM((width, 8 * LANES), BF16)],
        name="project",
        mib=28,
    )


def attend_kernel(blocks, block_rows, scale, rank_ref, table_ref, *refs):
    count = blocks // 2
    chunk_refs, out_refs = refs[:count], refs[count : 2 * count]
    q_s, k_s, v_s, d_s, kt_s, vt_s, ot_s, qt_s, dk_s, dv_s = refs[2 * count :]
    item = pl.program_id(0)

    def rows_of(index):
        return pl.ds(pl.multiple_of(rank_ref[item * blocks + index] * block_rows, block_rows), block_rows)

    for index in range(blocks):
        rows, chunk, side = rows_of(index), chunk_refs[index // 2], index % 2
        q_s[rows, :] = chunk[side, 0, :, :LANES]
        k_s[rows, :] = chunk[side, 0, :, LANES : 2 * LANES]
        v_s[rows, :] = chunk[side, 0, :, 2 * LANES : 3 * LANES]
        d_s[rows, :] = chunk[side, 0, :, 3 * LANES :]
    kt_s[...] = k_s[...].T
    vt_s[...] = v_s[...].T
    lane = lax.broadcasted_iota(jnp.int32, (block_rows, LANES), 1)
    dk_s[...] = jnp.zeros_like(dk_s)
    dv_s[...] = jnp.zeros_like(dv_s)

    def head_step(head, carry):
        inside = (lane // HD) == head
        heads = pl.ds(pl.multiple_of(head * HD, HD), HD)
        for rank in range(blocks):
            rows = slice(rank * block_rows, (rank + 1) * block_rows)
            keys = slice(0, (rank + 1) * block_rows)
            q_h = (jnp.where(inside, q_s[rows, :], 0).astype(F32) * scale).astype(BF16)
            d_h = jnp.where(inside, d_s[rows, :], 0).astype(BF16)
            scores = against(k_s[keys, :], q_h)
            weights = jnp.exp(scores - jnp.max(scores, axis=0, keepdims=True))
            weights = weights * (1.0 / jnp.sum(weights, axis=0, keepdims=True))
            low = weights.astype(BF16)
            ot_s[heads, rows] = matmul(vt_s[heads, keys], low)
            dv_s[keys, :] += matmul(low, d_h)
            slope = against(v_s[keys, :], d_h)
            delta = jnp.sum(weights * slope, axis=0, keepdims=True)
            slope = (weights * (slope - delta)).astype(BF16)
            qt_s[heads, rows] = matmul(kt_s[heads, keys], slope)
            dk_s[keys, :] += matmul(slope, q_h)
        return carry

    lax.fori_loop(0, LANES // HD, head_step, 0)
    for index in range(blocks):
        rows, out, side = rows_of(index), out_refs[index // 2], index % 2
        cosine, sine = table_ref[0, rows, :], -table_ref[1, rows, :]
        out[side, 0, :, :LANES] = turn(qt_s[:, rows].T * scale, cosine, sine).astype(BF16)
        out[side, 0, :, LANES : 2 * LANES] = turn(dk_s[rows, :], cosine, sine).astype(BF16)
        out[side, 0, :, 2 * LANES : 3 * LANES] = dv_s[rows, :].astype(BF16)
        out[side, 0, :, 3 * LANES :] = ot_s[:, rows].T.astype(BF16)


def attend(ranks, table, chunks, waits=()):
    sides, count, block_rows, _ = chunks[0].shape
    blocks = sides * len(chunks)
    length = blocks * block_rows
    spec = pl.BlockSpec((sides, 1, block_rows, 4 * LANES), lambda m, *_: (0, m, 0, 0))
    pairs = count * blocks * (blocks + 1) // 2 * block_rows * block_rows
    return launch(
        lambda *refs: attend_kernel(blocks, block_rows, HD ** (-0.5), *refs),
        ranks,
        [table, *chunks],
        waits,
        11 * count,
        out_shape=[jax.ShapeDtypeStruct(chunk.shape, BF16) for chunk in chunks],
        grid=(count,),
        in_specs=[pl.BlockSpec(table.shape, lambda m, *_: (0, 0, 0))] + [spec] * len(chunks),
        out_specs=[spec] * len(chunks),
        scratch_shapes=[pltpu.VMEM((length, LANES), BF16)] * 4
        + [pltpu.VMEM((LANES, length), BF16)] * 2
        + [pltpu.VMEM((LANES, length), F32)] * 2
        + [pltpu.VMEM((length, LANES), F32)] * 2,
        name="attend",
        mib=24,
    )


def forward_kernel(fsdp, two_ref, g_ref, two_t, g_t, bias_ref, *refs):
    up_refs, down_refs = refs[:fsdp], refs[fsdp : 2 * fsdp]
    branch_ref, slope_ref, sum_ref = refs[2 * fsdp : 2 * fsdp + 3]
    out_refs, (up_s, down_s) = refs[2 * fsdp + 3 : -2], refs[-2:]
    width = two_ref.shape[1]
    span = width // fsdp
    lanes = [slice(offset * span, (offset + 1) * span) for offset in range(fsdp)]
    for offset in range(fsdp):
        up_s[lanes[offset], :] = up_refs[offset][...]
        down_s[lanes[offset], :] = down_refs[offset][...]
    pre = matmul(two_ref[...], up_s[...]) + bias_ref[...]
    back = matmul(g_ref[...], down_s[...])
    gate = 0.5 * (1.0 + lax.erf(pre * math.sqrt(0.5)))
    bell = jnp.exp(-0.5 * pre * pre) * (1.0 / math.sqrt(2.0 * math.pi))
    hidden = (pre * gate).astype(BF16)
    pre_grad = (back * (gate + pre * bell)).astype(BF16)
    sum_ref[...] = jnp.sum(pre_grad.astype(F32), axis=0, keepdims=True)

    @pl.when(pl.program_id(0) == 0)
    def _():
        branch_ref[...] = against(hidden, down_s[...])
        slope_ref[...] = against(pre_grad, up_s[...])

    @pl.when(pl.program_id(0) != 0)
    def _():
        branch_ref[...] += against(hidden, down_s[...])
        slope_ref[...] += against(pre_grad, up_s[...])

    for offset in range(fsdp):
        out = out_refs[offset]
        out[0] = matmul(two_t[lanes[offset], :], pre_grad).astype(out.dtype)
        out[1] = matmul(g_t[lanes[offset], :], hidden).astype(out.dtype)


def feed_forward(two, g, two_t, g_t, bias, pieces, waits=()):
    tokens, width = two.shape
    fsdp = len(pieces)
    span, hidden = pieces[0].shape[0], pieces[0].shape[1] // 2
    tile = 512
    tiles = hidden // tile
    once = pl.Buffered(1)
    whole = pl.BlockSpec((tokens, width), lambda n: (0, 0), pipeline_mode=once)
    whole_t = pl.BlockSpec((width, tokens), lambda n: (0, 0), pipeline_mode=once)
    piece = pl.BlockSpec((span, tile), lambda n: (0, n))
    later = pl.BlockSpec((span, tile), lambda n: (0, n + tiles))
    line = pl.BlockSpec((1, tile), lambda n: (0, n))
    grads = [jax.ShapeDtypeStruct((2, span, hidden), BF16 if offset else F32) for offset in range(fsdp)]
    grad = pl.BlockSpec((2, span, tile), lambda n: (0, 0, n))
    branch, slope, sums, *grads = launch(
        lambda *refs: forward_kernel(fsdp, *refs),
        None,
        [two, g, two_t, g_t, bias, *pieces, *pieces],
        waits,
        34,
        out_shape=[jax.ShapeDtypeStruct((tokens, width), F32)] * 2
        + [jax.ShapeDtypeStruct((1, hidden), F32)]
        + grads,
        grid=(tiles,),
        in_specs=[whole, whole, whole_t, whole_t, line] + [piece] * fsdp + [later] * fsdp,
        out_specs=[whole, whole, line] + [grad] * fsdp,
        scratch_shapes=[pltpu.VMEM((width, tile), BF16)] * 2,
        name="feed_forward",
        mib=60,
    )
    return branch, slope, sums, grads


def collect(place, local_ref, remote_ref, stack_s):
    for ref, group in ((local_ref, place), (remote_ref, 1 - place)):
        for field in range(4):
            here = pl.ds(pl.multiple_of((2 * field + group) * LANES, LANES), LANES)
            stack_s[:, here] = ref[:, field * LANES : (field + 1) * LANES]


def weights_kernel(fsdp, last, place_ref, one_t, g_t, local_ref, remote_ref, *refs):
    before_ref, small_ref = refs[:2] if last else (None, None)
    out_refs, stack_s = refs[2 if last else 0 : -1], refs[-1]
    step = pl.program_id(0)
    span = one_t.shape[0]

    @pl.when(step == 0)
    def _():
        collect(place_ref[0], local_ref, remote_ref, stack_s)

    pre_part = matmul(one_t[...], stack_s[:, : 6 * LANES])
    out_part = matmul(g_t[...], stack_s[:, 6 * LANES :])
    if not last:
        out_refs[0][0, :, : 6 * LANES] = pre_part
        out_refs[0][0, :, 6 * LANES :] = out_part
    else:
        pre_part = pre_part + before_ref[0, :, : 6 * LANES]
        out_part = out_part + before_ref[0, :, 6 * LANES :]
        small = small_ref[...].astype(BF16)
        for offset in range(fsdp):

            @pl.when(step == offset)
            def _():
                out = out_refs[offset]
                out[0, :span, : 6 * LANES] = pre_part.astype(out.dtype)
                out[0, :span, 6 * LANES :] = out_part.astype(out.dtype)
                out[0, span:, :] = small.astype(out.dtype)


def attention_weights(place, one_t, g_t, first, local, remote, before, fsdp, waits=()):
    width = one_t.shape[0]
    tokens = local.shape[0]
    span = width // fsdp
    columns = 8 * LANES
    last = before is not None
    stack = jax.ShapeDtypeStruct((fsdp, span, columns), F32)
    grads = [
        jax.ShapeDtypeStruct((1, span + SMALL_ROWS, columns), BF16 if offset else F32) for offset in range(fsdp)
    ]
    piece = pl.BlockSpec((span, tokens), lambda o, *_: (o, first // tokens))
    slab = pl.BlockSpec((1, span, columns), lambda o, *_: (o, 0, 0))
    whole = lambda item: pl.BlockSpec(item.shape, lambda o, *_: (0,) * len(item.shape))
    grads = launch(
        lambda *refs: weights_kernel(fsdp, last, *refs),
        place,
        [one_t, g_t, local, remote, *(before if last else [])],
        waits,
        7 if last else 0.5,
        out_shape=grads if last else [stack],
        grid=(fsdp,),
        in_specs=[piece, piece, whole(local), whole(remote)] + ([slab, whole(before[1])] if last else []),
        out_specs=[whole(item) for item in grads] if last else [slab],
        scratch_shapes=[pltpu.VMEM((tokens, columns), BF16)],
        name="attention_weights",
    )
    return list(grads) if last else grads[0]


def finish_kernel(fsdp, rows, scalar_ref, x_ref, gains_ref, branch_ref, slope_ref, local_ref, remote_ref, before_ref, *refs):
    piece_refs, (mine_ref, theirs_ref, small_ref, stack_s, one_s, branch_s, out_s, norm_s) = refs[:fsdp], refs[fsdp:]
    half, width = x_ref.shape
    span = width // fsdp
    step = pl.program_id(0)
    index = scalar_ref[0]
    gains = exchanged(lambda item: gains_ref[:, item], width, index, rows)

    @pl.when(step == 0)
    def _():
        norm_s[...] = jnp.zeros_like(norm_s)
        collect(scalar_ref[1], local_ref, remote_ref, stack_s)
        for offset in range(fsdp):
            lanes = slice(offset * span, (offset + 1) * span)
            one_s[:, lanes] = against(stack_s[:, : 6 * LANES], piece_refs[offset][:, : 6 * LANES])
            branch_s[:, lanes] = against(stack_s[:, 6 * LANES :], piece_refs[offset][:, 6 * LANES :])

    here = pl.ds(pl.multiple_of((2 * lax.rem(step, 2) + ((step // 2) ^ scalar_ref[3])) * half, half), half)
    one, two = one_s[here, :], slope_ref[...]
    normal, _ = normal_of(x_ref[...].astype(F32))
    norm_s[0:1, :] += jnp.sum(one * normal, axis=0, keepdims=True)
    norm_s[1:2, :] += jnp.sum(one, axis=0, keepdims=True)
    norm_s[2:3, :] += jnp.sum(two * normal, axis=0, keepdims=True)
    norm_s[3:4, :] += jnp.sum(two, axis=0, keepdims=True)
    plain = []
    for value in (branch_ref[...] + branch_s[here, :], one * gains[0:1] + two * gains[2:3]):
        out_s[...] = value
        plain.append(exchanged(lambda item: out_s[:, item], width, index, rows).astype(BF16))

    for which, ref in enumerate((mine_ref, theirs_ref)):

        @pl.when(step // 2 == which)
        def _():
            ref[0, 0], ref[0, 1] = plain

    @pl.when(step == 3)
    def _():
        small_ref[...] = before_ref[...]
        small_ref[0:4, :] += exchanged(lambda item: norm_s[0:4, item], width, index, rows)
        small_ref[pl.ds(5 + scalar_ref[2], 1), : 6 * LANES] += jnp.sum(
            stack_s[:, : 6 * LANES].astype(F32), axis=0, keepdims=True
        )


def finish(scalars, x, gains, branch, slope, first, local, remote, small, pieces, rows, waits=()):
    width = x.shape[1]
    fsdp = len(pieces)
    half = local.shape[0] // 4
    base = first // half
    once = pl.Buffered(1)
    fixed = lambda item: pl.BlockSpec(item.shape, lambda t, *_: (0, 0))
    place = lambda t, scalars: 2 * lax.rem(t, 2) + ((t // 2) ^ scalars[3])
    row_spec = pl.BlockSpec((half, width), lambda t, scalars: (base + place(t, scalars), 0))
    back_spec = pl.BlockSpec(local.shape, lambda t, *_: (0, 0), pipeline_mode=once)
    mine_spec = pl.BlockSpec((1, 2, half, width), lambda t, *_: (jnp.minimum(t, 1), 0, 0, 0))
    theirs_spec = pl.BlockSpec((1, 2, half, width), lambda t, *_: (jnp.maximum(t - 2, 0), 0, 0, 0))
    sums = jax.ShapeDtypeStruct((2, 2, half, width), BF16)
    return launch(
        lambda *refs: finish_kernel(fsdp, rows, *refs),
        scalars,
        [x, gains, branch, slope, local, remote, small, *pieces],
        waits,
        half / 20 if first else 0.5,
        out_shape=[sums, sums, jax.ShapeDtypeStruct(small.shape, F32)],
        grid=(4,),
        in_specs=[row_spec, fixed(gains), row_spec, row_spec, back_spec, back_spec, fixed(small)]
        + [pl.BlockSpec(piece.shape, lambda t, *_: (0, 0), pipeline_mode=once) for piece in pieces],
        out_specs=[mine_spec, theirs_spec, fixed(small)],
        scratch_shapes=[
            pltpu.VMEM((4 * half, 8 * LANES), BF16),
            pltpu.VMEM((4 * half, width), F32),
            pltpu.VMEM((4 * half, width), F32),
            pltpu.VMEM((half, width), F32),
            pltpu.VMEM((8, width), F32),
        ],
        name="finish",
        mib=60 if first == 0 else 40,
    )


def sums_kernel(parts, *refs):
    terms, out = refs[:-1], refs[-1]
    start = 0
    for number in range(parts):
        mine, other = terms[2 * number : 2 * number + 2]
        rows = slice(start, start + mine.shape[2])
        total = mine[0, 0].astype(F32) + other[0, 0].astype(F32)
        if len(terms) > 2 * parts:
            total = total + terms[-1][0, rows, :].astype(F32)
        out[0, rows, :] = total.astype(BF16)
        start += mine.shape[2]


def core_sums(side, terms, more=(), waits=(), us=2):
    fields, width = terms[0].shape[1], terms[0].shape[3]
    rows = sum(item.shape[2] for item in terms[::2])
    field = pl.BlockSpec((1, rows, width), lambda n: (n, 0, 0))
    return launch(
        lambda *refs: sums_kernel(len(terms) // 2, *refs),
        None,
        [*terms, *more],
        waits,
        us,
        out_shape=jax.ShapeDtypeStruct((fields, rows, width), BF16),
        grid=(fields,),
        in_specs=[pl.BlockSpec((1, 1, item.shape[2], width), lambda n: (side, n, 0, 0)) for item in terms]
        + [field] * len(more),
        out_specs=field,
        name="core_sums",
    )


def tree_sum(terms):
    while len(terms) > 1:
        terms = [first + second for first, second in zip(terms[::2], terms[1::2])]
    return terms[0]


def reduce_kernel(body, cuts, *refs):
    in_refs, out_refs = refs[: -len(cuts)], refs[-len(cuts) :]
    extra = in_refs[0].shape[1] - body
    for (start, count, _), out in zip(cuts, out_refs):
        rows = slice(start, start + count)
        out[0, :count, :] = tree_sum([ref[0, rows, :].astype(F32) for ref in in_refs]).astype(out.dtype)
    if extra:
        small = tree_sum([ref[0, body:, :].astype(F32) for ref in in_refs]).astype(BF16)
        for (_, count, _), out in zip(cuts, out_refs):
            out[0, count:, :] = small.astype(out.dtype)


def reduce_and_cut(terms, cuts, waits=(), extra=0, us=3):
    stacks, rows, columns = terms[0].shape
    tile = min(columns, 512)
    spec = lambda count: pl.BlockSpec((1, count, tile), lambda a, b: (a, 0, b))
    return launch(
        lambda *refs: reduce_kernel(rows - extra, cuts, *refs),
        None,
        terms,
        waits,
        us,
        out_shape=[jax.ShapeDtypeStruct((stacks, count + extra, columns), dtype) for _, count, dtype in cuts],
        grid=(stacks, columns // tile),
        in_specs=[spec(rows)] * len(terms),
        out_specs=[spec(count + extra) for _, count, _ in cuts],
        name="reduce_and_cut",
    )


def scatter(stack):
    return [stack[0]] + [swap(piece, "fsdp", j) for j, piece in enumerate(stack) if j > 0]


def close_kernel(source, core_ref, x_ref, g_ref, mine_ref, other_ref, shift_ref, out_ref, grad_ref):
    core, _ = source(pl.program_id(0))
    values = x_ref[...].astype(F32)
    normal, spread = normal_of(values)
    total, slope = (
        jnp.where(core == core_ref[0], mine_ref[field].astype(F32), other_ref[field].astype(F32)) for field in range(2)
    )
    out_ref[...] = (values + total + shift_ref[...]).astype(BF16)
    slope_mean = jnp.mean(slope, axis=-1, keepdims=True)
    slope_dot = jnp.mean(slope * normal, axis=-1, keepdims=True)
    grad_ref[...] = (g_ref[...].astype(F32) + spread * (slope - slope_mean - normal * slope_dot)).astype(BF16)


def close(core, x, g, mine, other, shift, first_rows, waits=()):
    tokens, width = x.shape
    block = math.gcd(math.gcd(first_rows // 2, (tokens - first_rows) // 2), 128)
    first, rest = first_rows // (2 * block), (tokens - first_rows) // (2 * block)

    def source(m):
        late = m >= 2 * first
        local = m - jnp.where(late, 2 * first, 0)
        count = jnp.where(late, rest, first)
        core = jnp.where(local >= count, 1, 0)
        return core, local - core * count + jnp.where(late, first, 0)

    row_spec = pl.BlockSpec((block, width), lambda m, *_: (m, 0))
    total_spec = pl.BlockSpec((2, block, width), lambda m, *_: (0, source(m)[1], 0))
    return launch(
        lambda *refs: close_kernel(source, *refs),
        core,
        [x, g, mine, other, shift],
        waits,
        3,
        out_shape=[jax.ShapeDtypeStruct((tokens, width), BF16)] * 2,
        grid=(tokens // block,),
        in_specs=[row_spec, row_spec, total_spec, total_spec, pl.BlockSpec((1, width), lambda m, *_: (0, 0))],
        out_specs=[row_spec] * 2,
        name="close",
    )


def ranks_of(order, offsets):
    sources = lax.axis_index("ctx") ^ jnp.array(offsets, dtype=jnp.int32)
    match = sources[:, None] == jnp.arange(order.shape[1], dtype=jnp.int32)[None, :]
    return jnp.sum(jnp.where(match, order[:, None, :], 0), axis=-1)


def exchange_attention(local, remote, order, table, block_rows, waits):
    shape = (2, order.shape[0], block_rows, 4 * LANES)
    ranks = ranks_of(order, range(4)).reshape(-1)
    outs = attend(ranks, table, [local.reshape(shape), remote.reshape(shape)], waits)
    mine, theirs = (out.reshape(local.shape) for out in outs)
    return mine, swap(theirs, "ctx", 2)


def gathered_attention(local, remote, order, table, block_rows, waits):
    groups, micro = 2, order.shape[0]
    ctx = lax.axis_size("ctx")
    heads = groups * LANES // HD
    scale = HD ** (-0.5)
    packed = jnp.stack([local, remote]).reshape(groups, 2, micro, block_rows, 4 * LANES)
    packed = jnp.transpose(packed, (0, 2, 1, 3, 4))
    ranks = ranks_of(order, range(ctx))

    def split(array):
        array = array.reshape(groups, 2 * block_rows, LANES // HD, HD)
        return jnp.transpose(array, (1, 0, 2, 3)).reshape(2 * block_rows, heads, HD)

    def join(array):
        return jnp.transpose(array.reshape(2, block_rows, groups, LANES), (2, 0, 1, 3))

    def everywhere(array):
        return jnp.stack([array] + [swap(array, "ctx", j) for j in range(2, ctx, 2)])

    def home(array):
        total = array[0].astype(F32)
        for j in range(2, ctx, 2):
            total = total + swap(array[j // 2], "ctx", j).astype(F32)
        return total

    results = []
    for m in range(micro):
        parted = packed[:, m].reshape(groups, 2 * block_rows, 4, LANES)
        queries, keys, values, douts = (split(parted[:, :, i]) for i in range(4))
        all_keys, all_values = everywhere(keys), everywhere(values)
        key_ranks = jnp.repeat(ranks[m].reshape(-1, 2), block_rows, axis=1)
        query_ranks = key_ranks[0]
        allowed = (key_ranks[:, None, :] <= query_ranks[None, :, None])[:, None]

        def peak_step(state, item):
            key, value, ok = item
            peak, total, sums = state
            scores = jnp.einsum("bhe,rhe->hbr", queries, key, preferred_element_type=F32) * scale
            scores = jnp.where(ok, scores, -1e30)
            new = jnp.maximum(peak, jnp.max(scores, axis=-1))
            weights = jnp.where(ok, jnp.exp(scores - new[..., None]), 0.0)
            fade = jnp.exp(peak - new)
            part = jnp.einsum("hbr,rhe->hbe", weights.astype(BF16), value, preferred_element_type=F32)
            return (new, total * fade + jnp.sum(weights, axis=-1), sums * fade[..., None] + part), None

        start = (
            jnp.full((heads, 2 * block_rows), -1e30, F32),
            jnp.zeros((heads, 2 * block_rows), F32),
            jnp.zeros((heads, 2 * block_rows, HD), F32),
        )
        (peak, total, sums), _ = lax.scan(peak_step, start, (all_keys, all_values, allowed))
        attended = jnp.transpose(sums / total[..., None], (1, 0, 2))
        level = peak + jnp.log(total)
        delta = jnp.transpose(jnp.sum(douts.astype(F32) * attended, axis=-1))

        def back_step(query_sum, item):
            key, value, ok = item
            scores = jnp.einsum("bhe,rhe->hbr", queries, key, preferred_element_type=F32) * scale
            weights = jnp.where(ok, jnp.exp(scores - level[..., None]), 0.0)
            value_grad = jnp.einsum("hbr,bhe->rhe", weights.astype(BF16), douts, preferred_element_type=F32)
            slope = jnp.einsum("bhe,rhe->hbr", douts, value, preferred_element_type=F32)
            slope = (weights * (slope - delta[..., None])).astype(BF16)
            query_part = jnp.einsum("hbr,rhe->bhe", slope, key, preferred_element_type=F32) * scale
            key_grad = jnp.einsum("hbr,bhe->rhe", slope, queries, preferred_element_type=F32) * scale
            return query_sum + query_part, (key_grad.astype(BF16), value_grad.astype(BF16))

        query_grad, (key_grads, value_grads) = lax.scan(
            back_step, jnp.zeros(queries.shape, F32), (all_keys, all_values, allowed)
        )
        rows = [
            lax.dynamic_slice(table, (0, ranks[m, side] * block_rows, 0), (2, block_rows, LANES)) for side in range(2)
        ]
        rows = jnp.concatenate(rows, axis=1)

        def unturn(array):
            half = ROT // 2
            cosine, sine = rows[0, :, :half][:, None], rows[1, :, half:ROT][:, None]
            first, second = array[..., :half], array[..., half:ROT]
            return jnp.concatenate(
                [first * cosine + second * sine, second * cosine - first * sine, array[..., ROT:]], axis=-1
            )

        fields = (unturn(query_grad), unturn(home(key_grads)), home(value_grads), attended)
        results.append(jnp.concatenate([join(field.astype(BF16)) for field in fields], axis=-1))
    results = jnp.transpose(jnp.stack(results, axis=1), (0, 2, 1, 3, 4))
    mine, theirs = results.reshape(groups, *local.shape)
    return mine, theirs


def rotation_table(length):
    lane = jnp.arange(LANES, dtype=jnp.int32) % HD
    halves = ROT // 2
    frequency = jnp.exp((lane % halves).astype(F32) * (-2.0 * math.log(10000.0) / ROT))
    frequency = jnp.where(lane < ROT, frequency, 0.0)
    angles = jnp.arange(length, dtype=F32)[:, None] * frequency
    return jnp.stack([jnp.cos(angles), jnp.where(lane < halves, -1.0, 1.0) * jnp.sin(angles)])


def local(
    inputs,
    block_order,
    first_gain,
    first_shift,
    second_gain,
    second_shift,
    qkv_weight,
    qkv_bias,
    out_weight,
    out_bias,
    up_weight,
    up_bias,
    down_weight,
    down_bias,
    out_grad,
):
    micro, block_rows, _, width = inputs.shape
    ctx = lax.axis_size("ctx")
    f, z, core = lax.axis_index("fsdp"), lax.axis_index("ctx"), lax.axis_index("tp")
    low = z & 1
    rows = up_weight.shape[0]
    groups, hidden = 2, up_weight.shape[1] // 2
    tokens = micro * block_rows
    order = block_order[:, 0]
    first_part = micro - 1
    parts = ((0, first_part), (first_part, micro))
    exchanging = ctx == 2 * groups

    fields = [qkv_weight[0], qkv_weight[1], qkv_weight[2], jnp.transpose(out_weight)]
    extent = groups * LANES
    halves = [jnp.concatenate([field[:, i * extent : (i + 1) * extent] for field in fields], axis=1) for i in range(2)]
    shard = jnp.stack(halves)

    x, g = inputs.reshape(tokens, width), out_grad.reshape(tokens, width)
    fields = [up_weight, jnp.transpose(down_weight)]
    halves = [jnp.concatenate([field[:, i * hidden : (i + 1) * hidden] for field in fields], axis=1) for i in range(2)]
    forward_shard, both, shard = lax.optimization_barrier((jnp.stack(halves), jnp.stack([x, g]), shard))
    column = gather_column(*choose(low, shard[0], shard[1]))
    own, other = choose(low, forward_shard[0], forward_shard[1])
    forward_pair = jnp.concatenate([own, swap(other, "ctx", 1)], axis=0)
    lanes, _ = choose(core, both[:, :, : width // 2], both[:, :, width // 2 :])
    lanes, column[1] = lax.optimization_barrier((lanes, column[1]))
    lanes = swap(lanes, "ctx", 1)
    column = jnp.concatenate(column, axis=0)
    pieces = gather_pieces(column)

    table = rotation_table(ctx * block_rows)
    index = jnp.stack([f * ctx + z, core]).astype(jnp.int32)
    gains = jnp.stack([first_gain, first_shift, second_gain, second_shift]).astype(F32)
    prepared, grad_sum = prepare_own(
        index, x, g, gains, rows, block_rows, (column, forward_pair, table)
    )
    forward_column = [forward_pair] + [swap(forward_pair, "ctx", j) for j in range(2, ctx, 2)]
    lanes, grad_sum, *pieces = lax.optimization_barrier((lanes, grad_sum, *pieces))
    arrived = (lanes, swap(lanes, "tp", 1))
    x_both, g_both, one = prepare_pair(
        index, arrived, gains, prepared, rows, block_rows, first_part
    )

    place = ((z >> 1) if exchanging else jnp.zeros_like(z)).astype(jnp.int32).reshape(1)
    bias = qkv_bias.astype(F32)
    bias = choose(low, bias[:, :extent], bias[:, extent:])[0].reshape(1, -1)
    attention = exchange_attention if exchanging else gathered_attention
    send = (lambda item: swap(item, "ctx", 2)) if exchanging else (lambda item: item)
    packed, first_block = [], 0
    for begin, end in parts:
        ranks = jnp.transpose(ranks_of(order[begin:end], (0, 1))).reshape(-1)
        count = 2 * (end - begin)
        waits = [forward_column] if packed else []
        mine, other = project(
            place, ranks, one, g_both, first_block, count, table, bias, pieces, block_rows, waits
        )
        if not packed:
            forward_column[0], mine = lax.optimization_barrier((forward_column[0], mine))
            forward_column = jnp.concatenate(forward_column, axis=0)
            forward_pieces = gather_pieces(forward_column)
        packed.append((first_block * block_rows, mine, other))
        first_block += count

    two, one_t, two_t, g_t = prepare_late(index, x_both, g_both, one, gains, rows, block_rows, (packed[1][1],))
    up_shift = up_bias.astype(F32).reshape(2, 1, hidden)
    up_shift = choose(low, up_shift[0], up_shift[1])[0]
    arrivals = [send(theirs) for _, _, theirs in packed]
    returned = [attention(packed[0][1], arrivals[0], order[: parts[0][1]], table, block_rows, (g_t,))]
    branch, slope, up_sum, forward_grads = feed_forward(
        two, g_both, two_t, g_t, up_shift, forward_pieces, (returned[0][0],)
    )
    returned.append(attention(packed[1][1], arrivals[1], order[parts[1][0] :], table, block_rows, (up_sum,)))

    scalars = jnp.stack([f * ctx + z, place[0], low, core]).astype(jnp.int32)
    end_shift = (out_bias.astype(F32) + down_bias.astype(F32)).reshape(1, width)
    forward_terms = scatter(forward_grads)
    pairs = range(2, ctx, 2)

    def finish_part(number, small, waits):
        first, (local, remote) = packed[number][0], returned[number]
        mine, theirs, small = finish(
            scalars, x_both, gains, branch, slope, first, local, remote, small, pieces, rows, waits
        )
        return (mine, swap(theirs, "tp", 1)), small

    def weights_part(number, before, waits):
        first, (local, remote) = packed[number][0], returned[number]
        return attention_weights(place, one_t, g_t, first, local, remote, before, len(pieces), waits)

    zero = jnp.zeros((1, width), F32)
    small = jnp.concatenate([zero] * 4 + [grad_sum, zero, zero, *choose(low, up_sum, zero)] + [zero] * (SMALL_ROWS - 9))
    made = {}

    def run(task, wait):
        if task == "finish_a":
            made["a"], made["small"] = finish_part(0, small, (wait,))
            return made["small"]
        if task == "weights_a":
            made["grads_a"] = weights_part(0, None, (wait,))
            return made["grads_a"]
        if task == "forward_first":
            keep, *send = reduce_and_cut(
                forward_terms, [(0, 2 * rows, F32)] + [(j * rows, 2 * rows, BF16) for j in pairs], (wait,)
            )
            made["forward"] = [keep] + [swap(item, "ctx", j) for j, item in zip(pairs, send)]
            return keep
        if task == "finish_b":
            made["b"], made["small"] = finish_part(1, made["small"], (wait,))
            return made["small"]
        if task == "weights_b":
            grads = weights_part(1, (made["grads_a"], made["small"]), (wait,))
            made["attention"] = scatter(grads)
            return grads[0]
        if task == "forward_second":
            made["mine"], made["send"] = reduce_and_cut(
                made["forward"], [(0, rows, F32), (rows, rows, BF16)], (wait,)
            )
            return made["mine"]
        if task == "attention_first":
            made["keep"], *send = reduce_and_cut(
                made["attention"],
                [(0, rows, F32)] + [(j * rows, rows, BF16) for j in range(1, ctx)],
                (wait,),
                SMALL_ROWS,
            )
            made["sent"] = [swap(item, "ctx", j) for j, item in enumerate(send, 1)]
            return made["keep"]
        if task == "sums":
            sums = core_sums(1, [*made["a"], *made["b"]], (), (wait,))
            made["pair"] = swap(sums, "ctx", 1)
            return sums
        if task == "totals":
            totals = core_sums(0, [*made["a"], *made["b"]], [made["pair"]], (wait, *made["sent"]))
            made["totals"] = (totals, swap(totals, "tp", 1))
            return totals
        core_place = core.astype(jnp.int32).reshape(1)
        made["results"] = close(core_place, x, g, *made["totals"], end_shift, packed[1][0] // 2, (wait,))
        return made["results"][0]

    wait = returned[1][0]
    for task in TASKS:
        wait = run(task, wait)
    forward_mine, forward_send, attention_keep, results = (made[key] for key in ("mine", "send", "keep", "results"))
    attention_got = made["sent"]
    forward_got, done = lax.optimization_barrier((swap(forward_send, "ctx", 1), results[0]))
    results = [done, results[1]]
    outputs, input_grad = (item.reshape(inputs.shape) for item in results)
    forward_sums = choose(low, forward_mine, forward_got.astype(F32))
    up_sums = jnp.concatenate([half[0] for half in forward_sums], axis=1)
    down_sums = jnp.concatenate([jnp.transpose(half[1]) for half in forward_sums], axis=0)

    terms = [attention_keep[0]] + [got[0].astype(F32) for got in attention_got]
    halves = choose(low, tree_sum([term[:rows] for term in terms[::2]]), tree_sum([term[:rows] for term in terms[1::2]]))
    small = tree_sum([term[rows:] for term in terms])
    fields = [
        jnp.concatenate([half[:, i * extent : (i + 1) * extent] for half in halves], axis=1) for i in range(4)
    ]
    norm_sums = small[:4] + swap(small[:4], "tp", 1)
    pre_sums = small[5:7, : 3 * extent].reshape(2, 3, extent)
    return (
        outputs,
        input_grad,
        norm_sums[0],
        norm_sums[1],
        norm_sums[2],
        norm_sums[3],
        jnp.stack(fields[:3]),
        jnp.concatenate([pre_sums[0], pre_sums[1]], axis=1),
        jnp.transpose(fields[3]),
        small[4],
        up_sums,
        small[7:9].reshape(-1),
        down_sums,
        small[4],
    )


def solution(mesh):
    placed = (
        P(None, "ctx", "fsdp", None),
        P(None, "fsdp", None),
        P(),
        P(),
        P(),
        P(),
        P(None, ("fsdp", "ctx"), "tp"),
        P(None, "tp"),
        P("tp", ("fsdp", "ctx")),
        P(),
        P(("fsdp", "ctx"), "tp"),
        P("tp"),
        P("tp", ("fsdp", "ctx")),
        P(),
        P(None, "ctx", "fsdp", None),
    )
    return jax.shard_map(
        local,
        mesh=mesh,
        in_specs=placed,
        out_specs=(
            P(None, "ctx", "fsdp", None),
            P(None, "ctx", "fsdp", None),
            P(),
            P(),
            P(),
            P(),
            P(None, ("fsdp", "ctx"), "tp"),
            P(None, "tp"),
            P("tp", ("fsdp", "ctx")),
            P(),
            P(("fsdp", "ctx"), "tp"),
            P("tp"),
            P("tp", ("fsdp", "ctx")),
            P(),
        ),
        check_vma=False,
    )
```
